32 devices in a mesh: gx: 4 (over z), gy: 8 (over y, x, core).
Axes of the slice: x: 2, y: 2, z: 4, core: 2. Of those that a mesh axis runs over, the one named last changes fastest.
Arguments:
- state: float32 [3, 32, 256, 128], P(None, 'gx', 'gy'), as said below
- perm: float32 [3, 32, 256, 128], P(None, 'gx', 'gy'), may hold values from 0.1 to 1
- pore: float32 [32, 256, 128], P('gx', 'gy'), may hold values from 0.5 to 2
- old_mass: float32 [3, 32, 256, 128], P(None, 'gx', 'gy'), may hold values from 0.05 to 0.6
- scaling: float32 [3, 32, 256, 128], P(None, 'gx', 'gy'), may hold values from 0.005 to 0.2, as said below
- fault_cell: int32 [4, 8, 2048], P('gx', 'gy'), may hold values from 0 to 32767
- fault_tile: int32 [4, 8, 2048], P('gx', 'gy'), may hold values from 0 to 31, as said below
- fault_row: int32 [4, 8, 2048], P('gx', 'gy'), may hold values from 0 to 1023
- fault_trans: float32 [4, 8, 2048], P('gx', 'gy'), may hold values from 0.2 to 2
- fault_export: int32 [4, 8, 1024], P('gx', 'gy'), may hold values from 0 to 32767
- perf_cell: int32 [4, 8, 3, 3, 4, 16], P('gx', 'gy'), may hold values from -1 to 32767, as said below
- well_segments: int32 [4, 8, 4], P('gx', 'gy'), may hold values from 1 to 16, as said below
- well_index: float32 [4, 8, 4, 16], P('gx', 'gy'), may hold values from 0.5 to 2
- bhp: float32 [4, 8, 4], P('gx', 'gy'), may hold values from -1 to 0.5
- target: float32 [4, 8, 4], P('gx', 'gy'), may hold values from 0.5 to 2
Outputs:
- residual: float32 [3, 32, 256, 128], P(None, 'gx', 'gy')
- newton_step: float32 [3, 32, 256, 128], P(None, 'gx', 'gy')
- well_residual: float32 [4, 8, 4], P('gx', 'gy')
The draws below stay inside these ranges and needn't reach their ends.
Inputs may be any that keep to these rules, and one draw needn't show every extreme that they name: `fault_tile`: the partner tile's coordinates differ from the connection's own tile by at most one along each axis. `perf_cell`: -1 marks an empty entry; every live segment of a well appears in exactly one entry, on a tile at most one away from its home along each axis, and no dead segment appears. `well_segments`: some well has all 16 segments live. `state`: pressure within -3 to 3, saturations of water and gas each within 0.05 to 0.4. `scaling`: component 0 within 0.05 to 0.2, component 1 within 0.02 to 0.08, component 2 within 0.005 to 0.02.
All inputs are finite; a program needn't handle non-finite values.
Results may differ from the reference program's by a relative error of at most 0.00011.
Values sent between devices are 32-bit elements; how exact they have to be, the bound alone decides.
No kernel may reach another device: no remote copies, remote signals or barrier semaphores. Data moves between devices by JAX's collectives and lax.ppermute only.
A program may use at most 128 MiB of HBM per device.

```python
import math
import jax
import jax.numpy as jnp
from jax import lax

CX = 8
CY = 32
NZ = 128
FL = 2048
FE = 1024
W_DEV = 4
SEG = 16
TILES_X = 4
TILES_Y = 8
NX = 32
NY = 256
CELLS = 32768


def draw_state(key, part):
    subkeys = jax.random.split(key, 3)
    dims_all = (NX, NY, NZ)
    pressure = jnp.clip(jax.random.normal(subkeys[0], dims_all, jnp.float32), -3.0, 3.0)
    water_sat = jax.random.uniform(subkeys[1], dims_all, jnp.float32, 0.05, 0.4)
    gas_sat = jax.random.uniform(subkeys[2], dims_all, jnp.float32, 0.05, 0.4)
    return jnp.stack([pressure, water_sat, gas_sat])


def draw_scaling(key, part):
    dims_all = (3, NX, NY, NZ)
    lower = jnp.array([0.05, 0.02, 0.005], jnp.float32).reshape(3, 1, 1, 1)
    unit = jax.random.uniform(jax.random.fold_in(key, 11), dims_all, jnp.float32, 0.0, 1.0)
    return lower * jnp.exp(unit * jnp.log(4.0))


def draw_fault_tile(key, part):
    key_x, key_y = jax.random.split(jax.random.fold_in(key, 3))
    dims_all = (TILES_X, TILES_Y, FL)
    home_x = lax.broadcasted_iota(jnp.int32, dims_all, 0)
    home_y = lax.broadcasted_iota(jnp.int32, dims_all, 1)
    other_x = jnp.clip(home_x + jax.random.randint(key_x, dims_all, -1, 2), 0, TILES_X - 1)
    other_y = jnp.clip(home_y + jax.random.randint(key_y, dims_all, -1, 2), 0, TILES_Y - 1)
    return other_x * TILES_Y + other_y


def well_layout(key):
    key_c, key_p, key_x, key_y, key_cell = jax.random.split(jax.random.fold_in(key, 7), 5)
    counts = jax.random.randint(key_c, (TILES_X, TILES_Y, W_DEV), 1, SEG + 1)
    full_well = jax.random.randint(key_p, (), 0, TILES_X * TILES_Y * W_DEV)
    position = jnp.arange(TILES_X * TILES_Y * W_DEV, dtype=jnp.int32).reshape(TILES_X, TILES_Y, W_DEV)
    counts = jnp.where(position == full_well, SEG, counts)
    dims_all = (TILES_X, TILES_Y, W_DEV, SEG)
    home_x = lax.broadcasted_iota(jnp.int32, dims_all, 0)
    home_y = lax.broadcasted_iota(jnp.int32, dims_all, 1)
    shift_x = jnp.clip(home_x + jax.random.randint(key_x, dims_all, -1, 2), 0, TILES_X - 1) - home_x
    shift_y = jnp.clip(home_y + jax.random.randint(key_y, dims_all, -1, 2), 0, TILES_Y - 1) - home_y
    cell_ids = jax.random.randint(key_cell, dims_all, 0, CELLS)
    live_seg = lax.broadcasted_iota(jnp.int32, dims_all, 3) < counts[..., None]
    stacked = []
    for along_x in range(3):
        columns = []
        for along_y in range(3):
            chosen = jnp.where(live_seg & (shift_x == 1 - along_x) & (shift_y == 1 - along_y), cell_ids, -1)
            padded = jnp.pad(chosen, ((1, 1), (1, 1), (0, 0), (0, 0)), constant_values=-1)
            columns.append(padded[along_x:along_x + TILES_X, along_y:along_y + TILES_Y])
        stacked.append(jnp.stack(columns, axis=2))
    return (counts, jnp.stack(stacked, axis=2))


def draw_well_segments(key, part):
    return well_layout(key)[0]


def draw_perf_cell(key, part):
    return well_layout(key)[1]


def set_ends(drawn, own_key, least, top_value):
    longest = drawn.shape.index(max(drawn.shape))
    spots = []
    for shift in (0, 1):
        where = [jax.random.randint(jax.random.fold_in(own_key, axis), (), 0, length) for axis, length in enumerate(drawn.shape)]
        where[longest] = (where[longest] + shift) % drawn.shape[longest]
        spots.append(tuple(where))
    return drawn.at[spots[0]].set(least).at[spots[1]].set(top_value)


def level_of(rng, extent, cuts, smallest, largest):
    factor_of = 1.0
    for axis_at, blocks in cuts:
        draws = jax.random.uniform(jax.random.fold_in(jax.random.fold_in(rng, 6), axis_at), (blocks,), jnp.float32, smallest / len(cuts), largest / len(cuts))
        factor_of = factor_of * jnp.repeat(jnp.exp(draws), extent[axis_at] // blocks).reshape((-1,) + (1,) * (len(extent) - 1 - axis_at))
    return factor_of


def setup_inputs(seed: int = 0) -> dict:
    splits = jax.random.split(jax.random.key(seed), 16)
    state = draw_state(jax.random.fold_in(splits[15], 71), 0)
    perm = jnp.clip(jnp.exp(math.log(1.0) - 2.3025851 * jax.random.uniform(splits[1], (3, NX, NY, NZ), jnp.float32) ** level_of(splits[1], (3, NX, NY, NZ), ((1, 4), (2, 8)), -0.2, 0.2)), 0.1, 1.0)
    pore = jnp.clip(jnp.exp(math.log(2.0) - 1.3862944 * jax.random.uniform(splits[2], (NX, NY, NZ), jnp.float32) ** level_of(splits[2], (NX, NY, NZ), ((0, 4), (1, 8)), -0.2, 0.2)), 0.5, 2.0)
    old_mass = jnp.clip(0.05 + 0.55 * jax.random.uniform(splits[3], (3, NX, NY, NZ), jnp.float32) ** level_of(splits[3], (3, NX, NY, NZ), ((1, 4), (2, 8)), -0.2, 0.2), 0.05, 0.6)
    scaling = draw_scaling(jax.random.fold_in(splits[15], 71), 0)
    fault_cell = set_ends(jax.random.randint(splits[5], (TILES_X, TILES_Y, FL), 0, CELLS), jax.random.fold_in(splits[5], 1), 0, CELLS - 1).astype(jnp.int32)
    fault_tile = draw_fault_tile(jax.random.fold_in(splits[15], 71), 0)
    fault_row = set_ends(jax.random.randint(splits[7], (TILES_X, TILES_Y, FL), 0, FE), jax.random.fold_in(splits[7], 1), 0, FE - 1).astype(jnp.int32)
    fault_trans = jnp.clip(jnp.exp(math.log(2.0) - 2.3025851 * jax.random.uniform(splits[8], (TILES_X, TILES_Y, FL), jnp.float32) ** level_of(splits[8], (TILES_X, TILES_Y, FL), ((0, 4), (1, 8)), -0.2, 0.2)), 0.2, 2.0)
    fault_export = set_ends(jax.random.randint(splits[9], (TILES_X, TILES_Y, FE), 0, CELLS), jax.random.fold_in(splits[9], 1), 0, CELLS - 1).astype(jnp.int32)
    perf_cell = draw_perf_cell(jax.random.fold_in(splits[15], 71), 0)
    well_segments = draw_well_segments(jax.random.fold_in(splits[15], 71), 0)
    well_index = jnp.clip(jnp.exp(math.log(2.0) - 1.3862944 * jax.random.uniform(splits[12], (TILES_X, TILES_Y, W_DEV, SEG), jnp.float32) ** level_of(splits[12], (TILES_X, TILES_Y, W_DEV, SEG), ((0, 4), (1, 8)), -0.2, 0.2)), 0.5, 2.0)
    bhp = jnp.clip(-1.0 + 1.5 * jax.random.uniform(splits[13], (TILES_X, TILES_Y, W_DEV), jnp.float32) ** level_of(splits[13], (TILES_X, TILES_Y, W_DEV), ((0, 4), (1, 8)), -0.2, 0.2), -1.0, 0.5)
    target = jnp.clip(jnp.exp(math.log(2.0) - 1.3862944 * jax.random.uniform(splits[14], (TILES_X, TILES_Y, W_DEV), jnp.float32) ** level_of(splits[14], (TILES_X, TILES_Y, W_DEV), ((0, 4), (1, 8)), -0.2, 0.2)), 0.5, 2.0)
    return dict(state=state, perm=perm, pore=pore, old_mass=old_mass, scaling=scaling, fault_cell=fault_cell, fault_tile=fault_tile, fault_row=fault_row, fault_trans=fault_trans, fault_export=fault_export, perf_cell=perf_cell, well_segments=well_segments, well_index=well_index, bhp=bhp, target=target)


VISCOSITY = (0.5, 2.0, 0.1)
COMPRESS = (0.02, 0.05, 0.3)
DENSITY = (1.0, 0.8, 0.2)
GRAVITY = 0.2
SMOOTHING = 0.1
HEAD_SCALE = 0.3

def properties(field):
    water_sat = field[1]
    gas_sat = field[2]
    saturation = jnp.stack([water_sat, 1.0 - water_sat - gas_sat, gas_sat])
    factor = jnp.stack([jnp.exp(COMPRESS[phase_i] * field[0]) for phase_i in range(3)])
    mobility = jnp.stack([saturation[phase_i] * saturation[phase_i] * factor[phase_i] / VISCOSITY[phase_i] for phase_i in range(3)])
    return (saturation, factor, mobility)

def face_inflow(p_own, mob_own, p_other, mob_other, face_trans, depth_step):
    inflows = []
    for phase_i in range(3):
        potential = p_other - p_own - GRAVITY * DENSITY[phase_i] * depth_step
        weight = jax.nn.sigmoid(potential / SMOOTHING)
        inflows.append(face_trans * (weight * mob_other[phase_i] + (1.0 - weight) * mob_own[phase_i]) * potential)
    return jnp.stack(inflows)

def cell_inflow(padded, perm_pad):
    _, _, mobility = properties(padded)
    inner = (slice(1, -1), slice(1, -1), slice(1, -1))
    p_centre = padded[0][inner]
    mob_centre = mobility[(slice(None),) + inner]
    summed = jnp.zeros((3,) + p_centre.shape, jnp.float32)
    for dim_index in range(3):
        t_centre = perm_pad[dim_index][inner]
        for orient in (-1, 1):
            pieces = [slice(1, -1), slice(1, -1), slice(1, -1)]
            pieces[dim_index] = slice(1 + orient, padded.shape[dim_index + 1] - 1 + orient)
            pieces = tuple(pieces)
            t_other = perm_pad[dim_index][pieces]
            face_trans = 2.0 * t_centre * t_other / (t_centre + t_other)
            depth_step = float(orient) if dim_index == 2 else 0.0
            summed = summed + face_inflow(p_centre, mob_centre, padded[0][pieces], mobility[(slice(None),) + pieces], face_trans, depth_step)
    return summed

def fault_inflow(own_vals, partner, conn_trans):
    _, _, mob_own = properties(own_vals)
    _, _, mob_other = properties(partner)
    return face_inflow(own_vals[0], mob_own, partner[0], mob_other, conn_trans, 0.0)

def well_block(segments, live_seg, seg_index, head_press, goal_rate):
    _, _, mobility = properties(segments)
    total_mob = mobility[0] + mobility[1] + mobility[2]
    mix_density = (mobility[0] * DENSITY[0] + mobility[1] * DENSITY[1] + mobility[2] * DENSITY[2]) / total_mob
    head_sum = jnp.cumsum(live_seg * mix_density, axis=-1)
    seg_press = head_press[..., None] + HEAD_SCALE * head_sum
    seg_rates = live_seg * seg_index * mobility * (segments[0] - seg_press)
    return (seg_rates, lax.optimization_barrier(jnp.sum(seg_rates, axis=(0, -1))) / goal_rate - 1.0)

def forward_parts(function, primals):
    outputs, pullback = jax.vjp(function, *primals)
    zero_out = jax.tree.map(jnp.zeros_like, outputs)
    _, second_pull = jax.vjp(pullback, zero_out)
    return (outputs, second_pull)

def tangent_of(second_pull, tangents):
    return second_pull(tuple(tangents))[0]

def tile_view(field):
    return field.reshape(3, TILES_X, CX, TILES_Y, CY, NZ).transpose(0, 1, 3, 2, 4, 5).reshape(3, TILES_X, TILES_Y, CELLS)

def grid_view(tiled):
    return tiled.reshape(3, TILES_X, TILES_Y, CX, CY, NZ).transpose(0, 1, 3, 2, 4, 5).reshape(3, NX, NY, NZ)

def pick_cells(tiled, cell_ids):
    flat_ids = cell_ids.reshape(TILES_X, TILES_Y, -1)
    wide_ids = jnp.broadcast_to(flat_ids[None], (3,) + flat_ids.shape)
    return jnp.take_along_axis(tiled, wide_ids, axis=3)

def reference(state, perm, pore, old_mass, scaling, fault_cell, fault_tile, fault_row, fault_trans, fault_export, perf_cell, well_segments, well_index, bhp, target):
    pad_all = ((0, 0), (1, 1), (1, 1), (1, 1))
    perm_pad = jnp.pad(perm, pad_all)
    tile_base = (jnp.arange(TILES_X * TILES_Y, dtype=jnp.int32) * CELLS).reshape(TILES_X, TILES_Y, 1)
    live_slot = (perf_cell >= 0).astype(jnp.float32)
    slot_cell = jnp.maximum(perf_cell, 0)
    live_seg = (lax.broadcasted_iota(jnp.int32, (TILES_X, TILES_Y, W_DEV, SEG), 3) < well_segments[..., None]).astype(jnp.float32)
    slot_global = (tile_base.reshape(TILES_X, TILES_Y, 1, 1, 1, 1) + slot_cell).reshape(-1)
    fault_global = (tile_base + fault_cell).reshape(-1)

    def residual_of(field):
        saturation, factor, _ = properties(field)
        cell_res = pore[None] * factor * saturation - old_mass - cell_inflow(jnp.pad(field, pad_all), perm_pad)
        flat_res = tile_view(cell_res).reshape(3, -1)
        tiled = tile_view(field)
        table_rows = pick_cells(tiled, fault_export).reshape(3, TILES_X * TILES_Y, FE)
        own_vals = pick_cells(tiled, fault_cell)
        partner = table_rows[:, fault_tile, fault_row]
        flat_res = flat_res.at[:, fault_global].add(-fault_inflow(own_vals, partner, fault_trans).reshape(3, -1))
        outgoing = pick_cells(tiled, slot_cell).reshape(3, TILES_X, TILES_Y, 3, 3, W_DEV, SEG) * live_slot[None]
        out_pad = jnp.pad(outgoing, ((0, 0), (1, 1), (1, 1), (0, 0), (0, 0), (0, 0), (0, 0)))
        segments = jnp.zeros((3, TILES_X, TILES_Y, W_DEV, SEG), jnp.float32)
        for along_x in range(3):
            for along_y in range(3):
                segments = segments + out_pad[:, along_x:along_x + TILES_X, along_y:along_y + TILES_Y, 2 - along_x, 2 - along_y]
        seg_rates, well_res = well_block(segments, live_seg, well_index, bhp, target)
        rate_pad = jnp.pad(seg_rates, ((0, 0), (1, 1), (1, 1), (0, 0), (0, 0)))
        returned = jnp.stack([jnp.stack([rate_pad[:, along_x:along_x + TILES_X, along_y:along_y + TILES_Y] for along_y in range(3)], axis=3) for along_x in range(3)], axis=3)
        returned = returned * live_slot[None]
        flat_res = flat_res.at[:, slot_global].add(returned.reshape(3, -1))
        return (grid_view(flat_res.reshape(3, TILES_X, TILES_Y, CELLS)), well_res)
    current = state
    for step_index in range(2):
        outputs, second_pull = forward_parts(residual_of, (current,))
        cell_res, well_res = outputs
        direction = scaling * cell_res
        tangents = tangent_of(second_pull, (direction,))
        newton = 2.0 * direction - scaling * tangents[0]
        if step_index == 0:
            current = current - newton
    return (cell_res, newton, well_res)
```

```python
import functools

import jax
import jax.numpy as jnp
from jax import lax
from jax.experimental import pallas as pl
from jax.experimental.pallas import tpu as pltpu
from jax.sharding import PartitionSpec as P

VISCOSITY = (0.5, 2.0, 0.1)
COMPRESS = (0.02, 0.05, 0.3)
DENSITY = (1.0, 0.8, 0.2)
GRAVITY = 0.2
INV_SMOOTHING = 10.0
HEAD_SCALE = 0.3

LANES = 128
PACK = 32
PLANE = 16
VMEM_BYTES = 40 * 1024 * 1024
F32 = jnp.float32
BF16 = jnp.bfloat16


def props(field):
    p, sw, sg = field
    sats = (sw, 1.0 - sw - sg, sg)
    factors = tuple(jnp.exp(COMPRESS[a] * p) for a in range(3))
    return sats, factors


def mobilities(sats, factors):
    return tuple(sats[a] * sats[a] * factors[a] * (1.0 / VISCOSITY[a]) for a in range(3))


def tangents(sats, factors, mob, dfield):
    dp, dsw, dsg = dfield
    dsats = (dsw, -(dsw + dsg), dsg)
    dmob = tuple(
        mob[a] * (COMPRESS[a] * dp) + sats[a] * factors[a] * (2.0 / VISCOSITY[a]) * dsats[a]
        for a in range(3)
    )
    return dsats, dmob


def face(trans, p_c, mob_c, p_n, mob_n, depth=0.0):
    out = []
    diff = p_n - p_c
    for a in range(3):
        if a == 0 or depth:
            pot = diff - GRAVITY * DENSITY[a] * depth if depth else diff
            weight = jax.nn.sigmoid(pot * INV_SMOOTHING)
            scaled = trans * pot
        out.append(scaled * (mob_c[a] + weight * (mob_n[a] - mob_c[a])))
    return out


def face_tangent(trans, p_c, mob_c, p_n, mob_n, dp_c, dmob_c, dp_n, dmob_n, depth=0.0):
    out = []
    diff = p_n - p_c
    ddiff = dp_n - dp_c
    for a in range(3):
        if a == 0 or depth:
            pot = diff - GRAVITY * DENSITY[a] * depth if depth else diff
            weight = jax.nn.sigmoid(pot * INV_SMOOTHING)
            dweight = (weight * (1.0 - weight)) * (ddiff * INV_SMOOTHING)
        step = mob_n[a] - mob_c[a]
        mean = mob_c[a] + weight * step
        dmean = dmob_c[a] + weight * (dmob_n[a] - dmob_c[a]) + dweight * step
        out.append(trans * (mean * ddiff + pot * dmean))
    return out


def split2(x):
    high = x.astype(BF16)
    return high, (x - high.astype(F32)).astype(BF16)


def one_hot_rows(idx, count):
    rows = (idx >> 7).astype(F32).astype(BF16)
    at = lax.broadcasted_iota(jnp.int32, (count, idx.shape[1]), 0).astype(F32).astype(BF16)
    return jnp.where(at == rows, jnp.ones((), BF16), jnp.zeros((), BF16))


def gather_loop(table_ref, count, idx_ref, columns, put):
    for c in range(0, columns, 256):
        width = min(256, columns - c)
        idx = idx_ref[:, c:c + width]
        hot = one_hot_rows(idx, count)
        picked = jnp.dot(
            table_ref[...], jnp.concatenate([hot, hot], axis=0), preferred_element_type=F32
        )
        lane = idx & (LANES - 1)
        for h in range(width // LANES):
            cols = slice(h * LANES, (h + 1) * LANES)
            mask = lax.broadcasted_iota(jnp.int32, (LANES, LANES), 0) == lane[:, cols]
            for f in range(3):
                block = picked[f * LANES:(f + 1) * LANES, cols]
                value = jnp.sum(jnp.where(mask, block, 0.0), axis=0, keepdims=True)
                put(c // LANES + h, f, value)


def scatter_loop(values_ref, idx_ref, columns, count):
    total = jnp.zeros((count, 3 * LANES), F32)
    for c in range(0, columns, 256):
        width = min(256, columns - c)
        idx = idx_ref[:, c:c + width]
        hot = one_hot_rows(idx, count)
        lane = (idx & (LANES - 1)).astype(F32).astype(BF16)
        at = lax.broadcasted_iota(jnp.int32, (LANES, width), 0).astype(F32).astype(BF16)
        mask = at == lane
        highs, lows = [], []
        for f in range(3):
            r = c // LANES
            row = jnp.concatenate(
                [values_ref[f, r + h:r + h + 1, :] for h in range(width // LANES)], axis=1
            )
            high, low = split2(row)
            highs.append(jnp.where(mask, high, jnp.zeros((), BF16)))
            lows.append(jnp.where(mask, low, jnp.zeros((), BF16)))
        right = jnp.concatenate(
            [jnp.concatenate(highs, axis=0), jnp.concatenate(lows, axis=0)], axis=1
        )
        left = jnp.concatenate([hot, hot], axis=1)
        total = total + lax.dot_general(
            left, right, (((1,), (1,)), ((), ())), preferred_element_type=F32
        )
    return total


def fill_table(table_ref, f, cells):
    rows = cells.shape[0]
    high, low = split2(cells.T)
    table_ref[f * LANES:(f + 1) * LANES, 0:rows] = high
    table_ref[f * LANES:(f + 1) * LANES, rows:2 * rows] = low


def emit(dims, pos_ref, field_ref, idx_ref, static_ref, table_ref, outs, perm_ref=None):
    gxa, gxb, gxp, yfa, yfb, own = outs
    cx, cy, n_fault, n_exp = dims
    rows = cx * cy
    zeros = jnp.zeros((PACK, LANES), F32)
    for ref in (gxa, gxb, gxp):
        ref[0:PACK, :] = zeros
        ref[9:11, :] = static_ref[0:2, :]
    even_x = (pos_ref[0] & 1) == 0
    even_y = (pos_ref[1] & 1) == 0
    base = PACK + 3 * n_exp

    def put_faces(out_a, out_b, at, low, high, even):
        count = low.shape[0]
        out_a[at:at + count, :] = jnp.where(even, high, low)
        out_b[at:at + count, :] = jnp.where(even, low, high)

    for f in range(3):
        put_faces(gxa, gxb, base + f * cy, field_ref[f, 0], field_ref[f, cx - 1], even_x)
        put_faces(yfa, yfb, f * cx, field_ref[f, :, 0, :], field_ref[f, :, cy - 1, :], even_y)
        fill_table(table_ref, f, field_ref[f].reshape(rows, LANES))
    if perm_ref is not None:
        put_faces(gxa, gxb, base + 3 * cy, perm_ref[0, 0], perm_ref[0, cx - 1], even_x)
        put_faces(yfa, yfb, 3 * cx, perm_ref[1, :, 0, :], perm_ref[1, :, cy - 1, :], even_y)

    def put(r, f, value):
        if r < n_fault:
            own[f * n_fault + r:f * n_fault + r + 1, :] = value
        elif r < n_fault + 6:
            plane, e = divmod(r - n_fault, 3)
            at = plane * PLANE + f * 3 + e
            for ref in (gxa, gxb, gxp):
                ref[at:at + 1, :] = value
        else:
            at = PACK + f * n_exp + r - n_fault - 6
            for ref in (gxa, gxb):
                ref[at:at + 1, :] = value

    gather_loop(table_ref, rows, idx_ref, (n_fault + 6 + n_exp) * LANES, put)


def first_kernel(dims, pos, state, perm, idx, static, *refs):
    outs, (table,) = refs[:6], refs[6:]
    emit(dims, pos, state, idx, static, table, outs, perm)


def middle_kernel(dims, far_x, pos, mine, rec_a, rec_b, *refs):
    _, _, _, n_exp = dims
    far = refs[:far_x]
    yfa, yfb, msg_a, msg_b, msg_c, pick = refs[far_x:]
    even = (pos[0] & 1) == 0
    pick[2] = mine[0:PACK, :]
    pick[3] = jnp.where(even, rec_a[0:PACK, :], rec_b[0:PACK, :])
    pick[1] = jnp.where(even, rec_b[0:PACK, :], rec_a[0:PACK, :])
    if far_x == 1:
        pick[4] = far[0][...]
        pick[0] = far[0][...]
    else:
        up = ((pos[0] >> 1) & 1) == 0
        pick[4] = jnp.where(up, far[0][...], far[1][...])
        pick[0] = jnp.where(up, far[1][...], far[0][...])
    outs = (msg_a, msg_b, msg_c)
    for ref in outs:
        ref[0:PACK, :] = jnp.zeros((PACK, LANES), F32)
    for hx in range(3):
        for plane in range(2):
            for f in range(3):
                at = plane * PLANE + f * 3
                row = (
                    pick[hx, at + 2:at + 3, :]
                    + pick[hx + 1, at + 1:at + 2, :]
                    + pick[hx + 2, at:at + 1, :]
                )
                for ref in outs:
                    ref[at + hx:at + hx + 1, :] = row
        for ref in outs:
            ref[9 + hx:10 + hx, :] = pick[hx + 1, 9:10, :]
            ref[12 + hx:13 + hx, :] = pick[hx + 1, 10:11, :]
    rows = 3 * n_exp
    src = slice(PACK, PACK + rows)
    stack = (
        jnp.where(even, rec_b[src, :], rec_a[src, :]),
        mine[src, :],
        jnp.where(even, rec_a[src, :], rec_b[src, :]),
    )
    for hx in range(3):
        at = PACK + hx * rows
        msg_a[at:at + rows, :] = stack[hx]
        msg_b[at:at + rows, :] = stack[hx]
    at = PACK + 3 * rows
    msg_a[at:at + yfa.shape[0], :] = yfa[...]
    msg_b[at:at + yfb.shape[0], :] = yfb[...]


def roll_half(x):
    return pltpu.roll(x, LANES // 2, 1)


def low_half(shape):
    return lax.broadcasted_iota(jnp.int32, shape, 1) < LANES // 2


def segment_values(packs, seg_ref):
    tops = [packs[y, 0:PLANE, :] for y in range(5)]
    bottoms = [packs[y, PLANE:PACK, :] for y in range(5)]
    lo = low_half((PLANE, LANES))

    def home(hy):
        return tops[hy + 3] + roll_half(tops[hy + 2]) + bottoms[hy + 1]

    plane0 = jnp.where(lo, home(-1), roll_half(home(0)))
    plane1 = jnp.where(lo, home(1), 0.0)
    for f in range(3):
        seg_ref[f * 8:f * 8 + 3, :] = plane0[f * 3:f * 3 + 3, :]
        seg_ref[f * 8 + 3:f * 8 + 6, :] = plane1[f * 3:f * 3 + 3, :]
        seg_ref[f * 8 + 6:f * 8 + 8, :] = jnp.zeros((2, LANES), F32)


def well_constants(packs, const_ref):
    tops = [packs[y, 0:PLANE, :] for y in (1, 2, 3)]
    rolled = [roll_half(t) for t in tops]
    lo = low_half((PLANE, LANES))
    same0 = jnp.where(lo, tops[0], rolled[1])
    same1 = jnp.where(lo, tops[2], 0.0)
    other0 = jnp.where(lo, rolled[0], tops[1])
    other1 = rolled[2]
    const_ref[...] = jnp.zeros(const_ref.shape, F32)
    for at, (a, b), src in ((0, (same0, same1), 9), (8, (other0, other1), 9), (16, (same0, same1), 12)):
        const_ref[at:at + 3, :] = a[src:src + 3, :]
        const_ref[at + 3:at + 6, :] = b[src:src + 3, :]


def running_sum(x):
    lane = lax.broadcasted_iota(jnp.int32, x.shape, 1) & 15
    for shift in (1, 2, 4, 8):
        x = x + jnp.where(lane >= shift, pltpu.roll(x, shift, 1), 0.0)
    return x


def well_mix(seg_ref):
    field = tuple(seg_ref[f * 8:f * 8 + 8, :] for f in range(3))
    sats, factors = props(field)
    mob = mobilities(sats, factors)
    total = mob[0] + mob[1] + mob[2]
    mix = (mob[0] * DENSITY[0] + mob[1] * DENSITY[1] + mob[2] * DENSITY[2]) / total
    return field, sats, factors, mob, total, mix


def well_rates(seg_ref, const_ref):
    weight, bhp, live = (const_ref[i * 8:i * 8 + 8, :] for i in range(3))
    field, _, _, mob, _, mix = well_mix(seg_ref)
    press = bhp + HEAD_SCALE * running_sum(live * mix)
    return [weight * mob[a] * (field[0] - press) for a in range(3)]


def well_rate_tangents(seg_ref, dseg_ref, const_ref):
    weight, bhp, live = (const_ref[i * 8:i * 8 + 8, :] for i in range(3))
    field, sats, factors, mob, total, mix = well_mix(seg_ref)
    press = bhp + HEAD_SCALE * running_sum(live * mix)
    dfield = tuple(dseg_ref[f * 8:f * 8 + 8, :] for f in range(3))
    _, dmob = tangents(sats, factors, mob, dfield)
    dtotal = dmob[0] + dmob[1] + dmob[2]
    dnum = dmob[0] * DENSITY[0] + dmob[1] * DENSITY[1] + dmob[2] * DENSITY[2]
    dpress = HEAD_SCALE * running_sum(live * ((dnum - mix * dtotal) / total))
    return [
        weight * (dmob[a] * (field[0] - press) + mob[a] * (dfield[0] - dpress)) for a in range(3)
    ]


def stack_received(dims, pos, mine, rec_a, rec_b, far, packs, partner):
    _, _, _, n_exp = dims
    even = (pos[1] & 1) == 0
    packs[2] = mine[0:PACK, :]
    packs[3] = jnp.where(even, rec_a[0:PACK, :], rec_b[0:PACK, :])
    packs[1] = jnp.where(even, rec_b[0:PACK, :], rec_a[0:PACK, :])
    if len(far) == 1:
        packs[4] = far[0][...]
        packs[0] = far[0][...]
    else:
        up = ((pos[1] >> 1) & 1) == 0
        packs[4] = jnp.where(up, far[0][...], far[1][...])
        packs[0] = jnp.where(up, far[1][...], far[0][...])
    used = 9 * n_exp
    for f in range(3):
        for hx in range(3):
            at = PACK + hx * 3 * n_exp + f * n_exp
            src = slice(at, at + n_exp)
            first, second = rec_a[src, :], rec_b[src, :]
            blocks = (jnp.where(even, second, first), mine[src, :], jnp.where(even, first, second))
            for hy in range(3):
                to = (hx * 3 + hy) * n_exp
                partner[f, to:to + n_exp, :] = blocks[hy]
        partner[f, used:LANES, :] = jnp.zeros((LANES - used, LANES), F32)


def pick_partners(dims, partner, pidx, table, out):
    _, _, n_fault, _ = dims
    for f in range(3):
        fill_table(table, f, partner[f])

    def put(r, f, value):
        out[f * n_fault + r:f * n_fault + r + 1, :] = value

    gather_loop(table, LANES, pidx, n_fault * LANES, put)


def x_halo(dims, pos, rec_a, rec_b, at, count):
    even = (pos[0] & 1) == 0
    a, b = rec_a[at:at + count, :], rec_b[at:at + count, :]
    return jnp.where(even, b, a), jnp.where(even, a, b)


def y_halo(dims, pos, rec_a, rec_b, at, count):
    even = (pos[1] & 1) == 0
    a, b = rec_a[at:at + count, :], rec_b[at:at + count, :]
    return jnp.where(even, b, a), jnp.where(even, a, b)


def halo_fields(dims, pos, gx_a, gx_b, gy_a, gy_b):
    cx, cy, _, n_exp = dims
    xs = [x_halo(dims, pos, gx_a, gx_b, PACK + 3 * n_exp + f * cy, cy) for f in range(3)]
    ys = [y_halo(dims, pos, gy_a, gy_b, PACK + 9 * n_exp + f * cx, cx) for f in range(3)]
    return (
        [tuple(v[side] for v in xs) for side in range(2)],
        [tuple(v[side] for v in ys) for side in range(2)],
    )


def edge_trans(t_a, t_b):
    return 2.0 * t_a * t_b / (t_a + t_b)


def make_trans(dims, sizes, pos, perm, gx_a, gx_b, gy_a, gy_b, fx, fy, fym, fz):
    cx, cy, _, n_exp = dims
    low_x, high_x = x_halo(dims, pos, gx_a, gx_b, PACK + 3 * n_exp + 3 * cy, cy)
    low_y, high_y = y_halo(dims, pos, gy_a, gy_b, PACK + 9 * n_exp + 3 * cx, cx)
    inside = (pos[0] > 0, pos[0] < sizes[0] - 1, pos[1] > 0, pos[1] < sizes[1] - 1)
    fx[0] = jnp.where(inside[0], edge_trans(low_x, perm[0, 0]), 0.0)
    fx[cx] = jnp.where(inside[1], edge_trans(perm[0, cx - 1], high_x), 0.0)
    fym[...] = jnp.where(inside[2], edge_trans(low_y, perm[1, :, 0, :]), 0.0)
    last_row = lax.broadcasted_iota(jnp.int32, (cy, LANES), 0) == cy - 1
    last_lane = lax.broadcasted_iota(jnp.int32, (cy, LANES), 1) == LANES - 1
    for x in range(cx):
        if x:
            fx[x] = edge_trans(perm[0, x - 1], perm[0, x])
        t = perm[1, x]
        beside = jnp.where(last_row, high_y[x:x + 1, :], pltpu.roll(t, cy - 1, 0))
        value = edge_trans(t, beside)
        fy[x] = jnp.where(jnp.logical_and(last_row, jnp.logical_not(inside[3])), 0.0, value)
        t = perm[2, x]
        fz[x] = jnp.where(last_lane, 0.0, edge_trans(t, pltpu.roll(t, LANES - 1, 1)))


def down_row(flux, first):
    rows = flux.shape[0]
    at = lax.broadcasted_iota(jnp.int32, flux.shape, 0)
    return jnp.where(at == 0, first, pltpu.roll(flux, 1, 0))


def up_row(value, last):
    rows = value.shape[0]
    at = lax.broadcasted_iota(jnp.int32, value.shape, 0)
    return jnp.where(at == rows - 1, last, pltpu.roll(value, rows - 1, 0))


def plane_state(field_ref, x):
    field = tuple(field_ref[f, x] for f in range(3))
    sats, factors = props(field)
    return field, sats, factors, mobilities(sats, factors)


def own_rows(ref, x, row):
    return ref[:, row, :]


def residual_planes(dims, field, pore, old_mass, trans, halos, acc):
    cx, cy, _, _ = dims
    fx, fy, fym, fz = trans
    (low_x, high_x), (low_y, high_y) = halos
    mob_of = lambda fld: mobilities(*props(fld))
    mob_hy = mob_of(high_y)
    first_row = tuple(field[f, :, 0, :] for f in range(3))
    flux_ym = face(fym[...], low_y[0], mob_of(low_y), first_row[0], mob_of(first_row))
    cur = plane_state(field, 0)
    below = face(fx[0], low_x[0], mob_of(low_x), cur[0][0], cur[3])
    for x in range(cx):
        fld, sats, factors, mob = cur
        p = fld[0]
        if x + 1 < cx:
            nxt = plane_state(field, x + 1)
            above = face(fx[x + 1], p, mob, nxt[0][0], nxt[3])
        else:
            nxt = None
            above = face(fx[cx], p, mob, high_x[0], mob_of(high_x))
        y_up = face(
            fy[x], p, mob,
            up_row(p, high_y[0][x:x + 1, :]),
            [up_row(mob[a], mob_hy[a][x:x + 1, :]) for a in range(3)],
        )
        z_up = face(
            fz[x], p, mob,
            pltpu.roll(p, LANES - 1, 1),
            [pltpu.roll(mob[a], LANES - 1, 1) for a in range(3)],
            1.0,
        )
        for a in range(3):
            inflow = (
                (above[a] - below[a])
                + (y_up[a] - down_row(y_up[a], flux_ym[a][x:x + 1, :]))
                + (z_up[a] - pltpu.roll(z_up[a], 1, 1))
            )
            acc[a, x * cy:(x + 1) * cy, :] = pore[x] * (factors[a] * sats[a]) - old_mass[a, x] - inflow
        cur, below = nxt, above


def jacobian_planes(dims, field, dfield, pore, trans, halos, dhalos, acc):
    cx, cy, _, _ = dims
    fx, fy, fym, fz = trans
    (low_x, high_x), (low_y, high_y) = halos
    (dlow_x, dhigh_x), (dlow_y, dhigh_y) = dhalos

    def point(fld, dfld):
        sats, factors = props(fld)
        mob = mobilities(sats, factors)
        dsats, dmob = tangents(sats, factors, mob, dfld)
        return fld[0], mob, dfld[0], dmob, sats, factors, dsats

    def plane(x):
        return point(tuple(field[f, x] for f in range(3)), tuple(dfield[f, x] for f in range(3)))

    def between(t, c, n, depth=0.0):
        return face_tangent(t, c[0], c[1], n[0], n[1], c[2], c[3], n[2], n[3], depth)

    hy = point(high_y, dhigh_y)
    row0 = point(
        tuple(field[f, :, 0, :] for f in range(3)), tuple(dfield[f, :, 0, :] for f in range(3))
    )
    flux_ym = between(fym[...], point(low_y, dlow_y), row0)
    cur = plane(0)
    below = between(fx[0], point(low_x, dlow_x), cur)
    for x in range(cx):
        nxt = plane(x + 1) if x + 1 < cx else point(high_x, dhigh_x)
        above = between(fx[x + 1], cur, nxt)
        row = slice(x, x + 1)
        beside = (
            up_row(cur[0], hy[0][row, :]),
            [up_row(cur[1][a], hy[1][a][row, :]) for a in range(3)],
            up_row(cur[2], hy[2][row, :]),
            [up_row(cur[3][a], hy[3][a][row, :]) for a in range(3)],
        )
        y_up = between(fy[x], cur, beside)
        shift = lambda v: pltpu.roll(v, LANES - 1, 1)
        over = (
            shift(cur[0]),
            [shift(cur[1][a]) for a in range(3)],
            shift(cur[2]),
            [shift(cur[3][a]) for a in range(3)],
        )
        z_up = between(fz[x], cur, over, 1.0)
        _, _, dp, _, sats, factors, dsats = cur
        for a in range(3):
            inflow = (
                (above[a] - below[a])
                + (y_up[a] - down_row(y_up[a], flux_ym[a][row, :]))
                + (z_up[a] - pltpu.roll(z_up[a], 1, 1))
            )
            gain = pore[x] * (factors[a] * (dsats[a] + COMPRESS[a] * sats[a] * dp))
            acc[a, x * cy:(x + 1) * cy, :] = gain - inflow
        cur, below = nxt, above


def rows_of(ref, count):
    return tuple(ref[f * count:(f + 1) * count, :] for f in range(3))


def connection_trans(ftrans, tr, n_fault):
    for r in range(n_fault):
        tr[r:r + 1, :] = ftrans[:, r * LANES:(r + 1) * LANES]


def residual_kernel(dims, sizes, make, final, far_y, pos, *refs):
    cx, cy, n_fault, n_exp = dims
    rows = cx * cy
    refs = list(refs)
    take = lambda n: [refs.pop(0) for _ in range(n)]
    field, pore, old_mass, scaling, idx, pidx, ftrans, static, own = take(9)
    gx_a, gx_b, mine, gy_a, gy_b = take(5)
    far = take(far_y)
    if make:
        (perm,) = take(1)
    else:
        trans = take(4)
    direction, partner_vals, seg, const = take(4)
    outs = take(6)
    if make:
        trans = take(4)
    if final:
        residual, well = take(2)
    acc, packs, partner, values, tr, table, ptable = take(7)

    if make:
        make_trans(dims, sizes, pos, perm, gx_a, gx_b, gy_a, gy_b, *trans)
    stack_received(dims, pos, mine, gy_a, gy_b, far, packs, partner)
    pick_partners(dims, partner, pidx, ptable, partner_vals)
    connection_trans(ftrans, tr, n_fault)
    mine_f, other_f = rows_of(own, n_fault), rows_of(partner_vals, n_fault)
    mob_of = lambda fld: mobilities(*props(fld))
    flux = face(tr[...], mine_f[0], mob_of(mine_f), other_f[0], mob_of(other_f))
    segment_values(packs, seg)
    well_constants(packs, const)
    rates = well_rates(seg, const)
    for a in range(3):
        values[a, 0:n_fault, :] = -flux[a]
        values[a, n_fault:n_fault + 8, :] = rates[a]
    if final:
        done = running_sum(rates[0] + rates[1] + rates[2])[1:2, :]
        well[...] = done / packs[2, 13:14, :] - 1.0
    halos = halo_fields(dims, pos, gx_a, gx_b, gy_a, gy_b)
    residual_planes(dims, field, pore, old_mass, trans, halos, acc)
    total = scatter_loop(values, idx, (n_fault + 6) * LANES, rows)
    for a in range(3):
        res = (acc[a] + total[:, a * LANES:(a + 1) * LANES]).reshape(cx, cy, LANES)
        if final:
            residual[a] = res
        direction[a] = scaling[a] * res
    emit(dims, pos, direction, idx, static, table, outs)


def jacobian_kernel(dims, final, far_y, pos, *refs):
    cx, cy, n_fault, n_exp = dims
    rows = cx * cy
    refs = list(refs)
    take = lambda n: [refs.pop(0) for _ in range(n)]
    field, direction, pore, scaling, idx, pidx, ftrans, static = take(8)
    own, other, seg, const, down = take(5)
    trans = take(4)
    gx_a, gx_b, gy_a, gy_b = take(4)
    dgx_a, dgx_b, mine, dgy_a, dgy_b = take(5)
    far = take(far_y)
    (result,) = take(1)
    outs = None if final else take(6)
    acc, packs, partner, values, tr, ptable, dother, dseg = take(8)
    table = None if final else take(1)[0]

    stack_received(dims, pos, mine, dgy_a, dgy_b, far, packs, partner)
    pick_partners(dims, partner, pidx, ptable, dother)
    connection_trans(ftrans, tr, n_fault)

    def point(fld, dfld):
        sats, factors = props(fld)
        mob = mobilities(sats, factors)
        return fld[0], mob, dfld[0], tangents(sats, factors, mob, dfld)[1]

    c = point(rows_of(own, n_fault), rows_of(down, n_fault))
    n = point(rows_of(other, n_fault), rows_of(dother, n_fault))
    flux = face_tangent(tr[...], c[0], c[1], n[0], n[1], c[2], c[3], n[2], n[3])
    segment_values(packs, dseg)
    rates = well_rate_tangents(seg, dseg, const)
    for a in range(3):
        values[a, 0:n_fault, :] = -flux[a]
        values[a, n_fault:n_fault + 8, :] = rates[a]
    halos = halo_fields(dims, pos, gx_a, gx_b, gy_a, gy_b)
    dhalos = halo_fields(dims, pos, dgx_a, dgx_b, dgy_a, dgy_b)
    jacobian_planes(dims, field, direction, pore, trans, halos, dhalos, acc)
    total = scatter_loop(values, idx, (n_fault + 6) * LANES, rows)
    for a in range(3):
        jac = (acc[a] + total[:, a * LANES:(a + 1) * LANES]).reshape(cx, cy, LANES)
        step = 2.0 * direction[a] - scaling[a] * jac
        result[a] = step if final else field[a] - step
    if not final:
        emit(dims, pos, result, idx, static, table, outs)


def pair_swap(count, odd):
    out = list(range(count))
    for i in range(odd, count if odd else count - 1, 2):
        j = (i + 1) % count
        out[i], out[j] = j, i
    return [(i, out[i]) for i in range(count)]


def far_swap(count, late):
    if late:
        return [(i, (((i + 2) % count) ^ 2) - 2 if (((i + 2) % count) ^ 2) >= 2 else (((i + 2) % count) ^ 2) - 2 + count) for i in range(count)]
    return [(i, i ^ 2) for i in range(count)]


def body(
    state, perm, pore, old_mass, scaling, fault_cell, fault_tile, fault_row, fault_trans,
    fault_export, perf_cell, well_segments, well_index, bhp, target,
):
    size_x, size_y = lax.axis_size("gx"), lax.axis_size("gy")
    _, cx, cy, _ = state.shape
    wells, segs = well_index.shape[2:]
    n_fault, n_exp = fault_cell.shape[-1] // LANES, fault_export.shape[-1] // LANES
    dims = (cx, cy, n_fault, n_exp)
    far_x = 1 if size_x == 4 else 2
    far_y = 1 if size_y == 4 else 2
    at_x, at_y = lax.axis_index("gx"), lax.axis_index("gy")
    pos = jnp.stack([at_x, at_y]).astype(jnp.int32)

    slots = perf_cell.reshape(3, 3, wells * segs)
    empty = jnp.full((3, wells * segs), -1, jnp.int32)
    planes = jnp.stack([slots[:, 0], slots[:, 1], slots[:, 2], empty], axis=1).reshape(3, 2, LANES)
    idx = jnp.concatenate(
        [fault_cell.reshape(1, -1), planes.transpose(1, 0, 2).reshape(1, -1), fault_export.reshape(1, -1)],
        axis=1,
    )
    tile = fault_tile.reshape(1, -1)
    across = tile // size_y - at_x + 1
    along = tile % size_y - at_y + 1
    pidx = (across * 3 + along) * (n_exp * LANES) + fault_row.reshape(1, -1)
    ftrans = fault_trans.reshape(1, -1)
    live = (
        lax.broadcasted_iota(jnp.int32, (wells, segs), 1) < well_segments.reshape(wells, 1)
    ).astype(F32)
    wide = lambda v: jnp.broadcast_to(v.reshape(wells, 1), (wells, segs)).reshape(-1)
    static = jnp.concatenate(
        [
            (live * well_index.reshape(wells, segs)).reshape(-1), wide(bhp),
            live.reshape(-1), wide(target),
            jnp.zeros((6 * LANES,), F32),
        ]
    ).reshape(8, LANES)

    params = pltpu.CompilerParams(vmem_limit_bytes=VMEM_BYTES)
    smem = pl.BlockSpec(memory_space=pltpu.SMEM)
    vmem = pl.BlockSpec(memory_space=pltpu.VMEM)
    shape = lambda *dims_: jax.ShapeDtypeStruct(dims_, F32)
    rows = cx * cy
    gx_rows = PACK + 3 * n_exp + 3 * cy
    gy_rows = PACK + 9 * n_exp + 3 * cx
    table = pltpu.VMEM((3 * LANES, 2 * rows), BF16)

    def call(kernel, args, outs, scratch):
        return pl.pallas_call(
            kernel,
            out_shape=outs,
            in_specs=[smem] + [vmem] * (len(args) - 1),
            out_specs=[vmem] * len(outs),
            scratch_shapes=scratch,
            compiler_params=params,
        )(*args)

    def message_shapes(first):
        more_x, more_y = (cy, cx) if first else (0, 0)
        return [
            shape(gx_rows + more_x, LANES), shape(gx_rows + more_x, LANES), shape(PACK, LANES),
            shape(3 * cx + more_y, LANES), shape(3 * cx + more_y, LANES), shape(3 * n_fault, LANES),
        ]

    def exchange(messages):
        msg_a, msg_b, packet, yfa, yfb, own = messages
        rec_a = lax.ppermute(msg_a, "gx", pair_swap(size_x, 0))
        rec_b = lax.ppermute(msg_b, "gx", pair_swap(size_x, 1))
        far = [lax.ppermute(packet, "gx", far_swap(size_x, k)) for k in range(far_x)]
        total = PACK + 9 * n_exp + yfa.shape[0]
        mid_a, mid_b, mid_c = call(
            functools.partial(middle_kernel, dims, far_x),
            [pos, msg_a, rec_a, rec_b, *far, yfa, yfb],
            [shape(total, LANES), shape(total, LANES), shape(PACK, LANES)],
            [pltpu.VMEM((5, PACK, LANES), F32)],
        )
        got_a = lax.ppermute(mid_a, "gy", pair_swap(size_y, 0))
        got_b = lax.ppermute(mid_b, "gy", pair_swap(size_y, 1))
        got_far = [lax.ppermute(mid_c, "gy", far_swap(size_y, k)) for k in range(far_y)]
        return (rec_a, rec_b), (mid_a, got_a, got_b, *got_far)

    work = [
        pltpu.VMEM((3, rows, LANES), F32), pltpu.VMEM((5, PACK, LANES), F32),
        pltpu.VMEM((3, LANES, LANES), F32), pltpu.VMEM((3, n_fault + 8, LANES), F32),
        pltpu.VMEM((n_fault, LANES), F32),
    ]
    ptable = pltpu.VMEM((3 * LANES, 2 * LANES), BF16)
    grid = shape(3, cx, cy, LANES)
    wide_rows = shape(3 * n_fault, LANES)
    small = shape(24, LANES)

    messages = call(
        functools.partial(first_kernel, dims), [pos, state, perm, idx, static],
        message_shapes(True), [table],
    )
    current = state
    trans = None
    for step in range(2):
        final = step == 1
        own = messages[5]
        gx_got, gy_got = exchange(messages)
        results = call(
            functools.partial(residual_kernel, dims, (size_x, size_y), not final, final, far_y),
            [pos, current, pore, old_mass, scaling, idx, pidx, ftrans, static, own, *gx_got, *gy_got]
            + ([*trans] if final else [perm]),
            [grid, wide_rows, small, small] + message_shapes(False)
            + ([grid, shape(1, LANES)] if final else
               [shape(cx + 1, cy, LANES), shape(cx, cy, LANES), shape(cx, LANES), shape(cx, cy, LANES)]),
            work + [table, ptable],
        )
        direction, other, seg, const = results[:4]
        messages = results[4:10]
        if final:
            residual, well = results[10:]
        else:
            trans = results[10:]
        down = messages[5]
        dgx_got, dgy_got = exchange(messages)
        results = call(
            functools.partial(jacobian_kernel, dims, final, far_y),
            [pos, current, direction, pore, scaling, idx, pidx, ftrans, static, own, other, seg, const, down,
             *trans, *gx_got, gy_got[1], gy_got[2], *dgx_got, *dgy_got],
            [grid] + ([] if final else message_shapes(False)),
            work + [ptable, pltpu.VMEM((3 * n_fault, LANES), F32), pltpu.VMEM((24, LANES), F32)]
            + ([] if final else [table]),
        )
        current, messages = results[0], results[1:]
    half = LANES // 2
    well_res = well[0, half:].reshape(wells, segs)[:, segs - 1]
    return residual, current, well_res.reshape(1, 1, wells)


def solution(mesh):
    grid = P(None, "gx", "gy", None)
    tile = P("gx", "gy", None)
    return jax.shard_map(
        body,
        mesh=mesh,
        in_specs=(
            grid, grid, tile, grid, grid, tile, tile, tile, tile, tile,
            P("gx", "gy", None, None, None, None), tile, P("gx", "gy", None, None), tile, tile,
        ),
        out_specs=(grid, grid, tile),
        check_vma=False,
    )
```

```python
import functools

import jax
import jax.numpy as jnp
from jax import lax
from jax.experimental import pallas as pl
from jax.experimental.pallas import tpu as pltpu
from jax.sharding import PartitionSpec as P

VISCOSITY = (0.5, 2.0, 0.1)
COMPRESS = (0.02, 0.05, 0.3)
DENSITY = (1.0, 0.8, 0.2)
GRAVITY = 0.2
INV_SMOOTHING = 10.0
HEAD_SCALE = 0.3

LANES = 128
PACK = 32
PLANE = 16
VMEM_BYTES = 40 * 1024 * 1024
F32 = jnp.float32
BF16 = jnp.bfloat16


def props(field):
    p, sw, sg = field
    sats = (sw, 1.0 - sw - sg, sg)
    factors = tuple(jnp.exp(COMPRESS[a] * p) for a in range(3))
    return sats, factors


def mobilities(sats, factors):
    return tuple(sats[a] * sats[a] * factors[a] * (1.0 / VISCOSITY[a]) for a in range(3))


def tangents(sats, factors, mob, dfield):
    dp, dsw, dsg = dfield
    dsats = (dsw, -(dsw + dsg), dsg)
    dmob = tuple(
        mob[a] * (COMPRESS[a] * dp) + sats[a] * factors[a] * (2.0 / VISCOSITY[a]) * dsats[a]
        for a in range(3)
    )
    return dsats, dmob


def face(trans, p_c, mob_c, p_n, mob_n, depth=0.0):
    out = []
    diff = p_n - p_c
    for a in range(3):
        if a == 0 or depth:
            pot = diff - GRAVITY * DENSITY[a] * depth if depth else diff
            weight = jax.nn.sigmoid(pot * INV_SMOOTHING)
            scaled = trans * pot
        out.append(scaled * (mob_c[a] + weight * (mob_n[a] - mob_c[a])))
    return out


def face_tangent(trans, p_c, mob_c, p_n, mob_n, dp_c, dmob_c, dp_n, dmob_n, depth=0.0):
    out = []
    diff = p_n - p_c
    ddiff = dp_n - dp_c
    for a in range(3):
        if a == 0 or depth:
            pot = diff - GRAVITY * DENSITY[a] * depth if depth else diff
            weight = jax.nn.sigmoid(pot * INV_SMOOTHING)
            dweight = (weight * (1.0 - weight)) * (ddiff * INV_SMOOTHING)
        step = mob_n[a] - mob_c[a]
        mean = mob_c[a] + weight * step
        dmean = dmob_c[a] + weight * (dmob_n[a] - dmob_c[a]) + dweight * step
        out.append(trans * (mean * ddiff + pot * dmean))
    return out


def split2(x):
    high = x.astype(BF16)
    return high, (x - high.astype(F32)).astype(BF16)


def one_hot_rows(idx, count):
    rows = (idx >> 7).astype(F32).astype(BF16)
    at = lax.broadcasted_iota(jnp.int32, (count, idx.shape[1]), 0).astype(F32).astype(BF16)
    return jnp.where(at == rows, jnp.ones((), BF16), jnp.zeros((), BF16))


def gather_loop(table_ref, count, idx_ref, columns, put):
    for c in range(0, columns, 256):
        width = min(256, columns - c)
        idx = idx_ref[:, c:c + width]
        hot = one_hot_rows(idx, count)
        picked = jnp.dot(
            table_ref[...], jnp.concatenate([hot, hot], axis=0), preferred_element_type=F32
        )
        lane = idx & (LANES - 1)
        for h in range(width // LANES):
            cols = slice(h * LANES, (h + 1) * LANES)
            mask = lax.broadcasted_iota(jnp.int32, (LANES, LANES), 0) == lane[:, cols]
            for f in range(3):
                block = picked[f * LANES:(f + 1) * LANES, cols]
                value = jnp.sum(jnp.where(mask, block, 0.0), axis=0, keepdims=True)
                put(c // LANES + h, f, value)


def scatter_loop(values_ref, idx_ref, columns, count):
    total = jnp.zeros((count, 3 * LANES), F32)
    for c in range(0, columns, 256):
        width = min(256, columns - c)
        idx = idx_ref[:, c:c + width]
        hot = one_hot_rows(idx, count)
        lane = (idx & (LANES - 1)).astype(F32).astype(BF16)
        at = lax.broadcasted_iota(jnp.int32, (LANES, width), 0).astype(F32).astype(BF16)
        mask = at == lane
        highs, lows = [], []
        for f in range(3):
            r = c // LANES
            row = jnp.concatenate(
                [values_ref[f, r + h:r + h + 1, :] for h in range(width // LANES)], axis=1
            )
            high, low = split2(row)
            highs.append(jnp.where(mask, high, jnp.zeros((), BF16)))
            lows.append(jnp.where(mask, low, jnp.zeros((), BF16)))
        right = jnp.concatenate(
            [jnp.concatenate(highs, axis=0), jnp.concatenate(lows, axis=0)], axis=1
        )
        left = jnp.concatenate([hot, hot], axis=1)
        total = total + lax.dot_general(
            left, right, (((1,), (1,)), ((), ())), preferred_element_type=F32
        )
    return total


def fill_table(table_ref, f, cells):
    rows = cells.shape[0]
    high, low = split2(cells.T)
    table_ref[f * LANES:(f + 1) * LANES, 0:rows] = high
    table_ref[f * LANES:(f + 1) * LANES, rows:2 * rows] = low


def emit(dims, pos_ref, field_ref, idx_ref, static_ref, table_ref, outs, perm_ref=None):
    gxa, gxb, gxp, yfa, yfb, own = outs
    cx, cy, n_fault, n_exp = dims
    rows = cx * cy
    zeros = jnp.zeros((PACK, LANES), F32)
    for ref in (gxa, gxb, gxp):
        ref[0:PACK, :] = zeros
        ref[9:11, :] = static_ref[0:2, :]
    even_x = (pos_ref[0] & 1) == 0
    even_y = (pos_ref[1] & 1) == 0
    base = PACK + 3 * n_exp

    def put_faces(out_a, out_b, at, low, high, even):
        count = low.shape[0]
        out_a[at:at + count, :] = jnp.where(even, high, low)
        out_b[at:at + count, :] = jnp.where(even, low, high)

    for f in range(3):
        put_faces(gxa, gxb, base + f * cy, field_ref[f, 0], field_ref[f, cx - 1], even_x)
        put_faces(yfa, yfb, f * cx, field_ref[f, :, 0, :], field_ref[f, :, cy - 1, :], even_y)
        fill_table(table_ref, f, field_ref[f].reshape(rows, LANES))
    if perm_ref is not None:
        put_faces(gxa, gxb, base + 3 * cy, perm_ref[0, 0], perm_ref[0, cx - 1], even_x)
        put_faces(yfa, yfb, 3 * cx, perm_ref[1, :, 0, :], perm_ref[1, :, cy - 1, :], even_y)

    def put(r, f, value):
        if r < n_fault:
            own[f * n_fault + r:f * n_fault + r + 1, :] = value
        elif r < n_fault + 6:
            plane, e = divmod(r - n_fault, 3)
            at = plane * PLANE + f * 3 + e
            for ref in (gxa, gxb, gxp):
                ref[at:at + 1, :] = value
        else:
            at = PACK + f * n_exp + r - n_fault - 6
            for ref in (gxa, gxb):
                ref[at:at + 1, :] = value

    gather_loop(table_ref, rows, idx_ref, (n_fault + 6 + n_exp) * LANES, put)


def first_kernel(dims, pos, state, perm, idx, static, *refs):
    outs, (table,) = refs[:6], refs[6:]
    emit(dims, pos, state, idx, static, table, outs, perm)


def choose_packets(at, count, mine, rec_a, rec_b, far, pick):
    even = (at & 1) == 0
    near = slice(0, PACK)
    a, b = rec_a[near, :], rec_b[near, :]
    if len(far) == 1:
        up_far = down_far = far[0][...]
    else:
        up = ((at >> 1) & 1) == 0
        c, d = far[0][...], far[1][...]
        up_far, down_far = jnp.where(up, c, d), jnp.where(up, d, c)
    pick[2] = mine[near, :]
    pick[3] = jnp.where(at + 1 < count, jnp.where(even, a, b), 0.0)
    pick[1] = jnp.where(at >= 1, jnp.where(even, b, a), 0.0)
    pick[4] = jnp.where(at + 2 < count, up_far, 0.0)
    pick[0] = jnp.where(at >= 2, down_far, 0.0)


def middle_kernel(dims, sizes, far_x, pos, mine, rec_a, rec_b, *refs):
    _, _, _, n_exp = dims
    far = refs[:far_x]
    yfa, yfb, msg_a, msg_b, msg_c, pick = refs[far_x:]
    even = (pos[0] & 1) == 0
    choose_packets(pos[0], sizes[0], mine, rec_a, rec_b, far, pick)
    outs = (msg_a, msg_b, msg_c)
    for ref in outs:
        ref[0:PACK, :] = jnp.zeros((PACK, LANES), F32)
    for hx in range(3):
        for plane in range(2):
            for f in range(3):
                at = plane * PLANE + f * 3
                row = (
                    pick[hx, at + 2:at + 3, :]
                    + pick[hx + 1, at + 1:at + 2, :]
                    + pick[hx + 2, at:at + 1, :]
                )
                for ref in outs:
                    ref[at + hx:at + hx + 1, :] = row
        for ref in outs:
            ref[9 + hx:10 + hx, :] = pick[hx + 1, 9:10, :]
            ref[12 + hx:13 + hx, :] = pick[hx + 1, 10:11, :]
    rows = 3 * n_exp
    src = slice(PACK, PACK + rows)
    stack = (
        jnp.where(even, rec_b[src, :], rec_a[src, :]),
        mine[src, :],
        jnp.where(even, rec_a[src, :], rec_b[src, :]),
    )
    for hx in range(3):
        at = PACK + hx * rows
        msg_a[at:at + rows, :] = stack[hx]
        msg_b[at:at + rows, :] = stack[hx]
    at = PACK + 3 * rows
    msg_a[at:at + yfa.shape[0], :] = yfa[...]
    msg_b[at:at + yfb.shape[0], :] = yfb[...]


def roll_half(x):
    return pltpu.roll(x, LANES // 2, 1)


def low_half(shape):
    return lax.broadcasted_iota(jnp.int32, shape, 1) < LANES // 2


def segment_values(packs, seg_ref):
    tops = [packs[y, 0:PLANE, :] for y in range(5)]
    bottoms = [packs[y, PLANE:PACK, :] for y in range(5)]
    lo = low_half((PLANE, LANES))

    def home(hy):
        return tops[hy + 3] + roll_half(tops[hy + 2]) + bottoms[hy + 1]

    plane0 = jnp.where(lo, home(-1), roll_half(home(0)))
    plane1 = jnp.where(lo, home(1), 0.0)
    for f in range(3):
        seg_ref[f * 8:f * 8 + 3, :] = plane0[f * 3:f * 3 + 3, :]
        seg_ref[f * 8 + 3:f * 8 + 6, :] = plane1[f * 3:f * 3 + 3, :]
        seg_ref[f * 8 + 6:f * 8 + 8, :] = jnp.zeros((2, LANES), F32)


def well_constants(packs, const_ref):
    tops = [packs[y, 0:PLANE, :] for y in (1, 2, 3)]
    rolled = [roll_half(t) for t in tops]
    lo = low_half((PLANE, LANES))
    same0 = jnp.where(lo, tops[0], rolled[1])
    same1 = jnp.where(lo, tops[2], 0.0)
    other0 = jnp.where(lo, rolled[0], tops[1])
    other1 = rolled[2]
    const_ref[...] = jnp.zeros(const_ref.shape, F32)
    for at, (a, b), src in ((0, (same0, same1), 9), (8, (other0, other1), 9), (16, (same0, same1), 12)):
        const_ref[at:at + 3, :] = a[src:src + 3, :]
        const_ref[at + 3:at + 6, :] = b[src:src + 3, :]


def running_sum(x):
    lane = lax.broadcasted_iota(jnp.int32, x.shape, 1) & 15
    for shift in (1, 2, 4, 8):
        x = x + jnp.where(lane >= shift, pltpu.roll(x, shift, 1), 0.0)
    return x


def well_mix(seg_ref):
    field = tuple(seg_ref[f * 8:f * 8 + 8, :] for f in range(3))
    sats, factors = props(field)
    mob = mobilities(sats, factors)
    total = mob[0] + mob[1] + mob[2]
    mix = (mob[0] * DENSITY[0] + mob[1] * DENSITY[1] + mob[2] * DENSITY[2]) / total
    return field, sats, factors, mob, total, mix


def well_rates(seg_ref, const_ref):
    weight, bhp, live = (const_ref[i * 8:i * 8 + 8, :] for i in range(3))
    field, _, _, mob, _, mix = well_mix(seg_ref)
    press = bhp + HEAD_SCALE * running_sum(live * mix)
    return [weight * mob[a] * (field[0] - press) for a in range(3)]


def well_rate_tangents(seg_ref, dseg_ref, const_ref):
    weight, bhp, live = (const_ref[i * 8:i * 8 + 8, :] for i in range(3))
    field, sats, factors, mob, total, mix = well_mix(seg_ref)
    press = bhp + HEAD_SCALE * running_sum(live * mix)
    dfield = tuple(dseg_ref[f * 8:f * 8 + 8, :] for f in range(3))
    _, dmob = tangents(sats, factors, mob, dfield)
    dtotal = dmob[0] + dmob[1] + dmob[2]
    dnum = dmob[0] * DENSITY[0] + dmob[1] * DENSITY[1] + dmob[2] * DENSITY[2]
    dpress = HEAD_SCALE * running_sum(live * ((dnum - mix * dtotal) / total))
    return [
        weight * (dmob[a] * (field[0] - press) + mob[a] * (dfield[0] - dpress)) for a in range(3)
    ]


def stack_received(dims, sizes, pos, mine, rec_a, rec_b, far, packs, partner):
    _, _, _, n_exp = dims
    even = (pos[1] & 1) == 0
    choose_packets(pos[1], sizes[1], mine, rec_a, rec_b, far, packs)
    used = 9 * n_exp
    for f in range(3):
        for hx in range(3):
            at = PACK + hx * 3 * n_exp + f * n_exp
            src = slice(at, at + n_exp)
            first, second = rec_a[src, :], rec_b[src, :]
            blocks = (jnp.where(even, second, first), mine[src, :], jnp.where(even, first, second))
            for hy in range(3):
                to = (hx * 3 + hy) * n_exp
                partner[f, to:to + n_exp, :] = blocks[hy]
        partner[f, used:LANES, :] = jnp.zeros((LANES - used, LANES), F32)


def pick_partners(dims, partner, pidx, table, out):
    _, _, n_fault, _ = dims
    for f in range(3):
        fill_table(table, f, partner[f])

    def put(r, f, value):
        out[f * n_fault + r:f * n_fault + r + 1, :] = value

    gather_loop(table, LANES, pidx, n_fault * LANES, put)


def x_halo(dims, pos, rec_a, rec_b, at, count):
    even = (pos[0] & 1) == 0
    a, b = rec_a[at:at + count, :], rec_b[at:at + count, :]
    return jnp.where(even, b, a), jnp.where(even, a, b)


def y_halo(dims, pos, rec_a, rec_b, at, count):
    even = (pos[1] & 1) == 0
    a, b = rec_a[at:at + count, :], rec_b[at:at + count, :]
    return jnp.where(even, b, a), jnp.where(even, a, b)


def halo_fields(dims, pos, gx_a, gx_b, gy_a, gy_b):
    cx, cy, _, n_exp = dims
    xs = [x_halo(dims, pos, gx_a, gx_b, PACK + 3 * n_exp + f * cy, cy) for f in range(3)]
    ys = [y_halo(dims, pos, gy_a, gy_b, PACK + 9 * n_exp + f * cx, cx) for f in range(3)]
    return (
        [tuple(v[side] for v in xs) for side in range(2)],
        [tuple(v[side] for v in ys) for side in range(2)],
    )


def edge_trans(t_a, t_b):
    return 2.0 * t_a * t_b / (t_a + t_b)


def make_trans(dims, sizes, pos, perm, gx_a, gx_b, gy_a, gy_b, fx, fy, fym, fz):
    cx, cy, _, n_exp = dims
    low_x, high_x = x_halo(dims, pos, gx_a, gx_b, PACK + 3 * n_exp + 3 * cy, cy)
    low_y, high_y = y_halo(dims, pos, gy_a, gy_b, PACK + 9 * n_exp + 3 * cx, cx)
    inside = (pos[0] > 0, pos[0] < sizes[0] - 1, pos[1] > 0, pos[1] < sizes[1] - 1)
    fx[0] = jnp.where(inside[0], edge_trans(low_x, perm[0, 0]), 0.0)
    fx[cx] = jnp.where(inside[1], edge_trans(perm[0, cx - 1], high_x), 0.0)
    fym[...] = jnp.where(inside[2], edge_trans(low_y, perm[1, :, 0, :]), 0.0)
    last_row = lax.broadcasted_iota(jnp.int32, (cy, LANES), 0) == cy - 1
    last_lane = lax.broadcasted_iota(jnp.int32, (cy, LANES), 1) == LANES - 1
    for x in range(cx):
        if x:
            fx[x] = edge_trans(perm[0, x - 1], perm[0, x])
        t = perm[1, x]
        beside = jnp.where(last_row, high_y[x:x + 1, :], pltpu.roll(t, cy - 1, 0))
        value = edge_trans(t, beside)
        fy[x] = jnp.where(jnp.logical_and(last_row, jnp.logical_not(inside[3])), 0.0, value)
        t = perm[2, x]
        fz[x] = jnp.where(last_lane, 0.0, edge_trans(t, pltpu.roll(t, LANES - 1, 1)))


def down_row(flux, first):
    rows = flux.shape[0]
    at = lax.broadcasted_iota(jnp.int32, flux.shape, 0)
    return jnp.where(at == 0, first, pltpu.roll(flux, 1, 0))


def up_row(value, last):
    rows = value.shape[0]
    at = lax.broadcasted_iota(jnp.int32, value.shape, 0)
    return jnp.where(at == rows - 1, last, pltpu.roll(value, rows - 1, 0))


def plane_state(field_ref, x):
    field = tuple(field_ref[f, x] for f in range(3))
    sats, factors = props(field)
    return field, sats, factors, mobilities(sats, factors)


def own_rows(ref, x, row):
    return ref[:, row, :]


def residual_planes(dims, field, pore, old_mass, trans, halos, acc):
    cx, cy, _, _ = dims
    fx, fy, fym, fz = trans
    (low_x, high_x), (low_y, high_y) = halos
    mob_of = lambda fld: mobilities(*props(fld))
    mob_hy = mob_of(high_y)
    first_row = tuple(field[f, :, 0, :] for f in range(3))
    flux_ym = face(fym[...], low_y[0], mob_of(low_y), first_row[0], mob_of(first_row))
    cur = plane_state(field, 0)
    below = face(fx[0], low_x[0], mob_of(low_x), cur[0][0], cur[3])
    for x in range(cx):
        fld, sats, factors, mob = cur
        p = fld[0]
        if x + 1 < cx:
            nxt = plane_state(field, x + 1)
            above = face(fx[x + 1], p, mob, nxt[0][0], nxt[3])
        else:
            nxt = None
            above = face(fx[cx], p, mob, high_x[0], mob_of(high_x))
        y_up = face(
            fy[x], p, mob,
            up_row(p, high_y[0][x:x + 1, :]),
            [up_row(mob[a], mob_hy[a][x:x + 1, :]) for a in range(3)],
        )
        z_up = face(
            fz[x], p, mob,
            pltpu.roll(p, LANES - 1, 1),
            [pltpu.roll(mob[a], LANES - 1, 1) for a in range(3)],
            1.0,
        )
        for a in range(3):
            inflow = (
                (above[a] - below[a])
                + (y_up[a] - down_row(y_up[a], flux_ym[a][x:x + 1, :]))
                + (z_up[a] - pltpu.roll(z_up[a], 1, 1))
            )
            acc[a, x * cy:(x + 1) * cy, :] = pore[x] * (factors[a] * sats[a]) - old_mass[a, x] - inflow
        cur, below = nxt, above


def jacobian_planes(dims, field, dfield, pore, trans, halos, dhalos, acc):
    cx, cy, _, _ = dims
    fx, fy, fym, fz = trans
    (low_x, high_x), (low_y, high_y) = halos
    (dlow_x, dhigh_x), (dlow_y, dhigh_y) = dhalos

    def point(fld, dfld):
        sats, factors = props(fld)
        mob = mobilities(sats, factors)
        dsats, dmob = tangents(sats, factors, mob, dfld)
        return fld[0], mob, dfld[0], dmob, sats, factors, dsats

    def plane(x):
        return point(tuple(field[f, x] for f in range(3)), tuple(dfield[f, x] for f in range(3)))

    def between(t, c, n, depth=0.0):
        return face_tangent(t, c[0], c[1], n[0], n[1], c[2], c[3], n[2], n[3], depth)

    hy = point(high_y, dhigh_y)
    row0 = point(
        tuple(field[f, :, 0, :] for f in range(3)), tuple(dfield[f, :, 0, :] for f in range(3))
    )
    flux_ym = between(fym[...], point(low_y, dlow_y), row0)
    cur = plane(0)
    below = between(fx[0], point(low_x, dlow_x), cur)
    for x in range(cx):
        nxt = plane(x + 1) if x + 1 < cx else point(high_x, dhigh_x)
        above = between(fx[x + 1], cur, nxt)
        row = slice(x, x + 1)
        beside = (
            up_row(cur[0], hy[0][row, :]),
            [up_row(cur[1][a], hy[1][a][row, :]) for a in range(3)],
            up_row(cur[2], hy[2][row, :]),
            [up_row(cur[3][a], hy[3][a][row, :]) for a in range(3)],
        )
        y_up = between(fy[x], cur, beside)
        shift = lambda v: pltpu.roll(v, LANES - 1, 1)
        over = (
            shift(cur[0]),
            [shift(cur[1][a]) for a in range(3)],
            shift(cur[2]),
            [shift(cur[3][a]) for a in range(3)],
        )
        z_up = between(fz[x], cur, over, 1.0)
        _, _, dp, _, sats, factors, dsats = cur
        for a in range(3):
            inflow = (
                (above[a] - below[a])
                + (y_up[a] - down_row(y_up[a], flux_ym[a][row, :]))
                + (z_up[a] - pltpu.roll(z_up[a], 1, 1))
            )
            gain = pore[x] * (factors[a] * (dsats[a] + COMPRESS[a] * sats[a] * dp))
            acc[a, x * cy:(x + 1) * cy, :] = gain - inflow
        cur, below = nxt, above


def rows_of(ref, count):
    return tuple(ref[f * count:(f + 1) * count, :] for f in range(3))


def connection_trans(ftrans, tr, n_fault):
    for r in range(n_fault):
        tr[r:r + 1, :] = ftrans[:, r * LANES:(r + 1) * LANES]


def residual_kernel(dims, sizes, make, final, far_y, pos, *refs):
    cx, cy, n_fault, n_exp = dims
    rows = cx * cy
    refs = list(refs)
    take = lambda n: [refs.pop(0) for _ in range(n)]
    field, pore, old_mass, scaling, idx, pidx, ftrans, static, own = take(9)
    gx_a, gx_b, mine, gy_a, gy_b = take(5)
    far = take(far_y)
    if make:
        (perm,) = take(1)
    else:
        trans = take(4)
    direction, partner_vals, seg, const = take(4)
    outs = take(6)
    if make:
        trans = take(4)
    if final:
        residual, well = take(2)
    acc, packs, partner, values, tr, table, ptable = take(7)

    if make:
        make_trans(dims, sizes, pos, perm, gx_a, gx_b, gy_a, gy_b, *trans)
    stack_received(dims, sizes, pos, mine, gy_a, gy_b, far, packs, partner)
    pick_partners(dims, partner, pidx, ptable, partner_vals)
    connection_trans(ftrans, tr, n_fault)
    mine_f, other_f = rows_of(own, n_fault), rows_of(partner_vals, n_fault)
    mob_of = lambda fld: mobilities(*props(fld))
    flux = face(tr[...], mine_f[0], mob_of(mine_f), other_f[0], mob_of(other_f))
    segment_values(packs, seg)
    well_constants(packs, const)
    rates = well_rates(seg, const)
    for a in range(3):
        values[a, 0:n_fault, :] = -flux[a]
        values[a, n_fault:n_fault + 8, :] = rates[a]
    if final:
        done = running_sum(rates[0] + rates[1] + rates[2])[1:2, :]
        well[...] = done / packs[2, 13:14, :] - 1.0
    halos = halo_fields(dims, pos, gx_a, gx_b, gy_a, gy_b)
    residual_planes(dims, field, pore, old_mass, trans, halos, acc)
    total = scatter_loop(values, idx, (n_fault + 6) * LANES, rows)
    for a in range(3):
        res = (acc[a] + total[:, a * LANES:(a + 1) * LANES]).reshape(cx, cy, LANES)
        if final:
            residual[a] = res
        direction[a] = scaling[a] * res
    emit(dims, pos, direction, idx, static, table, outs)


def jacobian_kernel(dims, sizes, final, far_y, pos, *refs):
    cx, cy, n_fault, n_exp = dims
    rows = cx * cy
    refs = list(refs)
    take = lambda n: [refs.pop(0) for _ in range(n)]
    field, direction, pore, scaling, idx, pidx, ftrans, static = take(8)
    own, other, seg, const, down = take(5)
    trans = take(4)
    gx_a, gx_b, gy_a, gy_b = take(4)
    dgx_a, dgx_b, mine, dgy_a, dgy_b = take(5)
    far = take(far_y)
    (result,) = take(1)
    outs = None if final else take(6)
    acc, packs, partner, values, tr, ptable, dother, dseg = take(8)
    table = None if final else take(1)[0]

    stack_received(dims, sizes, pos, mine, dgy_a, dgy_b, far, packs, partner)
    pick_partners(dims, partner, pidx, ptable, dother)
    connection_trans(ftrans, tr, n_fault)

    def point(fld, dfld):
        sats, factors = props(fld)
        mob = mobilities(sats, factors)
        return fld[0], mob, dfld[0], tangents(sats, factors, mob, dfld)[1]

    c = point(rows_of(own, n_fault), rows_of(down, n_fault))
    n = point(rows_of(other, n_fault), rows_of(dother, n_fault))
    flux = face_tangent(tr[...], c[0], c[1], n[0], n[1], c[2], c[3], n[2], n[3])
    segment_values(packs, dseg)
    rates = well_rate_tangents(seg, dseg, const)
    for a in range(3):
        values[a, 0:n_fault, :] = -flux[a]
        values[a, n_fault:n_fault + 8, :] = rates[a]
    halos = halo_fields(dims, pos, gx_a, gx_b, gy_a, gy_b)
    dhalos = halo_fields(dims, pos, dgx_a, dgx_b, dgy_a, dgy_b)
    jacobian_planes(dims, field, direction, pore, trans, halos, dhalos, acc)
    total = scatter_loop(values, idx, (n_fault + 6) * LANES, rows)
    for a in range(3):
        jac = (acc[a] + total[:, a * LANES:(a + 1) * LANES]).reshape(cx, cy, LANES)
        step = 2.0 * direction[a] - scaling[a] * jac
        result[a] = step if final else field[a] - step
    if not final:
        emit(dims, pos, result, idx, static, table, outs)


def exchange_pairs(axis, kind, size_x, size_y):
    def partner(i, count):
        step = 1 if kind < 2 else 2
        shift = step if kind % 2 else 0
        if shift and not shift <= i < count - shift:
            return None
        return ((i + shift) ^ step) - shift

    out = []
    for i in range(size_x):
        for j in range(size_y):
            if axis == 0:
                got = partner(i, size_x)
                far = (got, j) if got is not None else ((i, j ^ 1) if kind < 2 else (i ^ 1, j))
            else:
                got = partner(j, size_y)
                far = (i, got) if got is not None else ((i ^ 1, j) if kind < 2 else (i, j ^ 1))
            out.append((i * size_y + j, far[0] * size_y + far[1]))
    return out


def body(
    state, perm, pore, old_mass, scaling, fault_cell, fault_tile, fault_row, fault_trans,
    fault_export, perf_cell, well_segments, well_index, bhp, target,
):
    size_x, size_y = lax.axis_size("gx"), lax.axis_size("gy")
    _, cx, cy, _ = state.shape
    wells, segs = well_index.shape[2:]
    n_fault, n_exp = fault_cell.shape[-1] // LANES, fault_export.shape[-1] // LANES
    dims = (cx, cy, n_fault, n_exp)
    far_x = 1 if size_x == 4 else 2
    far_y = 1 if size_y == 4 else 2
    at_x, at_y = lax.axis_index("gx"), lax.axis_index("gy")
    pos = jnp.stack([at_x, at_y]).astype(jnp.int32)

    slots = perf_cell.reshape(3, 3, wells * segs)
    empty = jnp.full((3, wells * segs), -1, jnp.int32)
    planes = jnp.stack([slots[:, 0], slots[:, 1], slots[:, 2], empty], axis=1).reshape(3, 2, LANES)
    idx = jnp.concatenate(
        [fault_cell.reshape(1, -1), planes.transpose(1, 0, 2).reshape(1, -1), fault_export.reshape(1, -1)],
        axis=1,
    )
    tile = fault_tile.reshape(1, -1)
    across = tile // size_y - at_x + 1
    along = tile % size_y - at_y + 1
    pidx = (across * 3 + along) * (n_exp * LANES) + fault_row.reshape(1, -1)
    ftrans = fault_trans.reshape(1, -1)
    live = (
        lax.broadcasted_iota(jnp.int32, (wells, segs), 1) < well_segments.reshape(wells, 1)
    ).astype(F32)
    wide = lambda v: jnp.broadcast_to(v.reshape(wells, 1), (wells, segs)).reshape(-1)
    static = jnp.concatenate(
        [
            (live * well_index.reshape(wells, segs)).reshape(-1), wide(bhp),
            live.reshape(-1), wide(target),
            jnp.zeros((6 * LANES,), F32),
        ]
    ).reshape(8, LANES)

    params = pltpu.CompilerParams(vmem_limit_bytes=VMEM_BYTES)
    smem = pl.BlockSpec(memory_space=pltpu.SMEM)
    vmem = pl.BlockSpec(memory_space=pltpu.VMEM)
    shape = lambda *dims_: jax.ShapeDtypeStruct(dims_, F32)
    rows = cx * cy
    gx_rows = PACK + 3 * n_exp + 3 * cy
    gy_rows = PACK + 9 * n_exp + 3 * cx
    table = pltpu.VMEM((3 * LANES, 2 * rows), BF16)

    def call(kernel, args, outs, scratch):
        return pl.pallas_call(
            kernel,
            out_shape=outs,
            in_specs=[smem] + [vmem] * (len(args) - 1),
            out_specs=[vmem] * len(outs),
            scratch_shapes=scratch,
            compiler_params=params,
        )(*args)

    def message_shapes(first):
        more_x, more_y = (cy, cx) if first else (0, 0)
        return [
            shape(gx_rows + more_x, LANES), shape(gx_rows + more_x, LANES), shape(PACK, LANES),
            shape(3 * cx + more_y, LANES), shape(3 * cx + more_y, LANES), shape(3 * n_fault, LANES),
        ]

    def send(value, axis, kind):
        return lax.ppermute(value, ("gx", "gy"), exchange_pairs(axis, kind, size_x, size_y))

    def exchange(messages):
        msg_a, msg_b, packet, yfa, yfb, own = messages
        far = [send(packet, 0, 2 + k) for k in range(far_x)]
        rec_b = send(msg_b, 0, 1)
        rec_a = send(msg_a, 0, 0)
        total = PACK + 9 * n_exp + yfa.shape[0]
        mid_a, mid_b, mid_c = call(
            functools.partial(middle_kernel, dims, (size_x, size_y), far_x),
            [pos, msg_a, rec_a, rec_b, *far, yfa, yfb],
            [shape(total, LANES), shape(total, LANES), shape(PACK, LANES)],
            [pltpu.VMEM((5, PACK, LANES), F32)],
        )
        got_far = [send(mid_c, 1, 2 + k) for k in reversed(range(far_y))][::-1]
        got_b = send(mid_b, 1, 1)
        got_a = send(mid_a, 1, 0)
        return (rec_a, rec_b), (mid_a, got_a, got_b, *got_far)

    work = [
        pltpu.VMEM((3, rows, LANES), F32), pltpu.VMEM((5, PACK, LANES), F32),
        pltpu.VMEM((3, LANES, LANES), F32), pltpu.VMEM((3, n_fault + 8, LANES), F32),
        pltpu.VMEM((n_fault, LANES), F32),
    ]
    ptable = pltpu.VMEM((3 * LANES, 2 * LANES), BF16)
    grid = shape(3, cx, cy, LANES)
    wide_rows = shape(3 * n_fault, LANES)
    small = shape(24, LANES)

    messages = call(
        functools.partial(first_kernel, dims), [pos, state, perm, idx, static],
        message_shapes(True), [table],
    )
    current = state
    trans = None
    for step in range(2):
        final = step == 1
        own = messages[5]
        gx_got, gy_got = exchange(messages)
        results = call(
            functools.partial(residual_kernel, dims, (size_x, size_y), not final, final, far_y),
            [pos, current, pore, old_mass, scaling, idx, pidx, ftrans, static, own, *gx_got, *gy_got]
            + ([*trans] if final else [perm]),
            [grid, wide_rows, small, small] + message_shapes(False)
            + ([grid, shape(1, LANES)] if final else
               [shape(cx + 1, cy, LANES), shape(cx, cy, LANES), shape(cx, LANES), shape(cx, cy, LANES)]),
            work + [table, ptable],
        )
        direction, other, seg, const = results[:4]
        messages = results[4:10]
        if final:
            residual, well = results[10:]
        else:
            trans = results[10:]
        down = messages[5]
        dgx_got, dgy_got = exchange(messages)
        results = call(
            functools.partial(jacobian_kernel, dims, (size_x, size_y), final, far_y),
            [pos, current, direction, pore, scaling, idx, pidx, ftrans, static, own, other, seg, const, down,
             *trans, *gx_got, gy_got[1], gy_got[2], *dgx_got, *dgy_got],
            [grid] + ([] if final else message_shapes(False)),
            work + [ptable, pltpu.VMEM((3 * n_fault, LANES), F32), pltpu.VMEM((24, LANES), F32)]
            + ([] if final else [table]),
        )
        current, messages = results[0], results[1:]
    half = LANES // 2
    well_res = well[0, half:].reshape(wells, segs)[:, segs - 1]
    return residual, current, well_res.reshape(1, 1, wells)


def solution(mesh):
    grid = P(None, "gx", "gy", None)
    tile = P("gx", "gy", None)
    return jax.shard_map(
        body,
        mesh=mesh,
        in_specs=(
            grid, grid, tile, grid, grid, tile, tile, tile, tile, tile,
            P("gx", "gy", None, None, None, None), tile, P("gx", "gy", None, None), tile, tile,
        ),
        out_specs=(grid, grid, tile),
        check_vma=False,
    )
```

```python
import functools

import jax
import jax.numpy as jnp
from jax import lax
from jax.experimental import pallas as pl
from jax.experimental.pallas import tpu as pltpu
from jax.sharding import PartitionSpec as P

VISCOSITY = (0.5, 2.0, 0.1)
COMPRESS = (0.02, 0.05, 0.3)
DENSITY = (1.0, 0.8, 0.2)
GRAVITY = 0.2
INV_SMOOTHING = 10.0
HEAD_SCALE = 0.3

LANES = 128
PACK = 32
PLANE = 16
VMEM_BYTES = 40 * 1024 * 1024
F32 = jnp.float32
BF16 = jnp.bfloat16


def props(field):
    p, sw, sg = field
    sats = (sw, 1.0 - sw - sg, sg)
    factors = tuple(jnp.exp(COMPRESS[a] * p) for a in range(3))
    return sats, factors


def mobilities(sats, factors):
    return tuple(sats[a] * sats[a] * factors[a] * (1.0 / VISCOSITY[a]) for a in range(3))


def tangents(sats, factors, mob, dfield):
    dp, dsw, dsg = dfield
    dsats = (dsw, -(dsw + dsg), dsg)
    dmob = tuple(
        mob[a] * (COMPRESS[a] * dp) + sats[a] * factors[a] * (2.0 / VISCOSITY[a]) * dsats[a]
        for a in range(3)
    )
    return dsats, dmob


def face(trans, p_c, mob_c, p_n, mob_n, depth=0.0):
    out = []
    diff = p_n - p_c
    for a in range(3):
        if a == 0 or depth:
            pot = diff - GRAVITY * DENSITY[a] * depth if depth else diff
            weight = jax.nn.sigmoid(pot * INV_SMOOTHING)
            scaled = trans * pot
        out.append(scaled * (mob_c[a] + weight * (mob_n[a] - mob_c[a])))
    return out


def face_tangent(trans, p_c, mob_c, p_n, mob_n, dp_c, dmob_c, dp_n, dmob_n, depth=0.0):
    out = []
    diff = p_n - p_c
    ddiff = dp_n - dp_c
    for a in range(3):
        if a == 0 or depth:
            pot = diff - GRAVITY * DENSITY[a] * depth if depth else diff
            weight = jax.nn.sigmoid(pot * INV_SMOOTHING)
            dweight = (weight * (1.0 - weight)) * (ddiff * INV_SMOOTHING)
        step = mob_n[a] - mob_c[a]
        mean = mob_c[a] + weight * step
        dmean = dmob_c[a] + weight * (dmob_n[a] - dmob_c[a]) + dweight * step
        out.append(trans * (mean * ddiff + pot * dmean))
    return out


def split2(x):
    high = x.astype(BF16)
    return high, (x - high.astype(F32)).astype(BF16)


def one_hot_rows(idx, count):
    rows = (idx >> 7).astype(F32).astype(BF16)
    at = lax.broadcasted_iota(jnp.int32, (count, idx.shape[1]), 0).astype(F32).astype(BF16)
    return jnp.where(at == rows, jnp.ones((), BF16), jnp.zeros((), BF16))


def even_at(axis):
    return (lax.axis_index(axis) & 1) == 0


def gather_loop(table_ref, count, idx_ref, start, columns, put):
    for c in range(start, columns, 256):
        width = min(256, columns - c)
        idx = idx_ref[:, c:c + width]
        hot = one_hot_rows(idx, count)
        picked = jnp.dot(
            table_ref[...], jnp.concatenate([hot, hot], axis=0), preferred_element_type=F32
        )
        lane = idx & (LANES - 1)
        for h in range(width // LANES):
            cols = slice(h * LANES, (h + 1) * LANES)
            mask = lax.broadcasted_iota(jnp.int32, (LANES, LANES), 0) == lane[:, cols]
            for f in range(3):
                block = picked[f * LANES:(f + 1) * LANES, cols]
                value = jnp.sum(jnp.where(mask, block, 0.0), axis=0, keepdims=True)
                put(c // LANES + h, f, value)


def scatter_loop(values_ref, idx_ref, start, columns, count):
    total = jnp.zeros((count, 3 * LANES), F32)
    for c in range(start, columns, 256):
        width = min(256, columns - c)
        idx = idx_ref[:, c:c + width]
        hot = one_hot_rows(idx, count)
        lane = (idx & (LANES - 1)).astype(F32).astype(BF16)
        at = lax.broadcasted_iota(jnp.int32, (LANES, width), 0).astype(F32).astype(BF16)
        mask = at == lane
        highs, lows = [], []
        for f in range(3):
            r = (c - start) // LANES
            row = jnp.concatenate(
                [values_ref[f, r + h:r + h + 1, :] for h in range(width // LANES)], axis=1
            )
            high, low = split2(row)
            highs.append(jnp.where(mask, high, jnp.zeros((), BF16)))
            lows.append(jnp.where(mask, low, jnp.zeros((), BF16)))
        right = jnp.concatenate(
            [jnp.concatenate(highs, axis=0), jnp.concatenate(lows, axis=0)], axis=1
        )
        left = jnp.concatenate([hot, hot], axis=1)
        total = total + lax.dot_general(
            left, right, (((1,), (1,)), ((), ())), preferred_element_type=F32
        )
    return total


def fill_table(table_ref, f, cells):
    rows = cells.shape[0]
    high, low = split2(cells.T)
    table_ref[f * LANES:(f + 1) * LANES, 0:rows] = high
    table_ref[f * LANES:(f + 1) * LANES, rows:2 * rows] = low


def emit(dims, field_ref, idx_ref, static_ref, outs, perm_ref=None):
    gxa, gxb, gxp, yfa, yfb, table_ref = outs
    cx, cy, n_fault, n_exp = dims
    rows = cx * cy
    zeros = jnp.zeros((PACK, LANES), F32)
    for ref in (gxa, gxb, gxp):
        ref[0:PACK, :] = zeros
        ref[9:11, :] = static_ref[0:2, :]
    even_x, even_y = even_at("gx"), even_at("gy")
    base = PACK + 3 * n_exp

    def put_faces(out_a, out_b, at, low, high, even):
        count = low.shape[0]
        out_a[at:at + count, :] = jnp.where(even, high, low)
        out_b[at:at + count, :] = jnp.where(even, low, high)

    for f in range(3):
        put_faces(gxa, gxb, base + f * cy, field_ref[f, 0], field_ref[f, cx - 1], even_x)
        put_faces(yfa, yfb, f * cx, field_ref[f, :, 0, :], field_ref[f, :, cy - 1, :], even_y)
        fill_table(table_ref, f, field_ref[f].reshape(rows, LANES))
    if perm_ref is not None:
        put_faces(gxa, gxb, base + 3 * cy, perm_ref[0, 0], perm_ref[0, cx - 1], even_x)
        put_faces(yfa, yfb, 3 * cx, perm_ref[1, :, 0, :], perm_ref[1, :, cy - 1, :], even_y)

    def put(r, f, value):
        if r < n_fault + 6:
            plane, e = divmod(r - n_fault, 3)
            at = plane * PLANE + f * 3 + e
            for ref in (gxa, gxb, gxp):
                ref[at:at + 1, :] = value
        else:
            at = PACK + f * n_exp + r - n_fault - 6
            for ref in (gxa, gxb):
                ref[at:at + 1, :] = value

    gather_loop(table_ref, rows, idx_ref, n_fault * LANES, (n_fault + 6 + n_exp) * LANES, put)


def flat_row(v, buf):
    buf[...] = jnp.zeros(buf.shape, F32)
    buf[0:v.shape[0], 0:v.shape[1]] = v
    moved = pltpu.roll(buf[...], 0, 1, stride=v.shape[1], stride_axis=0)
    return jnp.sum(moved, axis=0, keepdims=True)


def first_kernel(dims, *refs):
    sources, outs, (idx, static) = refs[:9], refs[9:15], refs[15:17]
    targets, (buf, sems) = refs[17:26], refs[26:]
    loads = [
        pltpu.make_async_copy(src, dst, sems.at[i]) for i, (src, dst) in enumerate(zip(sources, targets))
    ]
    for load in loads:
        load.start()
    state, perm, cells, exports, perf, windex, wseg, bhp, target = targets
    for load in loads[2:]:
        load.wait()
    cx, cy, n_fault, n_exp = dims
    count = n_fault * LANES
    idx[:, 0:count] = cells[0]
    idx[:, count + 6 * LANES:] = exports[0]
    for e in range(3):
        flat = [flat_row(perf[0, 0, e, k].astype(F32) + 1.0, buf) for k in range(3)]
        rows = (flat[0] + roll_half(flat[1]), flat[2])
        for plane in range(2):
            at = count + (plane * 3 + e) * LANES
            idx[:, at:at + LANES] = (rows[plane] - 1.0).astype(jnp.int32)
    shape = windex.shape[2:]
    well = lax.broadcasted_iota(jnp.int32, shape, 0)

    def spread(ref):
        value = jnp.full(shape, ref[0, 0, 0])
        for w in range(1, shape[0]):
            value = jnp.where(well == w, ref[0, 0, w], value)
        return value

    live = (lax.broadcasted_iota(jnp.int32, shape, 1) < spread(wseg)).astype(F32)
    static[...] = jnp.zeros(static.shape, F32)
    static[0:1, :] = flat_row(live * windex[0, 0], buf) + roll_half(flat_row(spread(bhp), buf))
    static[1:2, :] = flat_row(live, buf) + roll_half(flat_row(spread(target), buf))
    for load in loads[:2]:
        load.wait()
    emit(dims, state, idx, static, outs, perm)


def connection_kernel(dims, size_y, tiles, rows, trans, pidx, tr):
    _, _, n_fault, n_exp = dims
    tile = tiles[...]
    tile_x = jnp.floor((tile.astype(F32) + 0.5) * (1.0 / size_y)).astype(jnp.int32)
    tile_y = tile - tile_x * size_y
    across = tile_x - lax.axis_index("gx") + 1
    along = tile_y - lax.axis_index("gy") + 1
    pidx[...] = (across * 3 + along) * (n_exp * LANES) + rows[...]
    for r in range(n_fault):
        tr[r:r + 1, :] = trans[:, r * LANES:(r + 1) * LANES]


def gather_kernel(dims, table, idx, own):
    cx, cy, n_fault, _ = dims

    def put(r, f, value):
        own[f * n_fault + r:f * n_fault + r + 1, :] = value

    gather_loop(table, cx * cy, idx, 0, n_fault * LANES, put)


def choose_packets(axis, count, mine, rec_a, rec_b, far, pick):
    at = lax.axis_index(axis)
    even = even_at(axis)
    near = slice(0, PACK)
    a, b = rec_a[near, :], rec_b[near, :]
    if len(far) == 1:
        up_far = down_far = far[0][...]
    else:
        up = ((at >> 1) & 1) == 0
        c, d = far[0][...], far[1][...]
        up_far, down_far = jnp.where(up, c, d), jnp.where(up, d, c)
    pick[2] = mine[near, :]
    pick[3] = jnp.where(at + 1 < count, jnp.where(even, a, b), 0.0)
    pick[1] = jnp.where(at >= 1, jnp.where(even, b, a), 0.0)
    pick[4] = jnp.where(at + 2 < count, up_far, 0.0)
    pick[0] = jnp.where(at >= 2, down_far, 0.0)


def middle_kernel(dims, sizes, far_x, _, __, mine, rec_a, rec_b, *refs):
    _, _, _, n_exp = dims
    far = refs[:far_x]
    yfa, yfb, msg_a, msg_b, msg_c, pick = refs[far_x:]
    even = even_at("gx")
    choose_packets("gx", sizes[0], mine, rec_a, rec_b, far, pick)
    outs = (msg_a, msg_b, msg_c)
    for ref in outs:
        ref[0:PACK, :] = jnp.zeros((PACK, LANES), F32)
    for hx in range(3):
        for plane in range(2):
            for f in range(3):
                at = plane * PLANE + f * 3
                row = (
                    pick[hx, at + 2:at + 3, :]
                    + pick[hx + 1, at + 1:at + 2, :]
                    + pick[hx + 2, at:at + 1, :]
                )
                for ref in outs:
                    ref[at + hx:at + hx + 1, :] = row
        for ref in outs:
            ref[9 + hx:10 + hx, :] = pick[hx + 1, 9:10, :]
            ref[12 + hx:13 + hx, :] = pick[hx + 1, 10:11, :]
    rows = 3 * n_exp
    src = slice(PACK, PACK + rows)
    stack = (
        jnp.where(even, rec_b[src, :], rec_a[src, :]),
        mine[src, :],
        jnp.where(even, rec_a[src, :], rec_b[src, :]),
    )
    for hx in range(3):
        at = PACK + hx * rows
        msg_a[at:at + rows, :] = stack[hx]
        msg_b[at:at + rows, :] = stack[hx]
    at = PACK + 3 * rows
    msg_a[at:at + yfa.shape[0], :] = yfa[...]
    msg_b[at:at + yfb.shape[0], :] = yfb[...]


def roll_half(x):
    return pltpu.roll(x, LANES // 2, 1)


def low_half(shape):
    return lax.broadcasted_iota(jnp.int32, shape, 1) < LANES // 2


def segment_values(packs, seg_ref):
    tops = [packs[y, 0:PLANE, :] for y in range(5)]
    bottoms = [packs[y, PLANE:PACK, :] for y in range(5)]
    lo = low_half((PLANE, LANES))

    def home(hy):
        return tops[hy + 3] + roll_half(tops[hy + 2]) + bottoms[hy + 1]

    plane0 = jnp.where(lo, home(-1), roll_half(home(0)))
    plane1 = jnp.where(lo, home(1), 0.0)
    for f in range(3):
        seg_ref[f * 8:f * 8 + 3, :] = plane0[f * 3:f * 3 + 3, :]
        seg_ref[f * 8 + 3:f * 8 + 6, :] = plane1[f * 3:f * 3 + 3, :]
        seg_ref[f * 8 + 6:f * 8 + 8, :] = jnp.zeros((2, LANES), F32)


def well_constants(packs, const_ref):
    tops = [packs[y, 0:PLANE, :] for y in (1, 2, 3)]
    rolled = [roll_half(t) for t in tops]
    lo = low_half((PLANE, LANES))
    same0 = jnp.where(lo, tops[0], rolled[1])
    same1 = jnp.where(lo, tops[2], 0.0)
    other0 = jnp.where(lo, rolled[0], tops[1])
    other1 = rolled[2]
    const_ref[...] = jnp.zeros(const_ref.shape, F32)
    for at, (a, b), src in ((0, (same0, same1), 9), (8, (other0, other1), 9), (16, (same0, same1), 12)):
        const_ref[at:at + 3, :] = a[src:src + 3, :]
        const_ref[at + 3:at + 6, :] = b[src:src + 3, :]


def running_sum(x):
    lane = lax.broadcasted_iota(jnp.int32, x.shape, 1) & 15
    for shift in (1, 2, 4, 8):
        x = x + jnp.where(lane >= shift, pltpu.roll(x, shift, 1), 0.0)
    return x


def well_mix(seg_ref):
    field = tuple(seg_ref[f * 8:f * 8 + 8, :] for f in range(3))
    sats, factors = props(field)
    mob = mobilities(sats, factors)
    total = mob[0] + mob[1] + mob[2]
    mix = (mob[0] * DENSITY[0] + mob[1] * DENSITY[1] + mob[2] * DENSITY[2]) / total
    return field, sats, factors, mob, total, mix


def well_rates(seg_ref, const_ref):
    weight, bhp, live = (const_ref[i * 8:i * 8 + 8, :] for i in range(3))
    field, _, _, mob, _, mix = well_mix(seg_ref)
    press = bhp + HEAD_SCALE * running_sum(live * mix)
    return [weight * mob[a] * (field[0] - press) for a in range(3)]


def well_rate_tangents(seg_ref, dseg_ref, const_ref):
    weight, bhp, live = (const_ref[i * 8:i * 8 + 8, :] for i in range(3))
    field, sats, factors, mob, total, mix = well_mix(seg_ref)
    press = bhp + HEAD_SCALE * running_sum(live * mix)
    dfield = tuple(dseg_ref[f * 8:f * 8 + 8, :] for f in range(3))
    _, dmob = tangents(sats, factors, mob, dfield)
    dtotal = dmob[0] + dmob[1] + dmob[2]
    dnum = dmob[0] * DENSITY[0] + dmob[1] * DENSITY[1] + dmob[2] * DENSITY[2]
    dpress = HEAD_SCALE * running_sum(live * ((dnum - mix * dtotal) / total))
    return [
        weight * (dmob[a] * (field[0] - press) + mob[a] * (dfield[0] - dpress)) for a in range(3)
    ]


def stack_partners(dims, mine, rec_a, rec_b, partner):
    _, _, _, n_exp = dims
    even = even_at("gy")
    used = 9 * n_exp
    for f in range(3):
        for hx in range(3):
            at = PACK + hx * 3 * n_exp + f * n_exp
            src = slice(at, at + n_exp)
            first, second = rec_a[src, :], rec_b[src, :]
            blocks = (jnp.where(even, second, first), mine[src, :], jnp.where(even, first, second))
            for hy in range(3):
                to = (hx * 3 + hy) * n_exp
                partner[f, to:to + n_exp, :] = blocks[hy]
        partner[f, used:LANES, :] = jnp.zeros((LANES - used, LANES), F32)


def pick_partners(dims, partner, pidx, table, out):
    _, _, n_fault, _ = dims
    for f in range(3):
        fill_table(table, f, partner[f])

    def put(r, f, value):
        out[f * n_fault + r:f * n_fault + r + 1, :] = value

    gather_loop(table, LANES, pidx, 0, n_fault * LANES, put)


def halo(axis, rec_a, rec_b, at, count):
    even = even_at(axis)
    a, b = rec_a[at:at + count, :], rec_b[at:at + count, :]
    return jnp.where(even, b, a), jnp.where(even, a, b)


def halo_fields(dims, gx_a, gx_b, gy_a, gy_b):
    cx, cy, _, n_exp = dims
    xs = [halo("gx", gx_a, gx_b, PACK + 3 * n_exp + f * cy, cy) for f in range(3)]
    ys = [halo("gy", gy_a, gy_b, PACK + 9 * n_exp + f * cx, cx) for f in range(3)]
    return [tuple(v[side] for v in both) for both in (xs, ys) for side in range(2)]


def outermost(dims, ref):
    cx, cy, _, _ = dims
    return [
        tuple(ref[f, 0] for f in range(3)), tuple(ref[f, cx - 1] for f in range(3)),
        tuple(ref[f, :, 0, :] for f in range(3)), tuple(ref[f, :, cy - 1, :] for f in range(3)),
    ]


def edge_trans(t_a, t_b):
    return 2.0 * t_a * t_b / (t_a + t_b)


def inner_trans(dims, perm, fx, fy, fz, edge_x, edge_y):
    cx, cy, _, _ = dims
    last_row = lax.broadcasted_iota(jnp.int32, (cy, LANES), 0) == cy - 1
    last_lane = lax.broadcasted_iota(jnp.int32, (cy, LANES), 1) == LANES - 1
    for x in range(cx):
        if x + 1 < cx:
            fx[x] = edge_trans(perm[0, x], perm[0, x + 1])
        t = perm[1, x]
        fy[x] = jnp.where(last_row, 0.0, edge_trans(t, pltpu.roll(t, cy - 1, 0)))
        t = perm[2, x]
        fz[x] = jnp.where(last_lane, 0.0, edge_trans(t, pltpu.roll(t, LANES - 1, 1)))
    edge_x[0], edge_x[1] = perm[0, 0], perm[0, cx - 1]
    edge_y[0], edge_y[1] = perm[1, :, 0, :], perm[1, :, cy - 1, :]


def outer_trans(dims, sizes, edge_x, edge_y, gx_a, gx_b, gy_a, gy_b, out_x, out_y):
    cx, cy, _, n_exp = dims
    at_x, at_y = lax.axis_index("gx"), lax.axis_index("gy")
    low_x, high_x = halo("gx", gx_a, gx_b, PACK + 3 * n_exp + 3 * cy, cy)
    low_y, high_y = halo("gy", gy_a, gy_b, PACK + 9 * n_exp + 3 * cx, cx)
    out_x[0] = jnp.where(at_x > 0, edge_trans(low_x, edge_x[0]), 0.0)
    out_x[1] = jnp.where(at_x < sizes[0] - 1, edge_trans(edge_x[1], high_x), 0.0)
    out_y[0] = jnp.where(at_y > 0, edge_trans(low_y, edge_y[0]), 0.0)
    out_y[1] = jnp.where(at_y < sizes[1] - 1, edge_trans(edge_y[1], high_y), 0.0)


def mob_of(field):
    return mobilities(*props(field))


def residual_planes(dims, field, pore, old_mass, fx, fy, fz, acc):
    cx, cy, _, _ = dims

    def plane(x):
        fld = tuple(field[f, x] for f in range(3))
        sats, factors = props(fld)
        return fld[0], mobilities(sats, factors), sats, factors

    cur, below = plane(0), None
    for x in range(cx):
        p, mob, sats, factors = cur
        row = lambda v: pltpu.roll(v, cy - 1, 0)
        lane = lambda v: pltpu.roll(v, LANES - 1, 1)
        y_up = face(fy[x], p, mob, row(p), [row(m) for m in mob])
        z_up = face(fz[x], p, mob, lane(p), [lane(m) for m in mob], 1.0)
        nxt = above = None
        if x + 1 < cx:
            nxt = plane(x + 1)
            above = face(fx[x], p, mob, nxt[0], nxt[1])
        for a in range(3):
            inflow = (y_up[a] - pltpu.roll(y_up[a], 1, 0)) + (z_up[a] - pltpu.roll(z_up[a], 1, 1))
            if above is not None:
                inflow = inflow + above[a]
            if below is not None:
                inflow = inflow - below[a]
            acc[a, x] = pore[x] * (factors[a] * sats[a]) - old_mass[a, x] - inflow
        cur, below = nxt, above


def point(field, dfield):
    sats, factors = props(field)
    mob = mobilities(sats, factors)
    dsats, dmob = tangents(sats, factors, mob, dfield)
    return field[0], mob, dfield[0], dmob, sats, factors, dsats


def between(trans, c, n, depth=0.0):
    return face_tangent(trans, c[0], c[1], n[0], n[1], c[2], c[3], n[2], n[3], depth)


def jacobian_planes(dims, field, dfield, pore, fx, fy, fz, acc):
    cx, cy, _, _ = dims

    def plane(x):
        return point(tuple(field[f, x] for f in range(3)), tuple(dfield[f, x] for f in range(3)))

    def moved(c, shift):
        return shift(c[0]), [shift(m) for m in c[1]], shift(c[2]), [shift(m) for m in c[3]]

    cur, below = plane(0), None
    for x in range(cx):
        y_up = between(fy[x], cur, moved(cur, lambda v: pltpu.roll(v, cy - 1, 0)))
        z_up = between(fz[x], cur, moved(cur, lambda v: pltpu.roll(v, LANES - 1, 1)), 1.0)
        nxt = above = None
        if x + 1 < cx:
            nxt = plane(x + 1)
            above = between(fx[x], cur, nxt)
        _, _, dp, _, sats, factors, dsats = cur
        for a in range(3):
            inflow = (y_up[a] - pltpu.roll(y_up[a], 1, 0)) + (z_up[a] - pltpu.roll(z_up[a], 1, 1))
            if above is not None:
                inflow = inflow + above[a]
            if below is not None:
                inflow = inflow - below[a]
            gain = pore[x] * (factors[a] * (dsats[a] + COMPRESS[a] * sats[a] * dp))
            acc[a, x] = gain - inflow
        cur, below = nxt, above


def add_outer(dims, fluxes, acc):
    cx, cy, _, _ = dims
    for a in range(3):
        acc[a, 0] = acc[a, 0] + fluxes[0][a]
        acc[a, cx - 1] = acc[a, cx - 1] - fluxes[1][a]
        acc[a, :, 0, :] = acc[a, :, 0, :] + fluxes[2][a]
        acc[a, :, cy - 1, :] = acc[a, :, cy - 1, :] - fluxes[3][a]


def residual_inner_kernel(dims, make, field, pore, old_mass, *refs):
    if make:
        perm, acc, fx, fy, fz, edge_x, edge_y = refs
        inner_trans(dims, perm, fx, fy, fz, edge_x, edge_y)
    else:
        fx, fy, fz, acc = refs
    residual_planes(dims, field, pore, old_mass, fx, fy, fz, acc)


def jacobian_inner_kernel(dims, field, direction, pore, fx, fy, fz, acc):
    jacobian_planes(dims, field, direction, pore, fx, fy, fz, acc)


def rows_of(ref, count):
    return tuple(ref[f * count:(f + 1) * count, :] for f in range(3))


def finish_faults(dims, inner, flux, idx, values, fluxes, acc):
    cx, cy, n_fault, _ = dims
    for a in range(3):
        values[a, 0:n_fault, :] = -flux[a]
    total = scatter_loop(values, idx, 0, n_fault * LANES, cx * cy)
    for a in range(3):
        acc[a] = inner[a] + total[:, a * LANES:(a + 1) * LANES].reshape(cx, cy, LANES)
    add_outer(dims, fluxes, acc)


def residual_fault_kernel(dims, sizes, make, *refs):
    _, _, n_fault, _ = dims
    refs = list(refs)
    take = lambda n: [refs.pop(0) for _ in range(n)]
    inner, field, idx, pidx, tr, own = take(6)
    gx_a, gx_b, mine, gy_a, gy_b = take(5)
    edges, outer = (take(2), None) if make else (None, take(2))
    acc, partner_vals = take(2)
    if make:
        outer = take(2)
    partner, values, ptable = take(3)
    received = (gx_a, gx_b, gy_a, gy_b)
    if make:
        outer_trans(dims, sizes, *edges, *received, *outer)
    stack_partners(dims, mine, gy_a, gy_b, partner)
    pick_partners(dims, partner, pidx, ptable, partner_vals)
    mine_f, other_f = rows_of(own, n_fault), rows_of(partner_vals, n_fault)
    flux = face(tr[...], mine_f[0], mob_of(mine_f), other_f[0], mob_of(other_f))
    fluxes = []
    for k, (far_f, near_f) in enumerate(zip(halo_fields(dims, *received), outermost(dims, field))):
        low, high = (far_f, near_f) if k % 2 == 0 else (near_f, far_f)
        trans = outer[k // 2][k % 2]
        fluxes.append(face(trans, low[0], mob_of(low), high[0], mob_of(high)))
    finish_faults(dims, inner, flux, idx, values, fluxes, acc)


def jacobian_fault_kernel(dims, *refs):
    _, _, n_fault, _ = dims
    refs = list(refs)
    take = lambda n: [refs.pop(0) for _ in range(n)]
    inner, field, direction, idx, pidx, tr = take(6)
    own, other, down = take(3)
    outer = take(2)
    received = take(4)
    dgx_a, dgx_b, mine, dgy_a, dgy_b = take(5)
    (acc,) = take(1)
    partner, values, ptable, dother = take(4)
    stack_partners(dims, mine, dgy_a, dgy_b, partner)
    pick_partners(dims, partner, pidx, ptable, dother)
    flux = between(
        tr[...],
        point(rows_of(own, n_fault), rows_of(down, n_fault)),
        point(rows_of(other, n_fault), rows_of(dother, n_fault)),
    )
    fluxes = []
    groups = zip(
        halo_fields(dims, *received), halo_fields(dims, dgx_a, dgx_b, dgy_a, dgy_b),
        outermost(dims, field), outermost(dims, direction),
    )
    for k, (far_f, far_d, near_f, near_d) in enumerate(groups):
        there, here = point(far_f, far_d), point(near_f, near_d)
        low, high = (there, here) if k % 2 == 0 else (here, there)
        fluxes.append(between(outer[k // 2][k % 2], low, high))
    finish_faults(dims, inner, flux, idx, values, fluxes, acc)


def well_sums(dims, rates, idx, values):
    cx, cy, n_fault, _ = dims
    for a in range(3):
        values[a] = rates[a]
    start = n_fault * LANES
    total = scatter_loop(values, idx, start, start + 6 * LANES, cx * cy)
    return [total[:, a * LANES:(a + 1) * LANES].reshape(cx, cy, LANES) for a in range(3)]


def residual_kernel(dims, sizes, final, far_y, *refs):
    refs = list(refs)
    take = lambda n: [refs.pop(0) for _ in range(n)]
    partial, scaling, idx, static = take(4)
    mine, gy_a, gy_b = take(3)
    far = take(far_y)
    direction, seg, const = take(3)
    outs = take(6)
    if final:
        residual, well = take(2)
    packs, values = take(2)
    choose_packets("gy", sizes[1], mine, gy_a, gy_b, far, packs)
    segment_values(packs, seg)
    well_constants(packs, const)
    rates = well_rates(seg, const)
    if final:
        done = running_sum(rates[0] + rates[1] + rates[2])[1:2, :]
        well[...] = done / packs[2, 13:14, :] - 1.0
    sums = well_sums(dims, rates, idx, values)
    for a in range(3):
        res = partial[a] + sums[a]
        if final:
            residual[a] = res
        direction[a] = scaling[a] * res
    emit(dims, direction, idx, static, outs)


def jacobian_kernel(dims, sizes, final, far_y, *refs):
    refs = list(refs)
    take = lambda n: [refs.pop(0) for _ in range(n)]
    partial, field, direction, scaling, idx, static, seg, const = take(8)
    mine, dgy_a, dgy_b = take(3)
    far = take(far_y)
    (result,) = take(1)
    outs = None if final else take(6)
    packs, values, dseg = take(3)
    choose_packets("gy", sizes[1], mine, dgy_a, dgy_b, far, packs)
    segment_values(packs, dseg)
    sums = well_sums(dims, well_rate_tangents(seg, dseg, const), idx, values)
    for a in range(3):
        step = 2.0 * direction[a] - scaling[a] * (partial[a] + sums[a])
        result[a] = step if final else field[a] - step
    if not final:
        emit(dims, result, idx, static, outs)


def exchange_pairs(axis, kind, size_x, size_y):
    def partner(i, count):
        step = 1 if kind < 2 else 2
        shift = step if kind % 2 else 0
        if shift and not shift <= i < count - shift:
            return None
        return ((i + shift) ^ step) - shift

    out = []
    for i in range(size_x):
        for j in range(size_y):
            if axis == 0:
                got = partner(i, size_x)
                far = (got, j) if got is not None else ((i, j ^ 1) if kind < 2 else (i ^ 1, j))
            else:
                got = partner(j, size_y)
                far = (i, got) if got is not None else ((i ^ 1, j) if kind < 2 else (i, j ^ 1))
            out.append((i * size_y + j, far[0] * size_y + far[1]))
    return out


def body(
    state, perm, pore, old_mass, scaling, fault_cell, fault_tile, fault_row, fault_trans,
    fault_export, perf_cell, well_segments, well_index, bhp, target,
):
    size_x, size_y = lax.axis_size("gx"), lax.axis_size("gy")
    _, cx, cy, _ = state.shape
    wells, segs = well_index.shape[2:]
    n_fault, n_exp = fault_cell.shape[-1] // LANES, fault_export.shape[-1] // LANES
    dims = (cx, cy, n_fault, n_exp)
    far_x = 1 if size_x == 4 else 2
    far_y = 1 if size_y == 4 else 2
    params = pltpu.CompilerParams(vmem_limit_bytes=VMEM_BYTES)
    anywhere = pl.BlockSpec(memory_space=pl.ANY)
    hbm = pl.BlockSpec(memory_space=pltpu.HBM)
    vmem = pl.BlockSpec(memory_space=pltpu.VMEM)
    shape = lambda *dims_: jax.ShapeDtypeStruct(dims_, F32)
    rows = cx * cy
    gx_rows = PACK + 3 * n_exp + 3 * cy
    gy_rows = PACK + 9 * n_exp + 3 * cx
    table = jax.ShapeDtypeStruct((3 * LANES, 2 * rows), BF16)

    def call(kernel, args, outs, scratch=(), specs=None):
        return pl.pallas_call(
            kernel,
            out_shape=outs,
            in_specs=specs or [vmem] * len(args),
            out_specs=[vmem] * len(outs),
            scratch_shapes=scratch,
            compiler_params=params,
        )(*args)

    def message_shapes(first):
        more_x, more_y = (cy, cx) if first else (0, 0)
        return [
            shape(gx_rows + more_x, LANES), shape(gx_rows + more_x, LANES), shape(PACK, LANES),
            shape(3 * cx + more_y, LANES), shape(3 * cx + more_y, LANES), table,
        ]

    def send(value, axis, kind):
        return lax.ppermute(value, ("gx", "gy"), exchange_pairs(axis, kind, size_x, size_y))

    def send_x(messages):
        msg_a, msg_b, packet = messages[:3]
        far = [send(packet, 0, 2 + k) for k in range(far_x)]
        rec_b = send(msg_b, 0, 1)
        rec_a = send(msg_a, 0, 0)
        return rec_a, rec_b, far

    def send_y(messages, got, after):
        msg_a, _, _, yfa, yfb, _ = messages
        rec_a, rec_b, far = got
        total = PACK + 9 * n_exp + yfa.shape[0]
        mid_a, mid_b, mid_c = call(
            functools.partial(middle_kernel, dims, sizes, far_x),
            [*after, msg_a, rec_a, rec_b, *far, yfa, yfb],
            [shape(total, LANES), shape(total, LANES), shape(PACK, LANES)],
            [pltpu.VMEM((5, PACK, LANES), F32)],
            [anywhere] * 2 + [vmem] * (5 + far_x),
        )
        got_b = send(mid_b, 1, 1)
        got_a = send(mid_a, 1, 0)
        got_far = [send(mid_c, 1, 2 + k) for k in range(far_y)]
        return (mid_a, got_a, got_b), got_far

    sizes = (size_x, size_y)
    grid = shape(3, cx, cy, LANES)
    wide_rows = shape(3 * n_fault, LANES)
    small = shape(24, LANES)
    packs = pltpu.VMEM((5, PACK, LANES), F32)
    fault_work = [
        pltpu.VMEM((3, LANES, LANES), F32), pltpu.VMEM((3, n_fault, LANES), F32),
        pltpu.VMEM((3 * LANES, 2 * LANES), BF16),
    ]
    well_work = [packs, pltpu.VMEM((3, 8, LANES), F32)]
    columns = (n_fault + 6 + n_exp) * LANES

    sources = [state, perm, fault_cell, fault_export, perf_cell, well_index, well_segments, bhp, target]
    results = call(
        functools.partial(first_kernel, dims),
        [pltpu.with_memory_space_constraint(v, pltpu.HBM) for v in sources],
        message_shapes(True) + [jax.ShapeDtypeStruct((1, columns), jnp.int32), shape(8, LANES)],
        [(pltpu.VMEM if i < 6 else pltpu.SMEM)(v.shape, v.dtype) for i, v in enumerate(sources)]
        + [pltpu.VMEM((8, LANES), F32), pltpu.SemaphoreType.DMA((len(sources),))],
        [hbm] * len(sources),
    )
    messages, (idx, static) = results[:6], results[6:]
    current = state

    def own_cells(cells_table):
        return call(functools.partial(gather_kernel, dims), [cells_table, idx], [wide_rows])[0]

    for step in range(2):
        final = step == 1
        got = send_x(messages)
        gx_got = got[:2]
        if final:
            (inner,) = call(
                functools.partial(residual_inner_kernel, dims, False), [current, pore, old_mass, *trans], [grid]
            )
        else:
            inner, *trans, edge_x, edge_y = call(
                functools.partial(residual_inner_kernel, dims, True), [current, pore, old_mass, perm],
                [grid, shape(cx, cy, LANES), shape(cx, cy, LANES), shape(cx, cy, LANES),
                 shape(2, cy, LANES), shape(2, cx, LANES)],
            )
            pidx, tr = call(
                functools.partial(connection_kernel, dims, size_y),
                [fault_tile.reshape(1, -1), fault_row.reshape(1, -1), fault_trans.reshape(1, -1)],
                [jax.ShapeDtypeStruct((1, n_fault * LANES), jnp.int32), shape(n_fault, LANES)],
            )
        own = own_cells(messages[5])
        gy_got, gy_far = send_y(messages, got, (inner, own))
        results = call(
            functools.partial(residual_fault_kernel, dims, sizes, not final),
            [inner, current, idx, pidx, tr, own, *gx_got, *gy_got] + ([*outer] if final else [edge_x, edge_y]),
            [grid, wide_rows] + ([] if final else [shape(2, cy, LANES), shape(2, cx, LANES)]),
            fault_work,
        )
        partial, other = results[:2]
        if not final:
            outer = results[2:]
        results = call(
            functools.partial(residual_kernel, dims, sizes, final, far_y),
            [partial, scaling, idx, static, *gy_got, *gy_far],
            [grid, small, small] + message_shapes(False) + ([grid, shape(1, LANES)] if final else []),
            well_work,
        )
        direction, seg, const = results[:3]
        messages = results[3:9]
        if final:
            residual, well = results[9:]
        got = send_x(messages)
        (inner,) = call(
            functools.partial(jacobian_inner_kernel, dims), [current, direction, pore, *trans], [grid]
        )
        down = own_cells(messages[5])
        dgy_got, dgy_far = send_y(messages, got, (inner, down))
        (partial,) = call(
            functools.partial(jacobian_fault_kernel, dims),
            [inner, current, direction, idx, pidx, tr, own, other, down, *outer, *gx_got, *gy_got[1:],
             *got[:2], *dgy_got],
            [grid],
            fault_work + [pltpu.VMEM((3 * n_fault, LANES), F32)],
        )
        results = call(
            functools.partial(jacobian_kernel, dims, sizes, final, far_y),
            [partial, current, direction, scaling, idx, static, seg, const, *dgy_got, *dgy_far],
            [grid] + ([] if final else message_shapes(False)),
            well_work + [pltpu.VMEM((24, LANES), F32)],
        )
        current, messages = results[0], results[1:]
    half = LANES // 2
    well_res = well[0, half:].reshape(wells, segs)[:, segs - 1]
    return residual, current, well_res.reshape(1, 1, wells)


def solution(mesh):
    grid = P(None, "gx", "gy", None)
    tile = P("gx", "gy", None)
    return jax.shard_map(
        body,
        mesh=mesh,
        in_specs=(
            grid, grid, tile, grid, grid, tile, tile, tile, tile, tile,
            P("gx", "gy", None, None, None, None), tile, P("gx", "gy", None, None), tile, tile,
        ),
        out_specs=(grid, grid, tile),
        check_vma=False,
    )
```

```python
import functools

import jax
import jax.numpy as jnp
from jax import lax
from jax.experimental import pallas as pl
from jax.experimental.pallas import tpu as pltpu
from jax.sharding import PartitionSpec as P

VISCOSITY = (0.5, 2.0, 0.1)
COMPRESS = (0.02, 0.05, 0.3)
DENSITY = (1.0, 0.8, 0.2)
GRAVITY = 0.2
INV_SMOOTHING = 10.0
HEAD_SCALE = 0.3

LANES = 128
PACK = 32
PLANE = 16
VMEM_BYTES = 40 * 1024 * 1024
F32 = jnp.float32
BF16 = jnp.bfloat16


def props(field):
    p, sw, sg = field
    sats = (sw, 1.0 - sw - sg, sg)
    factors = tuple(jnp.exp(COMPRESS[a] * p) for a in range(3))
    return sats, factors


def mobilities(sats, factors):
    return tuple(sats[a] * sats[a] * factors[a] * (1.0 / VISCOSITY[a]) for a in range(3))


def tangents(sats, factors, mob, dfield):
    dp, dsw, dsg = dfield
    dsats = (dsw, -(dsw + dsg), dsg)
    dmob = tuple(
        mob[a] * (COMPRESS[a] * dp) + sats[a] * factors[a] * (2.0 / VISCOSITY[a]) * dsats[a]
        for a in range(3)
    )
    return dsats, dmob


def face(trans, p_c, mob_c, p_n, mob_n, depth=0.0):
    out = []
    diff = p_n - p_c
    for a in range(3):
        if a == 0 or depth:
            pot = diff - GRAVITY * DENSITY[a] * depth if depth else diff
            weight = jax.nn.sigmoid(pot * INV_SMOOTHING)
            scaled = trans * pot
        out.append(scaled * (mob_c[a] + weight * (mob_n[a] - mob_c[a])))
    return out


def face_tangent(trans, p_c, mob_c, p_n, mob_n, dp_c, dmob_c, dp_n, dmob_n, depth=0.0):
    out = []
    diff = p_n - p_c
    ddiff = dp_n - dp_c
    for a in range(3):
        if a == 0 or depth:
            pot = diff - GRAVITY * DENSITY[a] * depth if depth else diff
            weight = jax.nn.sigmoid(pot * INV_SMOOTHING)
            dweight = (weight * (1.0 - weight)) * (ddiff * INV_SMOOTHING)
        step = mob_n[a] - mob_c[a]
        mean = mob_c[a] + weight * step
        dmean = dmob_c[a] + weight * (dmob_n[a] - dmob_c[a]) + dweight * step
        out.append(trans * (mean * ddiff + pot * dmean))
    return out


def split2(x):
    high = x.astype(BF16)
    return high, (x - high.astype(F32)).astype(BF16)


def one_hot_rows(idx, count):
    rows = (idx >> 7).astype(F32).astype(BF16)
    at = lax.broadcasted_iota(jnp.int32, (count, idx.shape[1]), 0).astype(F32).astype(BF16)
    return jnp.where(at == rows, jnp.ones((), BF16), jnp.zeros((), BF16))


def even_at(axis):
    return (lax.axis_index(axis) & 1) == 0


def gather_loop(table_ref, count, idx_ref, start, columns, put):
    for c in range(start, columns, 256):
        width = min(256, columns - c)
        idx = idx_ref[:, c:c + width]
        hot = one_hot_rows(idx, count)
        picked = jnp.dot(
            table_ref[...], jnp.concatenate([hot, hot], axis=0), preferred_element_type=F32
        )
        lane = idx & (LANES - 1)
        for h in range(width // LANES):
            cols = slice(h * LANES, (h + 1) * LANES)
            mask = lax.broadcasted_iota(jnp.int32, (LANES, LANES), 0) == lane[:, cols]
            for f in range(3):
                block = picked[f * LANES:(f + 1) * LANES, cols]
                value = jnp.sum(jnp.where(mask, block, 0.0), axis=0, keepdims=True)
                put(c // LANES + h, f, value)


def scatter_loop(values_ref, idx_ref, start, columns, count):
    total = jnp.zeros((3 * LANES, count), F32)
    for c in range(start, columns, 256):
        width = min(256, columns - c)
        idx = idx_ref[:, c:c + width]
        hot = one_hot_rows(idx, count)
        lane = (idx & (LANES - 1)).astype(F32).astype(BF16)
        at = lax.broadcasted_iota(jnp.int32, (LANES, width), 0).astype(F32).astype(BF16)
        mask = at == lane
        highs, lows = [], []
        for f in range(3):
            r = (c - start) // LANES
            row = jnp.concatenate(
                [values_ref[f, r + h:r + h + 1, :] for h in range(width // LANES)], axis=1
            )
            high, low = split2(row)
            highs.append(jnp.where(mask, high, jnp.zeros((), BF16)))
            lows.append(jnp.where(mask, low, jnp.zeros((), BF16)))
        right = jnp.concatenate(
            [jnp.concatenate(highs, axis=0), jnp.concatenate(lows, axis=0)], axis=1
        )
        left = jnp.concatenate([hot, hot], axis=1)
        total = total + lax.dot_general(
            right, left, (((1,), (1,)), ((), ())), preferred_element_type=F32
        )
    return total


def fill_table(table_ref, f, cells):
    rows = cells.shape[0]
    high, low = split2(cells.T)
    table_ref[f * LANES:(f + 1) * LANES, 0:rows] = high
    table_ref[f * LANES:(f + 1) * LANES, rows:2 * rows] = low


def emit(dims, field_ref, idx_ref, static_ref, outs, perm_ref=None):
    gxa, gxb, gxp, yfa, yfb, table_ref = outs
    cx, cy, n_fault, n_exp = dims
    rows = cx * cy
    zeros = jnp.zeros((PACK, LANES), F32)
    for ref in (gxa, gxb, gxp):
        ref[0:PACK, :] = zeros
        ref[9:11, :] = static_ref[0:2, :]
    even_x, even_y = even_at("gx"), even_at("gy")
    base = PACK + 3 * n_exp

    def put_faces(out_a, out_b, at, low, high, even):
        count = low.shape[0]
        out_a[at:at + count, :] = jnp.where(even, high, low)
        out_b[at:at + count, :] = jnp.where(even, low, high)

    for f in range(3):
        put_faces(gxa, gxb, base + f * cy, field_ref[f, 0], field_ref[f, cx - 1], even_x)
        put_faces(yfa, yfb, f * cx, field_ref[f, :, 0, :], field_ref[f, :, cy - 1, :], even_y)
        fill_table(table_ref, f, field_ref[f].reshape(rows, LANES))
    if perm_ref is not None:
        put_faces(gxa, gxb, base + 3 * cy, perm_ref[0, 0], perm_ref[0, cx - 1], even_x)
        put_faces(yfa, yfb, 3 * cx, perm_ref[1, :, 0, :], perm_ref[1, :, cy - 1, :], even_y)

    def put(r, f, value):
        if r < n_fault + 6:
            plane, e = divmod(r - n_fault, 3)
            at = plane * PLANE + f * 3 + e
            for ref in (gxa, gxb, gxp):
                ref[at:at + 1, :] = value
        else:
            at = PACK + f * n_exp + r - n_fault - 6
            for ref in (gxa, gxb):
                ref[at:at + 1, :] = value

    gather_loop(table_ref, rows, idx_ref, n_fault * LANES, (n_fault + 6 + n_exp) * LANES, put)


def flat_row(v, buf):
    buf[...] = jnp.zeros(buf.shape, F32)
    buf[0:v.shape[0], 0:v.shape[1]] = v
    moved = pltpu.roll(buf[...], 0, 1, stride=v.shape[1], stride_axis=0)
    return jnp.sum(moved, axis=0, keepdims=True)


def first_kernel(dims, *refs):
    sources, outs, (idx, static) = refs[:9], refs[9:15], refs[15:17]
    targets, (buf, sems) = refs[17:26], refs[26:]
    loads = [
        pltpu.make_async_copy(src, dst, sems.at[i]) for i, (src, dst) in enumerate(zip(sources, targets))
    ]
    for load in loads:
        load.start()
    state, perm, cells, exports, perf, windex, wseg, bhp, target = targets
    for load in loads[2:]:
        load.wait()
    cx, cy, n_fault, n_exp = dims
    count = n_fault * LANES
    idx[:, 0:count] = cells[0]
    idx[:, count + 6 * LANES:] = exports[0]
    for e in range(3):
        flat = [flat_row(perf[0, 0, e, k].astype(F32) + 1.0, buf) for k in range(3)]
        rows = (flat[0] + roll_half(flat[1]), flat[2])
        for plane in range(2):
            at = count + (plane * 3 + e) * LANES
            idx[:, at:at + LANES] = (rows[plane] - 1.0).astype(jnp.int32)
    shape = windex.shape[2:]
    well = lax.broadcasted_iota(jnp.int32, shape, 0)

    def spread(ref):
        value = jnp.full(shape, ref[0, 0, 0])
        for w in range(1, shape[0]):
            value = jnp.where(well == w, ref[0, 0, w], value)
        return value

    live = (lax.broadcasted_iota(jnp.int32, shape, 1) < spread(wseg)).astype(F32)
    static[...] = jnp.zeros(static.shape, F32)
    static[0:1, :] = flat_row(live * windex[0, 0], buf) + roll_half(flat_row(spread(bhp), buf))
    static[1:2, :] = flat_row(live, buf) + roll_half(flat_row(spread(target), buf))
    for load in loads[:2]:
        load.wait()
    emit(dims, state, idx, static, outs, perm)


def connection_kernel(dims, size_y, tiles, rows, trans, pidx, tr):
    _, _, n_fault, n_exp = dims
    tile = tiles[...]
    tile_x = jnp.floor((tile.astype(F32) + 0.5) * (1.0 / size_y)).astype(jnp.int32)
    tile_y = tile - tile_x * size_y
    across = tile_x - lax.axis_index("gx") + 1
    along = tile_y - lax.axis_index("gy") + 1
    pidx[...] = (across * 3 + along) * (n_exp * LANES) + rows[...]
    for r in range(n_fault):
        tr[r:r + 1, :] = trans[:, r * LANES:(r + 1) * LANES]


def gather_kernel(dims, table, idx, own):
    cx, cy, n_fault, _ = dims

    def put(r, f, value):
        own[f * n_fault + r:f * n_fault + r + 1, :] = value

    gather_loop(table, cx * cy, idx, 0, n_fault * LANES, put)


def choose_packets(axis, count, mine, rec_a, rec_b, far, pick):
    at = lax.axis_index(axis)
    even = even_at(axis)
    near = slice(0, PACK)
    a, b = rec_a[near, :], rec_b[near, :]
    if len(far) == 1:
        up_far = down_far = far[0][...]
    else:
        up = ((at >> 1) & 1) == 0
        c, d = far[0][...], far[1][...]
        up_far, down_far = jnp.where(up, c, d), jnp.where(up, d, c)
    pick[2] = mine[near, :]
    pick[3] = jnp.where(at + 1 < count, jnp.where(even, a, b), 0.0)
    pick[1] = jnp.where(at >= 1, jnp.where(even, b, a), 0.0)
    pick[4] = jnp.where(at + 2 < count, up_far, 0.0)
    pick[0] = jnp.where(at >= 2, down_far, 0.0)


def middle_kernel(dims, sizes, far_x, _, __, mine, rec_a, rec_b, *refs):
    _, _, _, n_exp = dims
    far = refs[:far_x]
    yfa, yfb, msg_a, msg_b, msg_c, pick = refs[far_x:]
    even = even_at("gx")
    choose_packets("gx", sizes[0], mine, rec_a, rec_b, far, pick)
    outs = (msg_a, msg_b, msg_c)
    for ref in outs:
        ref[0:PACK, :] = jnp.zeros((PACK, LANES), F32)
    for hx in range(3):
        for plane in range(2):
            for f in range(3):
                at = plane * PLANE + f * 3
                row = (
                    pick[hx, at + 2:at + 3, :]
                    + pick[hx + 1, at + 1:at + 2, :]
                    + pick[hx + 2, at:at + 1, :]
                )
                for ref in outs:
                    ref[at + hx:at + hx + 1, :] = row
        for ref in outs:
            ref[9 + hx:10 + hx, :] = pick[hx + 1, 9:10, :]
            ref[12 + hx:13 + hx, :] = pick[hx + 1, 10:11, :]
    rows = 3 * n_exp
    src = slice(PACK, PACK + rows)
    stack = (
        jnp.where(even, rec_b[src, :], rec_a[src, :]),
        mine[src, :],
        jnp.where(even, rec_a[src, :], rec_b[src, :]),
    )
    for hx in range(3):
        at = PACK + hx * rows
        msg_a[at:at + rows, :] = stack[hx]
        msg_b[at:at + rows, :] = stack[hx]
    at = PACK + 3 * rows
    msg_a[at:at + yfa.shape[0], :] = yfa[...]
    msg_b[at:at + yfb.shape[0], :] = yfb[...]


def roll_half(x):
    return pltpu.roll(x, LANES // 2, 1)


def low_half(shape):
    return lax.broadcasted_iota(jnp.int32, shape, 1) < LANES // 2


def segment_values(packs, seg_ref):
    tops = [packs[y, 0:PLANE, :] for y in range(5)]
    bottoms = [packs[y, PLANE:PACK, :] for y in range(5)]
    lo = low_half((PLANE, LANES))

    def home(hy):
        return tops[hy + 3] + roll_half(tops[hy + 2]) + bottoms[hy + 1]

    plane0 = jnp.where(lo, home(-1), roll_half(home(0)))
    plane1 = jnp.where(lo, home(1), 0.0)
    for f in range(3):
        seg_ref[f * 8:f * 8 + 3, :] = plane0[f * 3:f * 3 + 3, :]
        seg_ref[f * 8 + 3:f * 8 + 6, :] = plane1[f * 3:f * 3 + 3, :]
        seg_ref[f * 8 + 6:f * 8 + 8, :] = jnp.zeros((2, LANES), F32)


def well_constants(packs, const_ref):
    tops = [packs[y, 0:PLANE, :] for y in (1, 2, 3)]
    rolled = [roll_half(t) for t in tops]
    lo = low_half((PLANE, LANES))
    same0 = jnp.where(lo, tops[0], rolled[1])
    same1 = jnp.where(lo, tops[2], 0.0)
    other0 = jnp.where(lo, rolled[0], tops[1])
    other1 = rolled[2]
    const_ref[...] = jnp.zeros(const_ref.shape, F32)
    for at, (a, b), src in ((0, (same0, same1), 9), (8, (other0, other1), 9), (16, (same0, same1), 12)):
        const_ref[at:at + 3, :] = a[src:src + 3, :]
        const_ref[at + 3:at + 6, :] = b[src:src + 3, :]


def running_sum(x):
    lane = lax.broadcasted_iota(jnp.int32, x.shape, 1) & 15
    for shift in (1, 2, 4, 8):
        x = x + jnp.where(lane >= shift, pltpu.roll(x, shift, 1), 0.0)
    return x


def well_mix(seg_ref):
    field = tuple(seg_ref[f * 8:f * 8 + 8, :] for f in range(3))
    sats, factors = props(field)
    mob = mobilities(sats, factors)
    total = mob[0] + mob[1] + mob[2]
    mix = (mob[0] * DENSITY[0] + mob[1] * DENSITY[1] + mob[2] * DENSITY[2]) / total
    return field, sats, factors, mob, total, mix


def well_rates(seg_ref, const_ref):
    weight, bhp, live = (const_ref[i * 8:i * 8 + 8, :] for i in range(3))
    field, _, _, mob, _, mix = well_mix(seg_ref)
    press = bhp + HEAD_SCALE * running_sum(live * mix)
    return [weight * mob[a] * (field[0] - press) for a in range(3)]


def well_rate_tangents(seg_ref, dseg_ref, const_ref):
    weight, bhp, live = (const_ref[i * 8:i * 8 + 8, :] for i in range(3))
    field, sats, factors, mob, total, mix = well_mix(seg_ref)
    press = bhp + HEAD_SCALE * running_sum(live * mix)
    dfield = tuple(dseg_ref[f * 8:f * 8 + 8, :] for f in range(3))
    _, dmob = tangents(sats, factors, mob, dfield)
    dtotal = dmob[0] + dmob[1] + dmob[2]
    dnum = dmob[0] * DENSITY[0] + dmob[1] * DENSITY[1] + dmob[2] * DENSITY[2]
    dpress = HEAD_SCALE * running_sum(live * ((dnum - mix * dtotal) / total))
    return [
        weight * (dmob[a] * (field[0] - press) + mob[a] * (dfield[0] - dpress)) for a in range(3)
    ]


def stack_partners(dims, mine, rec_a, rec_b, partner):
    _, _, _, n_exp = dims
    even = even_at("gy")
    used = 9 * n_exp
    for f in range(3):
        for hx in range(3):
            at = PACK + hx * 3 * n_exp + f * n_exp
            src = slice(at, at + n_exp)
            first, second = rec_a[src, :], rec_b[src, :]
            blocks = (jnp.where(even, second, first), mine[src, :], jnp.where(even, first, second))
            for hy in range(3):
                to = (hx * 3 + hy) * n_exp
                partner[f, to:to + n_exp, :] = blocks[hy]
        partner[f, used:LANES, :] = jnp.zeros((LANES - used, LANES), F32)


def pick_partners(dims, partner, pidx, table, out):
    _, _, n_fault, _ = dims
    for f in range(3):
        fill_table(table, f, partner[f])

    def put(r, f, value):
        out[f * n_fault + r:f * n_fault + r + 1, :] = value

    gather_loop(table, LANES, pidx, 0, n_fault * LANES, put)


def halo(axis, rec_a, rec_b, at, count):
    even = even_at(axis)
    a, b = rec_a[at:at + count, :], rec_b[at:at + count, :]
    return jnp.where(even, b, a), jnp.where(even, a, b)


def halo_fields(dims, gx_a, gx_b, gy_a, gy_b):
    cx, cy, _, n_exp = dims
    xs = [halo("gx", gx_a, gx_b, PACK + 3 * n_exp + f * cy, cy) for f in range(3)]
    ys = [halo("gy", gy_a, gy_b, PACK + 9 * n_exp + f * cx, cx) for f in range(3)]
    return [tuple(v[side] for v in both) for both in (xs, ys) for side in range(2)]


def outermost(dims, ref):
    cx, cy, _, _ = dims
    return [
        tuple(ref[f, 0] for f in range(3)), tuple(ref[f, cx - 1] for f in range(3)),
        tuple(ref[f, :, 0, :] for f in range(3)), tuple(ref[f, :, cy - 1, :] for f in range(3)),
    ]


def edge_trans(t_a, t_b):
    return 2.0 * t_a * t_b / (t_a + t_b)


def inner_trans(dims, perm, fx, fy, fz, edge_x, edge_y):
    cx, cy, _, _ = dims
    last_row = lax.broadcasted_iota(jnp.int32, (cy, LANES), 0) == cy - 1
    last_lane = lax.broadcasted_iota(jnp.int32, (cy, LANES), 1) == LANES - 1
    for x in range(cx):
        if x + 1 < cx:
            fx[x] = edge_trans(perm[0, x], perm[0, x + 1])
        t = perm[1, x]
        fy[x] = jnp.where(last_row, 0.0, edge_trans(t, pltpu.roll(t, cy - 1, 0)))
        t = perm[2, x]
        fz[x] = jnp.where(last_lane, 0.0, edge_trans(t, pltpu.roll(t, LANES - 1, 1)))
    edge_x[0], edge_x[1] = perm[0, 0], perm[0, cx - 1]
    edge_y[0], edge_y[1] = perm[1, :, 0, :], perm[1, :, cy - 1, :]


def outer_trans(dims, sizes, edge_x, edge_y, gx_a, gx_b, gy_a, gy_b, out_x, out_y):
    cx, cy, _, n_exp = dims
    at_x, at_y = lax.axis_index("gx"), lax.axis_index("gy")
    low_x, high_x = halo("gx", gx_a, gx_b, PACK + 3 * n_exp + 3 * cy, cy)
    low_y, high_y = halo("gy", gy_a, gy_b, PACK + 9 * n_exp + 3 * cx, cx)
    out_x[0] = jnp.where(at_x > 0, edge_trans(low_x, edge_x[0]), 0.0)
    out_x[1] = jnp.where(at_x < sizes[0] - 1, edge_trans(edge_x[1], high_x), 0.0)
    out_y[0] = jnp.where(at_y > 0, edge_trans(low_y, edge_y[0]), 0.0)
    out_y[1] = jnp.where(at_y < sizes[1] - 1, edge_trans(edge_y[1], high_y), 0.0)


def mob_of(field):
    return mobilities(*props(field))


def residual_planes(dims, field, pore, fx, fy, fz, acc):
    cx, cy, _, _ = dims

    def plane(x):
        fld = tuple(field[f, x] for f in range(3))
        sats, factors = props(fld)
        return fld[0], mobilities(sats, factors), sats, factors

    cur, below = plane(0), None
    for x in range(cx):
        p, mob, sats, factors = cur
        row = lambda v: pltpu.roll(v, cy - 1, 0)
        lane = lambda v: pltpu.roll(v, LANES - 1, 1)
        y_up = face(fy[x], p, mob, row(p), [row(m) for m in mob])
        z_up = face(fz[x], p, mob, lane(p), [lane(m) for m in mob], 1.0)
        nxt = above = None
        if x + 1 < cx:
            nxt = plane(x + 1)
            above = face(fx[x], p, mob, nxt[0], nxt[1])
        for a in range(3):
            inflow = (y_up[a] - pltpu.roll(y_up[a], 1, 0)) + (z_up[a] - pltpu.roll(z_up[a], 1, 1))
            if above is not None:
                inflow = inflow + above[a]
            if below is not None:
                inflow = inflow - below[a]
            acc[a, x] = pore[x] * (factors[a] * sats[a]) - inflow
        cur, below = nxt, above


def point(field, dfield):
    sats, factors = props(field)
    mob = mobilities(sats, factors)
    dsats, dmob = tangents(sats, factors, mob, dfield)
    return field[0], mob, dfield[0], dmob, sats, factors, dsats


def between(trans, c, n, depth=0.0):
    return face_tangent(trans, c[0], c[1], n[0], n[1], c[2], c[3], n[2], n[3], depth)


def jacobian_planes(dims, field, dfield, pore, fx, fy, fz, acc):
    cx, cy, _, _ = dims

    def plane(x):
        return point(tuple(field[f, x] for f in range(3)), tuple(dfield[f, x] for f in range(3)))

    def moved(c, shift):
        return shift(c[0]), [shift(m) for m in c[1]], shift(c[2]), [shift(m) for m in c[3]]

    cur, below = plane(0), None
    for x in range(cx):
        y_up = between(fy[x], cur, moved(cur, lambda v: pltpu.roll(v, cy - 1, 0)))
        z_up = between(fz[x], cur, moved(cur, lambda v: pltpu.roll(v, LANES - 1, 1)), 1.0)
        nxt = above = None
        if x + 1 < cx:
            nxt = plane(x + 1)
            above = between(fx[x], cur, nxt)
        _, _, dp, _, sats, factors, dsats = cur
        for a in range(3):
            inflow = (y_up[a] - pltpu.roll(y_up[a], 1, 0)) + (z_up[a] - pltpu.roll(z_up[a], 1, 1))
            if above is not None:
                inflow = inflow + above[a]
            if below is not None:
                inflow = inflow - below[a]
            gain = pore[x] * (factors[a] * (dsats[a] + COMPRESS[a] * sats[a] * dp))
            acc[a, x] = gain - inflow
        cur, below = nxt, above


def add_outer(dims, fluxes, acc):
    cx, cy, _, _ = dims
    for a in range(3):
        acc[a, 0] = acc[a, 0] + fluxes[0][a]
        acc[a, cx - 1] = acc[a, cx - 1] - fluxes[1][a]
        acc[a, :, 0, :] = acc[a, :, 0, :] + fluxes[2][a]
        acc[a, :, cy - 1, :] = acc[a, :, cy - 1, :] - fluxes[3][a]


def residual_inner_kernel(dims, make, field, pore, *refs):
    if make:
        perm, acc, fx, fy, fz, edge_x, edge_y = refs
        inner_trans(dims, perm, fx, fy, fz, edge_x, edge_y)
    else:
        fx, fy, fz, acc = refs
    residual_planes(dims, field, pore, fx, fy, fz, acc)


def jacobian_inner_kernel(dims, field, direction, pore, fx, fy, fz, acc):
    jacobian_planes(dims, field, direction, pore, fx, fy, fz, acc)


def rows_of(ref, count):
    return tuple(ref[f * count:(f + 1) * count, :] for f in range(3))


def finish_faults(dims, inner, old_mass, flux, idx, values, fluxes, acc):
    cx, cy, n_fault, _ = dims
    for a in range(3):
        values[a, 0:n_fault, :] = -flux[a]
    total = scatter_loop(values, idx, 0, n_fault * LANES, cx * cy)
    for a in range(3):
        part = inner[a] + total[a * LANES:(a + 1) * LANES, :].T.reshape(cx, cy, LANES)
        acc[a] = part if old_mass is None else part - old_mass[a]
    add_outer(dims, fluxes, acc)


def residual_fault_kernel(dims, sizes, make, *refs):
    _, _, n_fault, _ = dims
    refs = list(refs)
    take = lambda n: [refs.pop(0) for _ in range(n)]
    inner, old_mass, field, idx, pidx, tr, own = take(7)
    gx_a, gx_b, mine, gy_a, gy_b = take(5)
    edges, outer = (take(2), None) if make else (None, take(2))
    acc, partner_vals = take(2)
    if make:
        outer = take(2)
    partner, values, ptable = take(3)
    received = (gx_a, gx_b, gy_a, gy_b)
    if make:
        outer_trans(dims, sizes, *edges, *received, *outer)
    stack_partners(dims, mine, gy_a, gy_b, partner)
    pick_partners(dims, partner, pidx, ptable, partner_vals)
    mine_f, other_f = rows_of(own, n_fault), rows_of(partner_vals, n_fault)
    flux = face(tr[...], mine_f[0], mob_of(mine_f), other_f[0], mob_of(other_f))
    fluxes = []
    for k, (far_f, near_f) in enumerate(zip(halo_fields(dims, *received), outermost(dims, field))):
        low, high = (far_f, near_f) if k % 2 == 0 else (near_f, far_f)
        trans = outer[k // 2][k % 2]
        fluxes.append(face(trans, low[0], mob_of(low), high[0], mob_of(high)))
    finish_faults(dims, inner, old_mass, flux, idx, values, fluxes, acc)


def jacobian_fault_kernel(dims, *refs):
    _, _, n_fault, _ = dims
    refs = list(refs)
    take = lambda n: [refs.pop(0) for _ in range(n)]
    inner, field, direction, idx, pidx, tr = take(6)
    own, other, down = take(3)
    outer = take(2)
    received = take(4)
    dgx_a, dgx_b, mine, dgy_a, dgy_b = take(5)
    (acc,) = take(1)
    partner, values, ptable, dother = take(4)
    stack_partners(dims, mine, dgy_a, dgy_b, partner)
    pick_partners(dims, partner, pidx, ptable, dother)
    flux = between(
        tr[...],
        point(rows_of(own, n_fault), rows_of(down, n_fault)),
        point(rows_of(other, n_fault), rows_of(dother, n_fault)),
    )
    fluxes = []
    groups = zip(
        halo_fields(dims, *received), halo_fields(dims, dgx_a, dgx_b, dgy_a, dgy_b),
        outermost(dims, field), outermost(dims, direction),
    )
    for k, (far_f, far_d, near_f, near_d) in enumerate(groups):
        there, here = point(far_f, far_d), point(near_f, near_d)
        low, high = (there, here) if k % 2 == 0 else (here, there)
        fluxes.append(between(outer[k // 2][k % 2], low, high))
    finish_faults(dims, inner, None, flux, idx, values, fluxes, acc)


def well_sums(dims, rates, idx, values):
    cx, cy, n_fault, _ = dims
    for a in range(3):
        values[a] = rates[a]
    start = n_fault * LANES
    total = scatter_loop(values, idx, start, start + 6 * LANES, cx * cy)
    return [total[a * LANES:(a + 1) * LANES, :].T.reshape(cx, cy, LANES) for a in range(3)]


def residual_kernel(dims, sizes, final, far_y, *refs):
    refs = list(refs)
    take = lambda n: [refs.pop(0) for _ in range(n)]
    partial, scaling, idx, static = take(4)
    mine, gy_a, gy_b = take(3)
    far = take(far_y)
    direction, seg, const = take(3)
    outs = take(6)
    if final:
        residual, well = take(2)
    packs, values = take(2)
    choose_packets("gy", sizes[1], mine, gy_a, gy_b, far, packs)
    segment_values(packs, seg)
    well_constants(packs, const)
    rates = well_rates(seg, const)
    if final:
        done = running_sum(rates[0] + rates[1] + rates[2])[1:2, :]
        value = done / packs[2, 13:14, :] - 1.0
        lane = lax.broadcasted_iota(jnp.int32, value.shape, 1)
        column = lax.broadcasted_iota(jnp.int32, well.shape, 2)
        count = well.shape[2]
        result = jnp.zeros(well.shape, F32)
        for w in range(count):
            last = LANES // 2 + (w + 1) * (LANES // 2 // count) - 1
            result = jnp.where(column == w, jnp.sum(jnp.where(lane == last, value, 0.0)), result)
        well[...] = result
    sums = well_sums(dims, rates, idx, values)
    for a in range(3):
        res = partial[a] + sums[a]
        if final:
            residual[a] = res
        direction[a] = scaling[a] * res
    emit(dims, direction, idx, static, outs)


def jacobian_kernel(dims, sizes, final, far_y, *refs):
    refs = list(refs)
    take = lambda n: [refs.pop(0) for _ in range(n)]
    partial, field, direction, scaling, idx, static, seg, const = take(8)
    mine, dgy_a, dgy_b = take(3)
    far = take(far_y)
    (result,) = take(1)
    outs = None if final else take(6)
    packs, values, dseg = take(3)
    choose_packets("gy", sizes[1], mine, dgy_a, dgy_b, far, packs)
    segment_values(packs, dseg)
    sums = well_sums(dims, well_rate_tangents(seg, dseg, const), idx, values)
    for a in range(3):
        step = 2.0 * direction[a] - scaling[a] * (partial[a] + sums[a])
        result[a] = step if final else field[a] - step
    if not final:
        emit(dims, result, idx, static, outs)


def exchange_pairs(axis, kind, size_x, size_y):
    def partner(i, count):
        step = 1 if kind < 2 else 2
        shift = step if kind % 2 else 0
        if shift and not shift <= i < count - shift:
            return None
        return ((i + shift) ^ step) - shift

    out = []
    for i in range(size_x):
        for j in range(size_y):
            if axis == 0:
                got = partner(i, size_x)
                far = (got, j) if got is not None else ((i, j ^ 1) if kind < 2 else (i ^ 1, j))
            else:
                got = partner(j, size_y)
                far = (i, got) if got is not None else ((i ^ 1, j) if kind < 2 else (i, j ^ 1))
            out.append((i * size_y + j, far[0] * size_y + far[1]))
    return out


def body(
    state, perm, pore, old_mass, scaling, fault_cell, fault_tile, fault_row, fault_trans,
    fault_export, perf_cell, well_segments, well_index, bhp, target,
):
    size_x, size_y = lax.axis_size("gx"), lax.axis_size("gy")
    _, cx, cy, _ = state.shape
    wells, segs = well_index.shape[2:]
    n_fault, n_exp = fault_cell.shape[-1] // LANES, fault_export.shape[-1] // LANES
    dims = (cx, cy, n_fault, n_exp)
    far_x = 1 if size_x == 4 else 2
    far_y = 1 if size_y == 4 else 2
    params = pltpu.CompilerParams(vmem_limit_bytes=VMEM_BYTES)
    anywhere = pl.BlockSpec(memory_space=pl.ANY)
    hbm = pl.BlockSpec(memory_space=pltpu.HBM)
    vmem = pl.BlockSpec(memory_space=pltpu.VMEM)
    shape = lambda *dims_: jax.ShapeDtypeStruct(dims_, F32)
    rows = cx * cy
    gx_rows = PACK + 3 * n_exp + 3 * cy
    gy_rows = PACK + 9 * n_exp + 3 * cx
    table = jax.ShapeDtypeStruct((3 * LANES, 2 * rows), BF16)

    def call(kernel, args, outs, scratch=(), specs=None):
        return pl.pallas_call(
            kernel,
            out_shape=outs,
            in_specs=specs or [vmem] * len(args),
            out_specs=[vmem] * len(outs),
            scratch_shapes=scratch,
            compiler_params=params,
        )(*args)

    def message_shapes(first):
        more_x, more_y = (cy, cx) if first else (0, 0)
        return [
            shape(gx_rows + more_x, LANES), shape(gx_rows + more_x, LANES), shape(PACK, LANES),
            shape(3 * cx + more_y, LANES), shape(3 * cx + more_y, LANES), table,
        ]

    def send(value, axis, kind):
        return lax.ppermute(value, ("gx", "gy"), exchange_pairs(axis, kind, size_x, size_y))

    def send_x(messages):
        msg_a, msg_b, packet = messages[:3]
        far = [send(packet, 0, 2 + k) for k in range(far_x)]
        rec_b = send(msg_b, 0, 1)
        rec_a = send(msg_a, 0, 0)
        return rec_a, rec_b, far

    def send_y(messages, got, after):
        msg_a, _, _, yfa, yfb, _ = messages
        rec_a, rec_b, far = got
        total = PACK + 9 * n_exp + yfa.shape[0]
        mid_a, mid_b, mid_c = call(
            functools.partial(middle_kernel, dims, sizes, far_x),
            [*after, msg_a, rec_a, rec_b, *far, yfa, yfb],
            [shape(total, LANES), shape(total, LANES), shape(PACK, LANES)],
            [pltpu.VMEM((5, PACK, LANES), F32)],
            [anywhere] * 2 + [vmem] * (5 + far_x),
        )
        got_b = send(mid_b, 1, 1)
        got_a = send(mid_a, 1, 0)
        got_far = [send(mid_c, 1, 2 + k) for k in range(far_y)]
        return (mid_a, got_a, got_b), got_far

    sizes = (size_x, size_y)
    grid = shape(3, cx, cy, LANES)
    wide_rows = shape(3 * n_fault, LANES)
    small = shape(24, LANES)
    packs = pltpu.VMEM((5, PACK, LANES), F32)
    fault_work = [
        pltpu.VMEM((3, LANES, LANES), F32), pltpu.VMEM((3, n_fault, LANES), F32),
        pltpu.VMEM((3 * LANES, 2 * LANES), BF16),
    ]
    well_work = [packs, pltpu.VMEM((3, 8, LANES), F32)]
    columns = (n_fault + 6 + n_exp) * LANES

    sources = [state, perm, fault_cell, fault_export, perf_cell, well_index, well_segments, bhp, target]
    results = call(
        functools.partial(first_kernel, dims),
        [pltpu.with_memory_space_constraint(v, pltpu.HBM) for v in sources],
        message_shapes(True) + [jax.ShapeDtypeStruct((1, columns), jnp.int32), shape(8, LANES)],
        [(pltpu.VMEM if i < 6 else pltpu.SMEM)(v.shape, v.dtype) for i, v in enumerate(sources)]
        + [pltpu.VMEM((8, LANES), F32), pltpu.SemaphoreType.DMA((len(sources),))],
        [hbm] * len(sources),
    )
    messages, (idx, static) = results[:6], results[6:]
    current = state

    def own_cells(cells_table):
        return call(functools.partial(gather_kernel, dims), [cells_table, idx], [wide_rows])[0]

    for step in range(2):
        final = step == 1
        got = send_x(messages)
        gx_got = got[:2]
        if final:
            (inner,) = call(
                functools.partial(residual_inner_kernel, dims, False), [current, pore, *trans], [grid]
            )
        else:
            inner, *trans, edge_x, edge_y = call(
                functools.partial(residual_inner_kernel, dims, True), [current, pore, perm],
                [grid, shape(cx, cy, LANES), shape(cx, cy, LANES), shape(cx, cy, LANES),
                 shape(2, cy, LANES), shape(2, cx, LANES)],
            )
            pidx, tr = call(
                functools.partial(connection_kernel, dims, size_y),
                [fault_tile.reshape(1, -1), fault_row.reshape(1, -1), fault_trans.reshape(1, -1)],
                [jax.ShapeDtypeStruct((1, n_fault * LANES), jnp.int32), shape(n_fault, LANES)],
            )
        own = own_cells(messages[5])
        gy_got, gy_far = send_y(messages, got, (inner, own))
        results = call(
            functools.partial(residual_fault_kernel, dims, sizes, not final),
            [inner, old_mass, current, idx, pidx, tr, own, *gx_got, *gy_got] + ([*outer] if final else [edge_x, edge_y]),
            [grid, wide_rows] + ([] if final else [shape(2, cy, LANES), shape(2, cx, LANES)]),
            fault_work,
        )
        partial, other = results[:2]
        if not final:
            outer = results[2:]
        results = call(
            functools.partial(residual_kernel, dims, sizes, final, far_y),
            [partial, scaling, idx, static, *gy_got, *gy_far],
            [grid, small, small] + message_shapes(False) + ([grid, shape(1, 1, wells)] if final else []),
            well_work,
        )
        direction, seg, const = results[:3]
        messages = results[3:9]
        if final:
            residual, well = results[9:]
        got = send_x(messages)
        (inner,) = call(
            functools.partial(jacobian_inner_kernel, dims), [current, direction, pore, *trans], [grid]
        )
        down = own_cells(messages[5])
        dgy_got, dgy_far = send_y(messages, got, (inner, down))
        (partial,) = call(
            functools.partial(jacobian_fault_kernel, dims),
            [inner, current, direction, idx, pidx, tr, own, other, down, *outer, *gx_got, *gy_got[1:],
             *got[:2], *dgy_got],
            [grid],
            fault_work + [pltpu.VMEM((3 * n_fault, LANES), F32)],
        )
        results = call(
            functools.partial(jacobian_kernel, dims, sizes, final, far_y),
            [partial, current, direction, scaling, idx, static, seg, const, *dgy_got, *dgy_far],
            [grid] + ([] if final else message_shapes(False)),
            well_work + [pltpu.VMEM((24, LANES), F32)],
        )
        current, messages = results[0], results[1:]
    return residual, current, well


def solution(mesh):
    grid = P(None, "gx", "gy", None)
    tile = P("gx", "gy", None)
    return jax.shard_map(
        body,
        mesh=mesh,
        in_specs=(
            grid, grid, tile, grid, grid, tile, tile, tile, tile, tile,
            P("gx", "gy", None, None, None, None), tile, P("gx", "gy", None, None), tile, tile,
        ),
        out_specs=(grid, grid, tile),
        check_vma=False,
    )
```

```python
import functools

import jax
import jax.numpy as jnp
from jax import lax
from jax.experimental import pallas as pl
from jax.experimental.pallas import tpu as pltpu
from jax.sharding import PartitionSpec as P

VISCOSITY = (0.5, 2.0, 0.1)
COMPRESS = (0.02, 0.05, 0.3)
DENSITY = (1.0, 0.8, 0.2)
GRAVITY = 0.2
INV_SMOOTHING = 10.0
HEAD_SCALE = 0.3

LANES = 128
PACK = 32
PLANE = 16
VMEM_BYTES = 40 * 1024 * 1024
F32 = jnp.float32
BF16 = jnp.bfloat16


def props(field):
    p, sw, sg = field
    sats = (sw, 1.0 - sw - sg, sg)
    factors = tuple(jnp.exp(COMPRESS[a] * p) for a in range(3))
    return sats, factors


def mobilities(sats, factors):
    return tuple(sats[a] * sats[a] * factors[a] * (1.0 / VISCOSITY[a]) for a in range(3))


def tangents(sats, factors, mob, dfield):
    dp, dsw, dsg = dfield
    dsats = (dsw, -(dsw + dsg), dsg)
    dmob = tuple(
        mob[a] * (COMPRESS[a] * dp) + sats[a] * factors[a] * (2.0 / VISCOSITY[a]) * dsats[a]
        for a in range(3)
    )
    return dsats, dmob


def face(trans, p_c, mob_c, p_n, mob_n, depth=0.0):
    out = []
    diff = p_n - p_c
    for a in range(3):
        if a == 0 or depth:
            pot = diff - GRAVITY * DENSITY[a] * depth if depth else diff
            weight = jax.nn.sigmoid(pot * INV_SMOOTHING)
            scaled = trans * pot
        out.append(scaled * (mob_c[a] + weight * (mob_n[a] - mob_c[a])))
    return out


def face_tangent(trans, p_c, mob_c, p_n, mob_n, dp_c, dmob_c, dp_n, dmob_n, depth=0.0):
    out = []
    diff = p_n - p_c
    ddiff = dp_n - dp_c
    for a in range(3):
        if a == 0 or depth:
            pot = diff - GRAVITY * DENSITY[a] * depth if depth else diff
            weight = jax.nn.sigmoid(pot * INV_SMOOTHING)
            dweight = (weight * (1.0 - weight)) * (ddiff * INV_SMOOTHING)
        step = mob_n[a] - mob_c[a]
        mean = mob_c[a] + weight * step
        dmean = dmob_c[a] + weight * (dmob_n[a] - dmob_c[a]) + dweight * step
        out.append(trans * (mean * ddiff + pot * dmean))
    return out


def split2(x):
    high = x.astype(BF16)
    return high, (x - high.astype(F32)).astype(BF16)


def one_hot(place, count):
    at = lax.broadcasted_iota(jnp.int32, (count, place.shape[1]), 0).astype(F32).astype(BF16)
    return jnp.where(at == place.astype(F32).astype(BF16), jnp.ones((), BF16), jnp.zeros((), BF16))


def even_at(axis):
    return (lax.axis_index(axis) & 1) == 0


def gather_loop(table, count, by_lane, idx_ref, start, columns, put):
    kept = count if by_lane else LANES
    for c in range(start, columns, 256):
        width = min(256, columns - c)
        idx = idx_ref[:, c:c + width]
        row, lane = idx >> 7, idx & (LANES - 1)
        hot = one_hot(lane, LANES) if by_lane else one_hot(row, count)
        picked = jnp.dot(table[...], jnp.concatenate([hot, hot], axis=0), preferred_element_type=F32)
        rest = row if by_lane else lane
        for h in range(width // LANES):
            cols = slice(h * LANES, (h + 1) * LANES)
            mask = lax.broadcasted_iota(jnp.int32, (kept, LANES), 0) == rest[:, cols]
            for f in range(3):
                block = picked[f * kept:(f + 1) * kept, cols]
                value = jnp.sum(jnp.where(mask, block, 0.0), axis=0, keepdims=True)
                put(c // LANES + h, f, value)


def scatter_loop(values_ref, idx_ref, start, columns, count, turned):
    total = jnp.zeros((3 * LANES, count) if turned else (count, 3 * LANES), F32)
    for c in range(start, columns, 256):
        width = min(256, columns - c)
        idx = idx_ref[:, c:c + width]
        hot = one_hot(idx >> 7, count)
        lane = (idx & (LANES - 1)).astype(F32).astype(BF16)
        at = lax.broadcasted_iota(jnp.int32, (LANES, width), 0).astype(F32).astype(BF16)
        mask = at == lane
        highs, lows = [], []
        for f in range(3):
            r = (c - start) // LANES
            row = jnp.concatenate(
                [values_ref[f, r + h:r + h + 1, :] for h in range(width // LANES)], axis=1
            )
            high, low = split2(row)
            highs.append(jnp.where(mask, high, jnp.zeros((), BF16)))
            lows.append(jnp.where(mask, low, jnp.zeros((), BF16)))
        right = jnp.concatenate(
            [jnp.concatenate(highs, axis=0), jnp.concatenate(lows, axis=0)], axis=1
        )
        left = jnp.concatenate([hot, hot], axis=1)
        total = total + lax.dot_general(
            *((right, left) if turned else (left, right)), (((1,), (1,)), ((), ())), preferred_element_type=F32
        )
    if turned:
        return [total[f * LANES:(f + 1) * LANES, :].T for f in range(3)]
    return [total[:, f * LANES:(f + 1) * LANES] for f in range(3)]


def split_lanes(cells):
    return jnp.concatenate(split2(cells), axis=1)


def emit(dims, field_ref, idx_ref, static_ref, outs, perm_refs=None, loads=()):
    gxa, gxb, gxp, yfa, yfb, table_ref = outs
    cx, cy, n_fault, n_exp = dims
    rows = cx * cy
    zeros = jnp.zeros((PACK, LANES), F32)
    for ref in (gxa, gxb, gxp):
        ref[0:PACK, :] = zeros
        ref[9:11, :] = static_ref[0:2, :]
    even_x, even_y = even_at("gx"), even_at("gy")
    base = PACK + 3 * n_exp

    def put_faces(out_a, out_b, at, low, high, even):
        count = low.shape[0]
        out_a[at:at + count, :] = jnp.where(even, high, low)
        out_b[at:at + count, :] = jnp.where(even, low, high)

    for f in range(3):
        if loads:
            loads[f].wait()
        put_faces(gxa, gxb, base + f * cy, field_ref[f, 0], field_ref[f, cx - 1], even_x)
        put_faces(yfa, yfb, f * cx, field_ref[f, :, 0, :], field_ref[f, :, cy - 1, :], even_y)
        high, low = split2(field_ref[f].reshape(rows, LANES).T)
        table_ref[f * LANES:(f + 1) * LANES, 0:rows] = high
        table_ref[f * LANES:(f + 1) * LANES, rows:2 * rows] = low
    if perm_refs is not None:
        for load in loads[3:]:
            load.wait()
        perm_x, perm_y = perm_refs
        put_faces(gxa, gxb, base + 3 * cy, perm_x[0], perm_x[1], even_x)
        put_faces(yfa, yfb, 3 * cx, perm_y[0, :, 0, :], perm_y[1, :, 7, :], even_y)

    def put(r, f, value):
        if r < n_fault + 6:
            plane, e = divmod(r - n_fault, 3)
            at = plane * PLANE + f * 3 + e
            for ref in (gxa, gxb, gxp):
                ref[at:at + 1, :] = value
        else:
            at = PACK + f * n_exp + r - n_fault - 6
            for ref in (gxa, gxb):
                ref[at:at + 1, :] = value

    gather_loop(table_ref, rows, False, idx_ref, n_fault * LANES, (n_fault + 6 + n_exp) * LANES, put)


def flat_row(v, buf):
    buf[...] = jnp.zeros(buf.shape, F32)
    buf[0:v.shape[0], 0:v.shape[1]] = v
    moved = pltpu.roll(buf[...], 0, 1, stride=v.shape[1], stride_axis=0)
    return jnp.sum(moved, axis=0, keepdims=True)


def first_kernel(dims, *refs):
    sources, outs, (idx, static) = refs[:9], refs[9:15], refs[15:17]
    targets, (perm_y, buf, sems) = refs[17:26], refs[26:]
    cx, cy, n_fault, n_exp = dims
    state, perm_x, cells, exports, perf, windex, wseg, bhp, target = targets
    state_hbm, perm_hbm = sources[:2]
    pairs = list(zip(sources[2:], targets[2:]))
    pairs += [(state_hbm.at[f], state.at[f]) for f in range(3)]
    pairs += [(perm_hbm.at[0, 0], perm_x.at[0]), (perm_hbm.at[0, cx - 1], perm_x.at[1])]
    pairs += [(perm_hbm.at[1, :, 0:8, :], perm_y.at[0]), (perm_hbm.at[1, :, cy - 8:cy, :], perm_y.at[1])]
    loads = [pltpu.make_async_copy(src, dst, sems.at[i]) for i, (src, dst) in enumerate(pairs)]
    for load in loads:
        load.start()
    for load in loads[:7]:
        load.wait()
    count = n_fault * LANES
    idx[:, 0:count] = cells[0]
    idx[:, count + 6 * LANES:] = exports[0]
    for e in range(3):
        flat = [flat_row(perf[0, 0, e, k].astype(F32) + 1.0, buf) for k in range(3)]
        rows = (flat[0] + roll_half(flat[1]), flat[2])
        for plane in range(2):
            at = count + (plane * 3 + e) * LANES
            idx[:, at:at + LANES] = (rows[plane] - 1.0).astype(jnp.int32)
    shape = windex.shape[2:]
    well = lax.broadcasted_iota(jnp.int32, shape, 0)

    def spread(ref):
        value = jnp.full(shape, ref[0, 0, 0])
        for w in range(1, shape[0]):
            value = jnp.where(well == w, ref[0, 0, w], value)
        return value

    live = (lax.broadcasted_iota(jnp.int32, shape, 1) < spread(wseg)).astype(F32)
    static[...] = jnp.zeros(static.shape, F32)
    static[0:1, :] = flat_row(live * windex[0, 0], buf) + roll_half(flat_row(spread(bhp), buf))
    static[1:2, :] = flat_row(live, buf) + roll_half(flat_row(spread(target), buf))
    emit(dims, state, idx, static, outs, (perm_x, perm_y), loads[7:])


def connection_kernel(dims, size_y, tiles, rows, trans, pidx, tr):
    _, _, n_fault, n_exp = dims
    tile = tiles[...]
    tile_x = jnp.floor((tile.astype(F32) + 0.5) * (1.0 / size_y)).astype(jnp.int32)
    tile_y = tile - tile_x * size_y
    across = tile_x - lax.axis_index("gx") + 1
    along = tile_y - lax.axis_index("gy") + 1
    pidx[...] = (across * 3 + along) * (n_exp * LANES) + rows[...]
    for r in range(n_fault):
        tr[r:r + 1, :] = trans[:, r * LANES:(r + 1) * LANES]


def gather_kernel(dims, table, idx, own):
    cx, cy, n_fault, _ = dims

    def put(r, f, value):
        own[f * n_fault + r:f * n_fault + r + 1, :] = value

    gather_loop(table, cx * cy, False, idx, 0, n_fault * LANES, put)


def choose_packets(axis, count, mine, rec_a, rec_b, far, pick):
    at = lax.axis_index(axis)
    even = even_at(axis)
    near = slice(0, PACK)
    a, b = rec_a[near, :], rec_b[near, :]
    if len(far) == 1:
        up_far = down_far = far[0][...]
    else:
        up = ((at >> 1) & 1) == 0
        c, d = far[0][...], far[1][...]
        up_far, down_far = jnp.where(up, c, d), jnp.where(up, d, c)
    pick[2] = mine[near, :]
    pick[3] = jnp.where(at + 1 < count, jnp.where(even, a, b), 0.0)
    pick[1] = jnp.where(at >= 1, jnp.where(even, b, a), 0.0)
    pick[4] = jnp.where(at + 2 < count, up_far, 0.0)
    pick[0] = jnp.where(at >= 2, down_far, 0.0)


def middle_kernel(dims, sizes, far_x, _, __, mine, rec_a, rec_b, *refs):
    _, _, _, n_exp = dims
    far = refs[:far_x]
    yfa, yfb, msg_a, msg_b, msg_c, pick = refs[far_x:]
    even = even_at("gx")
    choose_packets("gx", sizes[0], mine, rec_a, rec_b, far, pick)
    outs = (msg_a, msg_b, msg_c)
    for ref in outs:
        ref[0:PACK, :] = jnp.zeros((PACK, LANES), F32)
    for hx in range(3):
        for plane in range(2):
            for f in range(3):
                at = plane * PLANE + f * 3
                row = (
                    pick[hx, at + 2:at + 3, :]
                    + pick[hx + 1, at + 1:at + 2, :]
                    + pick[hx + 2, at:at + 1, :]
                )
                for ref in outs:
                    ref[at + hx:at + hx + 1, :] = row
        for ref in outs:
            ref[9 + hx:10 + hx, :] = pick[hx + 1, 9:10, :]
            ref[12 + hx:13 + hx, :] = pick[hx + 1, 10:11, :]
    rows = 3 * n_exp
    src = slice(PACK, PACK + rows)
    stack = (
        jnp.where(even, rec_b[src, :], rec_a[src, :]),
        mine[src, :],
        jnp.where(even, rec_a[src, :], rec_b[src, :]),
    )
    for hx in range(3):
        at = PACK + hx * rows
        msg_a[at:at + rows, :] = stack[hx]
        msg_b[at:at + rows, :] = stack[hx]
    at = PACK + 3 * rows
    msg_a[at:at + yfa.shape[0], :] = yfa[...]
    msg_b[at:at + yfb.shape[0], :] = yfb[...]


def roll_half(x):
    return pltpu.roll(x, LANES // 2, 1)


def low_half(shape):
    return lax.broadcasted_iota(jnp.int32, shape, 1) < LANES // 2


def segment_values(packs, seg_ref):
    tops = [packs[y, 0:PLANE, :] for y in range(5)]
    bottoms = [packs[y, PLANE:PACK, :] for y in range(5)]
    lo = low_half((PLANE, LANES))

    def home(hy):
        return tops[hy + 3] + roll_half(tops[hy + 2]) + bottoms[hy + 1]

    plane0 = jnp.where(lo, home(-1), roll_half(home(0)))
    plane1 = jnp.where(lo, home(1), 0.0)
    for f in range(3):
        seg_ref[f * 8:f * 8 + 3, :] = plane0[f * 3:f * 3 + 3, :]
        seg_ref[f * 8 + 3:f * 8 + 6, :] = plane1[f * 3:f * 3 + 3, :]
        seg_ref[f * 8 + 6:f * 8 + 8, :] = jnp.zeros((2, LANES), F32)


def well_constants(packs, const_ref):
    tops = [packs[y, 0:PLANE, :] for y in (1, 2, 3)]
    rolled = [roll_half(t) for t in tops]
    lo = low_half((PLANE, LANES))
    same0 = jnp.where(lo, tops[0], rolled[1])
    same1 = jnp.where(lo, tops[2], 0.0)
    other0 = jnp.where(lo, rolled[0], tops[1])
    other1 = rolled[2]
    const_ref[...] = jnp.zeros(const_ref.shape, F32)
    for at, (a, b), src in ((0, (same0, same1), 9), (8, (other0, other1), 9), (16, (same0, same1), 12)):
        const_ref[at:at + 3, :] = a[src:src + 3, :]
        const_ref[at + 3:at + 6, :] = b[src:src + 3, :]


def running_sum(x):
    lane = lax.broadcasted_iota(jnp.int32, x.shape, 1) & 15
    for shift in (1, 2, 4, 8):
        x = x + jnp.where(lane >= shift, pltpu.roll(x, shift, 1), 0.0)
    return x


def well_mix(seg_ref):
    field = tuple(seg_ref[f * 8:f * 8 + 8, :] for f in range(3))
    sats, factors = props(field)
    mob = mobilities(sats, factors)
    total = mob[0] + mob[1] + mob[2]
    mix = (mob[0] * DENSITY[0] + mob[1] * DENSITY[1] + mob[2] * DENSITY[2]) / total
    return field, sats, factors, mob, total, mix


def well_rates(seg_ref, const_ref):
    weight, bhp, live = (const_ref[i * 8:i * 8 + 8, :] for i in range(3))
    field, _, _, mob, _, mix = well_mix(seg_ref)
    press = bhp + HEAD_SCALE * running_sum(live * mix)
    return [weight * mob[a] * (field[0] - press) for a in range(3)]


def well_rate_tangents(seg_ref, dseg_ref, const_ref):
    weight, bhp, live = (const_ref[i * 8:i * 8 + 8, :] for i in range(3))
    field, sats, factors, mob, total, mix = well_mix(seg_ref)
    press = bhp + HEAD_SCALE * running_sum(live * mix)
    dfield = tuple(dseg_ref[f * 8:f * 8 + 8, :] for f in range(3))
    _, dmob = tangents(sats, factors, mob, dfield)
    dtotal = dmob[0] + dmob[1] + dmob[2]
    dnum = dmob[0] * DENSITY[0] + dmob[1] * DENSITY[1] + dmob[2] * DENSITY[2]
    dpress = HEAD_SCALE * running_sum(live * ((dnum - mix * dtotal) / total))
    return [
        weight * (dmob[a] * (field[0] - press) + mob[a] * (dfield[0] - dpress)) for a in range(3)
    ]


def stack_partners(dims, mine, rec_a, rec_b, partner):
    _, _, _, n_exp = dims
    even = even_at("gy")
    used = 9 * n_exp
    for f in range(3):
        for hx in range(3):
            at = PACK + hx * 3 * n_exp + f * n_exp
            src = slice(at, at + n_exp)
            first, second = rec_a[src, :], rec_b[src, :]
            blocks = (jnp.where(even, second, first), mine[src, :], jnp.where(even, first, second))
            for hy in range(3):
                to = (hx * 3 + hy) * n_exp
                partner[f, to:to + n_exp, :] = blocks[hy]
        if used < partner.shape[1]:
            partner[f, used:, :] = jnp.zeros((partner.shape[1] - used, LANES), F32)


def pick_partners(dims, partner, pidx, table, out):
    _, _, n_fault, _ = dims
    count = partner.shape[1]
    table[...] = split_lanes(partner[...].reshape(3 * count, LANES))

    def put(r, f, value):
        out[f * n_fault + r:f * n_fault + r + 1, :] = value

    gather_loop(table, count, True, pidx, 0, n_fault * LANES, put)


def halo(axis, rec_a, rec_b, at, count):
    even = even_at(axis)
    a, b = rec_a[at:at + count, :], rec_b[at:at + count, :]
    return jnp.where(even, b, a), jnp.where(even, a, b)


def halo_part(dims, axis, rec_a, rec_b, part):
    cx, cy, _, n_exp = dims
    at, count = (PACK + 3 * n_exp, cy) if axis == "gx" else (PACK + 9 * n_exp, cx)
    return halo(axis, rec_a, rec_b, at + part * count, count)


def halo_fields(dims, axis, rec_a, rec_b):
    parts = [halo_part(dims, axis, rec_a, rec_b, f) for f in range(3)]
    return [tuple(v[side] for v in parts) for side in range(2)]


def outermost(dims, axis, ref):
    cx, cy, _, _ = dims
    if axis == "gx":
        return [tuple(ref[f, 0] for f in range(3)), tuple(ref[f, cx - 1] for f in range(3))]
    return [tuple(ref[f, :, 0, :] for f in range(3)), tuple(ref[f, :, cy - 1, :] for f in range(3))]


def edge_fluxes(dims, axis, trans, field, rec_a, rec_b):
    far, near = halo_fields(dims, axis, rec_a, rec_b), outermost(dims, axis, field)
    return [
        face(trans[k], low[0], mob_of(low), high[0], mob_of(high))
        for k, (low, high) in enumerate(((far[0], near[0]), (near[1], far[1])))
    ]


def edge_tangents(dims, axis, trans, field, direction, rec_a, rec_b, drec_a, drec_b):
    far, near = halo_fields(dims, axis, rec_a, rec_b), outermost(dims, axis, field)
    dfar, dnear = halo_fields(dims, axis, drec_a, drec_b), outermost(dims, axis, direction)
    there = [point(far[k], dfar[k]) for k in range(2)]
    here = [point(near[k], dnear[k]) for k in range(2)]
    return [between(trans[0], there[0], here[0]), between(trans[1], here[1], there[1])]


def residual_edge_kernel(dims, size, make, field, gx_a, gx_b, trans, fluxes, *out):
    if make:
        low, high = halo_part(dims, "gx", gx_a, gx_b, 3)
        outer_trans("gx", size, trans, low, high, out[0])
        trans = out[0]
    for k, flux in enumerate(edge_fluxes(dims, "gx", trans, field, gx_a, gx_b)):
        for a in range(3):
            fluxes[k, a] = flux[a]


def jacobian_edge_kernel(dims, field, direction, trans, gx_a, gx_b, dgx_a, dgx_b, fluxes):
    for k, flux in enumerate(edge_tangents(dims, "gx", trans, field, direction, gx_a, gx_b, dgx_a, dgx_b)):
        for a in range(3):
            fluxes[k, a] = flux[a]


def edge_trans(t_a, t_b):
    return 2.0 * t_a * t_b / (t_a + t_b)


def inner_trans(dims, perm, fx, fy, fz, edge_x, edge_y):
    cx, cy, _, _ = dims
    last_row = lax.broadcasted_iota(jnp.int32, (cy, LANES), 0) == cy - 1
    last_lane = lax.broadcasted_iota(jnp.int32, (cy, LANES), 1) == LANES - 1
    for x in range(cx):
        if x + 1 < cx:
            fx[x] = edge_trans(perm[0, x], perm[0, x + 1])
        t = perm[1, x]
        fy[x] = jnp.where(last_row, 0.0, edge_trans(t, pltpu.roll(t, cy - 1, 0)))
        t = perm[2, x]
        fz[x] = jnp.where(last_lane, 0.0, edge_trans(t, pltpu.roll(t, LANES - 1, 1)))
    edge_x[0], edge_x[1] = perm[0, 0], perm[0, cx - 1]
    edge_y[0], edge_y[1] = perm[1, :, 0, :], perm[1, :, cy - 1, :]


def outer_trans(axis, count, edge, low, high, out):
    at = lax.axis_index(axis)
    out[0] = jnp.where(at > 0, edge_trans(low, edge[0]), 0.0)
    out[1] = jnp.where(at < count - 1, edge_trans(edge[1], high), 0.0)


def mob_of(field):
    return mobilities(*props(field))


def residual_planes(dims, field, pore, fx, fy, fz, acc):
    cx, cy, _, _ = dims

    def plane(x):
        fld = tuple(field[f, x] for f in range(3))
        sats, factors = props(fld)
        return fld[0], mobilities(sats, factors), sats, factors

    cur, below = plane(0), None
    for x in range(cx):
        p, mob, sats, factors = cur
        row = lambda v: pltpu.roll(v, cy - 1, 0)
        lane = lambda v: pltpu.roll(v, LANES - 1, 1)
        y_up = face(fy[x], p, mob, row(p), [row(m) for m in mob])
        z_up = face(fz[x], p, mob, lane(p), [lane(m) for m in mob], 1.0)
        nxt = above = None
        if x + 1 < cx:
            nxt = plane(x + 1)
            above = face(fx[x], p, mob, nxt[0], nxt[1])
        for a in range(3):
            inflow = (y_up[a] - pltpu.roll(y_up[a], 1, 0)) + (z_up[a] - pltpu.roll(z_up[a], 1, 1))
            if above is not None:
                inflow = inflow + above[a]
            if below is not None:
                inflow = inflow - below[a]
            acc[a, x] = pore[x] * (factors[a] * sats[a]) - inflow
        cur, below = nxt, above


def point(field, dfield):
    sats, factors = props(field)
    mob = mobilities(sats, factors)
    dsats, dmob = tangents(sats, factors, mob, dfield)
    return field[0], mob, dfield[0], dmob, sats, factors, dsats


def between(trans, c, n, depth=0.0):
    return face_tangent(trans, c[0], c[1], n[0], n[1], c[2], c[3], n[2], n[3], depth)


def jacobian_planes(dims, field, dfield, pore, fx, fy, fz, acc):
    cx, cy, _, _ = dims

    def plane(x):
        return point(tuple(field[f, x] for f in range(3)), tuple(dfield[f, x] for f in range(3)))

    def moved(c, shift):
        return shift(c[0]), [shift(m) for m in c[1]], shift(c[2]), [shift(m) for m in c[3]]

    cur, below = plane(0), None
    for x in range(cx):
        y_up = between(fy[x], cur, moved(cur, lambda v: pltpu.roll(v, cy - 1, 0)))
        z_up = between(fz[x], cur, moved(cur, lambda v: pltpu.roll(v, LANES - 1, 1)), 1.0)
        nxt = above = None
        if x + 1 < cx:
            nxt = plane(x + 1)
            above = between(fx[x], cur, nxt)
        _, _, dp, _, sats, factors, dsats = cur
        for a in range(3):
            inflow = (y_up[a] - pltpu.roll(y_up[a], 1, 0)) + (z_up[a] - pltpu.roll(z_up[a], 1, 1))
            if above is not None:
                inflow = inflow + above[a]
            if below is not None:
                inflow = inflow - below[a]
            gain = pore[x] * (factors[a] * (dsats[a] + COMPRESS[a] * sats[a] * dp))
            acc[a, x] = gain - inflow
        cur, below = nxt, above


def add_outer(dims, x_fluxes, y_fluxes, acc):
    cx, cy, _, _ = dims
    for a in range(3):
        acc[a, 0] = acc[a, 0] + x_fluxes[0, a]
        acc[a, cx - 1] = acc[a, cx - 1] - x_fluxes[1, a]
        acc[a, :, 0, :] = acc[a, :, 0, :] + y_fluxes[0][a]
        acc[a, :, cy - 1, :] = acc[a, :, cy - 1, :] - y_fluxes[1][a]


def residual_inner_kernel(dims, make, field, pore, *refs):
    if make:
        perm, acc, fx, fy, fz, edge_x, edge_y = refs
        inner_trans(dims, perm, fx, fy, fz, edge_x, edge_y)
    else:
        fx, fy, fz, acc = refs
    residual_planes(dims, field, pore, fx, fy, fz, acc)


def jacobian_inner_kernel(dims, field, direction, pore, fx, fy, fz, acc):
    jacobian_planes(dims, field, direction, pore, fx, fy, fz, acc)


def rows_of(ref, count):
    return tuple(ref[f * count:(f + 1) * count, :] for f in range(3))


def finish_faults(dims, inner, old_mass, flux, idx, values, x_fluxes, y_fluxes, acc):
    cx, cy, n_fault, _ = dims
    for a in range(3):
        values[a, 0:n_fault, :] = -flux[a]
    total = scatter_loop(values, idx, 0, n_fault * LANES, cx * cy, True)
    for a in range(3):
        part = inner[a] + total[a].reshape(cx, cy, LANES)
        acc[a] = part if old_mass is None else part - old_mass[a]
    add_outer(dims, x_fluxes, y_fluxes, acc)


def residual_fault_kernel(dims, size, make, *refs):
    _, _, n_fault, _ = dims
    inner, old_mass, field, idx, pidx, tr, own, x_fluxes, mine, gy_a, gy_b, trans, acc, partner_vals = refs[:14]
    if make:
        low, high = halo_part(dims, "gy", gy_a, gy_b, 3)
        outer_trans("gy", size, trans, low, high, refs[14])
        trans = refs[14]
    partner, values, ptable = refs[-3:]
    stack_partners(dims, mine, gy_a, gy_b, partner)
    pick_partners(dims, partner, pidx, ptable, partner_vals)
    mine_f, other_f = rows_of(own, n_fault), rows_of(partner_vals, n_fault)
    flux = face(tr[...], mine_f[0], mob_of(mine_f), other_f[0], mob_of(other_f))
    y_fluxes = edge_fluxes(dims, "gy", trans, field, gy_a, gy_b)
    finish_faults(dims, inner, old_mass, flux, idx, values, x_fluxes, y_fluxes, acc)


def jacobian_fault_kernel(dims, *refs):
    _, _, n_fault, _ = dims
    inner, field, direction, idx, pidx, tr, own, other, down, trans, x_fluxes = refs[:11]
    gy_a, gy_b, mine, dgy_a, dgy_b, acc, partner, values, ptable, dother = refs[11:]
    stack_partners(dims, mine, dgy_a, dgy_b, partner)
    pick_partners(dims, partner, pidx, ptable, dother)
    flux = between(
        tr[...],
        point(rows_of(own, n_fault), rows_of(down, n_fault)),
        point(rows_of(other, n_fault), rows_of(dother, n_fault)),
    )
    y_fluxes = edge_tangents(dims, "gy", trans, field, direction, gy_a, gy_b, dgy_a, dgy_b)
    finish_faults(dims, inner, None, flux, idx, values, x_fluxes, y_fluxes, acc)


def well_sums(dims, rates, idx, values, turned):
    cx, cy, n_fault, _ = dims
    for a in range(3):
        values[a] = rates[a]
    start = n_fault * LANES
    total = scatter_loop(values, idx, start, start + 6 * LANES, cx * cy, turned)
    return [part.reshape(cx, cy, LANES) for part in total]


def residual_kernel(dims, sizes, final, far_y, *refs):
    refs = list(refs)
    take = lambda n: [refs.pop(0) for _ in range(n)]
    partial, scaling, idx, static = take(4)
    mine, gy_a, gy_b = take(3)
    far = take(far_y)
    direction, seg, const = take(3)
    outs = take(6)
    if final:
        residual, well = take(2)
    packs, values = take(2)
    choose_packets("gy", sizes[1], mine, gy_a, gy_b, far, packs)
    segment_values(packs, seg)
    well_constants(packs, const)
    rates = well_rates(seg, const)
    if final:
        done = running_sum(rates[0] + rates[1] + rates[2])[1:2, :]
        value = done / packs[2, 13:14, :] - 1.0
        lane = lax.broadcasted_iota(jnp.int32, value.shape, 1)
        column = lax.broadcasted_iota(jnp.int32, well.shape, 2)
        count = well.shape[2]
        result = jnp.zeros(well.shape, F32)
        for w in range(count):
            last = LANES // 2 + (w + 1) * (LANES // 2 // count) - 1
            result = jnp.where(column == w, jnp.sum(jnp.where(lane == last, value, 0.0)), result)
        well[...] = result
    sums = well_sums(dims, rates, idx, values, False)
    for a in range(3):
        res = partial[a] + sums[a]
        if final:
            residual[a] = res
        direction[a] = scaling[a] * res
    emit(dims, direction, idx, static, outs)


def jacobian_kernel(dims, sizes, final, far_y, *refs):
    refs = list(refs)
    take = lambda n: [refs.pop(0) for _ in range(n)]
    partial, field, direction, scaling, idx, static, seg, const = take(8)
    mine, dgy_a, dgy_b = take(3)
    far = take(far_y)
    (result,) = take(1)
    outs = None if final else take(6)
    packs, values, dseg = take(3)
    choose_packets("gy", sizes[1], mine, dgy_a, dgy_b, far, packs)
    segment_values(packs, dseg)
    sums = well_sums(dims, well_rate_tangents(seg, dseg, const), idx, values, final)
    for a in range(3):
        step = 2.0 * direction[a] - scaling[a] * (partial[a] + sums[a])
        result[a] = step if final else field[a] - step
    if not final:
        emit(dims, result, idx, static, outs)


def exchange_pairs(axis, kind, size_x, size_y):
    def partner(i, count):
        step = 1 if kind < 2 else 2
        shift = step if kind % 2 else 0
        if shift and not shift <= i < count - shift:
            return None
        return ((i + shift) ^ step) - shift

    out = []
    for i in range(size_x):
        for j in range(size_y):
            if axis == 0:
                got = partner(i, size_x)
                far = (got, j) if got is not None else ((i, j ^ 1) if kind < 2 else (i ^ 1, j))
            else:
                got = partner(j, size_y)
                far = (i, got) if got is not None else ((i ^ 1, j) if kind < 2 else (i, j ^ 1))
            out.append((i * size_y + j, far[0] * size_y + far[1]))
    return out


def body(
    state, perm, pore, old_mass, scaling, fault_cell, fault_tile, fault_row, fault_trans,
    fault_export, perf_cell, well_segments, well_index, bhp, target,
):
    size_x, size_y = lax.axis_size("gx"), lax.axis_size("gy")
    _, cx, cy, _ = state.shape
    wells, segs = well_index.shape[2:]
    n_fault, n_exp = fault_cell.shape[-1] // LANES, fault_export.shape[-1] // LANES
    dims = (cx, cy, n_fault, n_exp)
    far_x = 1 if size_x == 4 else 2
    far_y = 1 if size_y == 4 else 2
    params = pltpu.CompilerParams(vmem_limit_bytes=VMEM_BYTES)
    anywhere = pl.BlockSpec(memory_space=pl.ANY)
    hbm = pl.BlockSpec(memory_space=pltpu.HBM)
    vmem = pl.BlockSpec(memory_space=pltpu.VMEM)
    shape = lambda *dims_: jax.ShapeDtypeStruct(dims_, F32)
    rows = cx * cy
    gx_rows = PACK + 3 * n_exp + 3 * cy
    gy_rows = PACK + 9 * n_exp + 3 * cx
    table = jax.ShapeDtypeStruct((3 * LANES, 2 * rows), BF16)
    near_rows = -(-9 * n_exp // 16) * 16

    def call(kernel, args, outs, scratch=(), specs=None):
        return pl.pallas_call(
            kernel,
            out_shape=outs,
            in_specs=specs or [vmem] * len(args),
            out_specs=[vmem] * len(outs),
            scratch_shapes=scratch,
            compiler_params=params,
        )(*args)

    def message_shapes(first):
        more_x, more_y = (cy, cx) if first else (0, 0)
        return [
            shape(gx_rows + more_x, LANES), shape(gx_rows + more_x, LANES), shape(PACK, LANES),
            shape(3 * cx + more_y, LANES), shape(3 * cx + more_y, LANES), table,
        ]

    def send(value, axis, kind):
        return lax.ppermute(value, ("gx", "gy"), exchange_pairs(axis, kind, size_x, size_y))

    def send_x(messages):
        msg_a, msg_b, packet = messages[:3]
        far = [send(packet, 0, 2 + k) for k in range(far_x)]
        rec_b = send(msg_b, 0, 1)
        rec_a = send(msg_a, 0, 0)
        return rec_a, rec_b, far

    def send_y(messages, got, after):
        msg_a, _, _, yfa, yfb, _ = messages
        rec_a, rec_b, far = got
        total = PACK + 9 * n_exp + yfa.shape[0]
        mid_a, mid_b, mid_c = call(
            functools.partial(middle_kernel, dims, sizes, far_x),
            [*after, msg_a, rec_a, rec_b, *far, yfa, yfb],
            [shape(total, LANES), shape(total, LANES), shape(PACK, LANES)],
            [pltpu.VMEM((5, PACK, LANES), F32)],
            [anywhere] * 2 + [vmem] * (5 + far_x),
        )
        got_b = send(mid_b, 1, 1)
        got_a = send(mid_a, 1, 0)
        got_far = [send(mid_c, 1, 2 + k) for k in range(far_y)]
        return (mid_a, got_a, got_b), got_far

    sizes = (size_x, size_y)
    grid = shape(3, cx, cy, LANES)
    wide_rows = shape(3 * n_fault, LANES)
    small = shape(24, LANES)
    packs = pltpu.VMEM((5, PACK, LANES), F32)
    fault_work = [
        pltpu.VMEM((3, near_rows, LANES), F32), pltpu.VMEM((3, n_fault, LANES), F32),
        pltpu.VMEM((3 * near_rows, 2 * LANES), BF16),
    ]
    well_work = [packs, pltpu.VMEM((3, 8, LANES), F32)]
    columns = (n_fault + 6 + n_exp) * LANES

    sources = [state, perm, fault_cell, fault_export, perf_cell, well_index, well_segments, bhp, target]
    results = call(
        functools.partial(first_kernel, dims),
        [pltpu.with_memory_space_constraint(v, pltpu.HBM) for v in sources],
        message_shapes(True) + [jax.ShapeDtypeStruct((1, columns), jnp.int32), shape(8, LANES), shape(*state.shape)],
        [pltpu.VMEM((2, cy, LANES), F32)]
        + [(pltpu.VMEM if i < 4 else pltpu.SMEM)(v.shape, v.dtype) for i, v in enumerate(sources[2:])]
        + [pltpu.VMEM((2, cx, 8, LANES), F32), pltpu.VMEM((8, LANES), F32), pltpu.SemaphoreType.DMA((14,))],
        [hbm] * len(sources),
    )
    messages, (idx, static, current) = results[:6], results[6:]

    def own_cells(cells_table):
        return call(functools.partial(gather_kernel, dims), [cells_table, idx], [wide_rows])[0]

    for step in range(2):
        final = step == 1
        got = send_x(messages)
        gx_got = got[:2]
        if final:
            (inner,) = call(
                functools.partial(residual_inner_kernel, dims, False), [current, pore, *trans], [grid]
            )
        else:
            inner, *trans, edge_x, edge_y = call(
                functools.partial(residual_inner_kernel, dims, True), [current, pore, perm],
                [grid, shape(cx, cy, LANES), shape(cx, cy, LANES), shape(cx, cy, LANES),
                 shape(2, cy, LANES), shape(2, cx, LANES)],
            )
            pidx, tr = call(
                functools.partial(connection_kernel, dims, size_y),
                [fault_tile.reshape(1, -1), fault_row.reshape(1, -1), fault_trans.reshape(1, -1)],
                [jax.ShapeDtypeStruct((1, n_fault * LANES), jnp.int32), shape(n_fault, LANES)],
            )
        own = own_cells(messages[5])
        gy_got, gy_far = send_y(messages, got, (inner, own))
        edge_shape = shape(2, 3, cy, LANES)
        results = call(
            functools.partial(residual_edge_kernel, dims, size_x, not final),
            [current, *gx_got, outer_x if final else edge_x],
            [edge_shape] + ([] if final else [shape(2, cy, LANES)]),
        )
        x_fluxes = results[0]
        if not final:
            outer_x = results[1]
        results = call(
            functools.partial(residual_fault_kernel, dims, size_y, not final),
            [inner, old_mass, current, idx, pidx, tr, own, x_fluxes, *gy_got, outer_y if final else edge_y],
            [grid, wide_rows] + ([] if final else [shape(2, cx, LANES)]),
            fault_work,
        )
        partial, other = results[:2]
        if not final:
            outer_y = results[2]
        results = call(
            functools.partial(residual_kernel, dims, sizes, final, far_y),
            [partial, scaling, idx, static, *gy_got, *gy_far],
            [grid, small, small] + message_shapes(False) + ([grid, shape(1, 1, wells)] if final else []),
            well_work,
        )
        direction, seg, const = results[:3]
        messages = results[3:9]
        if final:
            residual, well = results[9:]
        got = send_x(messages)
        (inner,) = call(
            functools.partial(jacobian_inner_kernel, dims), [current, direction, pore, *trans], [grid]
        )
        down = own_cells(messages[5])
        dgy_got, dgy_far = send_y(messages, got, (inner, down))
        (x_fluxes,) = call(
            functools.partial(jacobian_edge_kernel, dims),
            [current, direction, outer_x, *gx_got, *got[:2]],
            [edge_shape],
        )
        (partial,) = call(
            functools.partial(jacobian_fault_kernel, dims),
            [inner, current, direction, idx, pidx, tr, own, other, down, outer_y, x_fluxes, *gy_got[1:], *dgy_got],
            [grid],
            fault_work + [pltpu.VMEM((3 * n_fault, LANES), F32)],
        )
        results = call(
            functools.partial(jacobian_kernel, dims, sizes, final, far_y),
            [partial, current, direction, scaling, idx, static, seg, const, *dgy_got, *dgy_far],
            [grid] + ([] if final else message_shapes(False)),
            well_work + [pltpu.VMEM((24, LANES), F32)],
        )
        current, messages = results[0], results[1:]
    return residual, current, well


def solution(mesh):
    grid = P(None, "gx", "gy", None)
    tile = P("gx", "gy", None)
    return jax.shard_map(
        body,
        mesh=mesh,
        in_specs=(
            grid, grid, tile, grid, grid, tile, tile, tile, tile, tile,
            P("gx", "gy", None, None, None, None), tile, P("gx", "gy", None, None), tile, tile,
        ),
        out_specs=(grid, grid, tile),
        check_vma=False,
    )
```

```python
import functools

import jax
import jax.numpy as jnp
from jax import lax
from jax.experimental import pallas as pl
from jax.experimental.pallas import tpu as pltpu
from jax.sharding import PartitionSpec as P

VISCOSITY = (0.5, 2.0, 0.1)
COMPRESS = (0.02, 0.05, 0.3)
DENSITY = (1.0, 0.8, 0.2)
GRAVITY = 0.2
INV_SMOOTHING = 10.0
HEAD_SCALE = 0.3

LANES = 128
PACK = 32
PLANE = 16
VMEM_BYTES = 40 * 1024 * 1024
F32 = jnp.float32
BF16 = jnp.bfloat16


def props(field):
    p, sw, sg = field
    sats = (sw, 1.0 - sw - sg, sg)
    factors = tuple(jnp.exp(COMPRESS[a] * p) for a in range(3))
    return sats, factors


def mobilities(sats, factors):
    return tuple(sats[a] * sats[a] * factors[a] * (1.0 / VISCOSITY[a]) for a in range(3))


def tangents(sats, factors, mob, dfield):
    dp, dsw, dsg = dfield
    dsats = (dsw, -(dsw + dsg), dsg)
    dmob = tuple(
        mob[a] * (COMPRESS[a] * dp) + sats[a] * factors[a] * (2.0 / VISCOSITY[a]) * dsats[a]
        for a in range(3)
    )
    return dsats, dmob


def face(trans, p_c, mob_c, p_n, mob_n, depth=0.0):
    out = []
    diff = p_n - p_c
    for a in range(3):
        if a == 0 or depth:
            pot = diff - GRAVITY * DENSITY[a] * depth if depth else diff
            weight = jax.nn.sigmoid(pot * INV_SMOOTHING)
            scaled = trans * pot
        out.append(scaled * (mob_c[a] + weight * (mob_n[a] - mob_c[a])))
    return out


def face_tangent(trans, p_c, mob_c, p_n, mob_n, dp_c, dmob_c, dp_n, dmob_n, depth=0.0):
    out = []
    diff = p_n - p_c
    ddiff = dp_n - dp_c
    for a in range(3):
        if a == 0 or depth:
            pot = diff - GRAVITY * DENSITY[a] * depth if depth else diff
            weight = jax.nn.sigmoid(pot * INV_SMOOTHING)
            dweight = (weight * (1.0 - weight)) * (ddiff * INV_SMOOTHING)
        step = mob_n[a] - mob_c[a]
        mean = mob_c[a] + weight * step
        dmean = dmob_c[a] + weight * (dmob_n[a] - dmob_c[a]) + dweight * step
        out.append(trans * (mean * ddiff + pot * dmean))
    return out


def split2(x):
    high = x.astype(BF16)
    return high, (x - high.astype(F32)).astype(BF16)


def one_hot(place, count):
    at = lax.broadcasted_iota(jnp.int32, (count, place.shape[1]), 0).astype(F32).astype(BF16)
    return jnp.where(at == place.astype(F32).astype(BF16), jnp.ones((), BF16), jnp.zeros((), BF16))


def even_at(axis):
    return (lax.axis_index(axis) & 1) == 0


def gather_loop(table, count, by_lane, idx_ref, start, columns, put):
    kept = count if by_lane else LANES
    for c in range(start, columns, 256):
        width = min(256, columns - c)
        idx = idx_ref[:, c:c + width]
        row, lane = idx >> 7, idx & (LANES - 1)
        hot = one_hot(lane, LANES) if by_lane else one_hot(row, count)
        picked = jnp.dot(table[...], jnp.concatenate([hot, hot], axis=0), preferred_element_type=F32)
        rest = row if by_lane else lane
        for h in range(width // LANES):
            cols = slice(h * LANES, (h + 1) * LANES)
            mask = lax.broadcasted_iota(jnp.int32, (kept, LANES), 0) == rest[:, cols]
            for f in range(3):
                block = picked[f * kept:(f + 1) * kept, cols]
                value = jnp.sum(jnp.where(mask, block, 0.0), axis=0, keepdims=True)
                put(c // LANES + h, f, value)


def scatter_loop(values_ref, idx_ref, start, columns, count, turned):
    total = jnp.zeros((3 * LANES, count) if turned else (count, 3 * LANES), F32)
    for c in range(start, columns, 256):
        width = min(256, columns - c)
        idx = idx_ref[:, c:c + width]
        hot = one_hot(idx >> 7, count)
        lane = (idx & (LANES - 1)).astype(F32).astype(BF16)
        at = lax.broadcasted_iota(jnp.int32, (LANES, width), 0).astype(F32).astype(BF16)
        mask = at == lane
        highs, lows = [], []
        for f in range(3):
            r = (c - start) // LANES
            row = jnp.concatenate(
                [values_ref[f, r + h:r + h + 1, :] for h in range(width // LANES)], axis=1
            )
            high, low = split2(row)
            highs.append(jnp.where(mask, high, jnp.zeros((), BF16)))
            lows.append(jnp.where(mask, low, jnp.zeros((), BF16)))
        right = jnp.concatenate(
            [jnp.concatenate(highs, axis=0), jnp.concatenate(lows, axis=0)], axis=1
        )
        left = jnp.concatenate([hot, hot], axis=1)
        total = total + lax.dot_general(
            *((right, left) if turned else (left, right)), (((1,), (1,)), ((), ())), preferred_element_type=F32
        )
    if turned:
        return [total[f * LANES:(f + 1) * LANES, :].T for f in range(3)]
    return [total[:, f * LANES:(f + 1) * LANES] for f in range(3)]


def split_lanes(cells):
    return jnp.concatenate(split2(cells), axis=1)


def emit(dims, field_ref, idx_ref, static_ref, outs, perm_refs=None, loads=(), parts=0):
    gxa, gxb, gxp, yfa, yfb, table_ref = outs
    cx, cy, n_fault, n_exp = dims
    rows = cx * cy
    zeros = jnp.zeros((PACK, LANES), F32)
    for ref in (gxa, gxb, gxp):
        ref[0:PACK, :] = zeros
        ref[9:11, :] = static_ref[0:2, :]
    even_x, even_y = even_at("gx"), even_at("gy")
    base = PACK + 3 * n_exp

    def put_faces(out_a, out_b, at, low, high, even):
        count = low.shape[0]
        out_a[at:at + count, :] = jnp.where(even, high, low)
        out_b[at:at + count, :] = jnp.where(even, low, high)

    for f in range(3):
        for load in loads[f * parts:(f + 1) * parts]:
            load.wait()
        put_faces(gxa, gxb, base + f * cy, field_ref[f, 0], field_ref[f, cx - 1], even_x)
        put_faces(yfa, yfb, f * cx, field_ref[f, :, 0, :], field_ref[f, :, cy - 1, :], even_y)
        high, low = split2(field_ref[f].reshape(rows, LANES).T)
        table_ref[f * LANES:(f + 1) * LANES, 0:rows] = high
        table_ref[f * LANES:(f + 1) * LANES, rows:2 * rows] = low
    if perm_refs is not None:
        for load in loads[3 * parts:]:
            load.wait()
        perm_x, perm_y = perm_refs
        put_faces(gxa, gxb, base + 3 * cy, perm_x[0], perm_x[1], even_x)
        put_faces(yfa, yfb, 3 * cx, perm_y[0, :, 0, :], perm_y[1, :, 7, :], even_y)

    def put(r, f, value):
        if r < n_fault + 6:
            plane, e = divmod(r - n_fault, 3)
            at = plane * PLANE + f * 3 + e
            for ref in (gxa, gxb, gxp):
                ref[at:at + 1, :] = value
        else:
            at = PACK + f * n_exp + r - n_fault - 6
            for ref in (gxa, gxb):
                ref[at:at + 1, :] = value

    gather_loop(table_ref, rows, False, idx_ref, n_fault * LANES, (n_fault + 6 + n_exp) * LANES, put)


def flat_rows(blocks, buf):
    rows, width = blocks[0].shape
    buf[...] = jnp.zeros(buf.shape, F32)
    for i, block in enumerate(blocks):
        buf[8 * i:8 * i + rows, 0:width] = block
    moved = pltpu.roll(buf[...], 0, 1, stride=width, stride_axis=0)
    return [jnp.sum(moved[8 * i:8 * i + 8, :], axis=0, keepdims=True) for i in range(len(blocks))]


def first_kernel(dims, *refs):
    sources, outs, (idx, static) = refs[:9], refs[9:15], refs[15:17]
    targets, (perm_y, buf, sems) = refs[17:26], refs[26:]
    cx, cy, n_fault, n_exp = dims
    state, perm_x, cells, exports, perf, windex, wseg, bhp, target = targets
    state_hbm, perm_hbm = sources[:2]
    pairs = list(zip(sources[2:], targets[2:]))
    parts = [slice(x, x + 2) for x in range(0, cx, 2)]
    pairs += [(state_hbm.at[f, part], state.at[f, part]) for f in range(3) for part in parts]
    pairs += [(perm_hbm.at[0, 0], perm_x.at[0]), (perm_hbm.at[0, cx - 1], perm_x.at[1])]
    pairs += [(perm_hbm.at[1, :, 0:8, :], perm_y.at[0]), (perm_hbm.at[1, :, cy - 8:cy, :], perm_y.at[1])]
    loads = [pltpu.make_async_copy(src, dst, sems.at[i]) for i, (src, dst) in enumerate(pairs)]
    for load in loads:
        load.start()
    for load in loads[:7]:
        load.wait()
    count = n_fault * LANES
    idx[:, 0:count] = cells[0]
    idx[:, count + 6 * LANES:] = exports[0]
    shape = windex.shape[2:]
    well = lax.broadcasted_iota(jnp.int32, shape, 0)

    def spread(ref):
        value = jnp.full(shape, ref[0, 0, 0])
        for w in range(1, shape[0]):
            value = jnp.where(well == w, ref[0, 0, w], value)
        return value

    live = (lax.broadcasted_iota(jnp.int32, shape, 1) < spread(wseg)).astype(F32)
    flats = flat_rows(
        [perf[0, 0, e, k].astype(F32) + 1.0 for e in range(3) for k in range(3)]
        + [live * windex[0, 0], spread(bhp), live, spread(target)],
        buf,
    )
    for e in range(3):
        flat = flats[3 * e:3 * e + 3]
        rows = (flat[0] + roll_half(flat[1]), flat[2])
        for plane in range(2):
            at = count + (plane * 3 + e) * LANES
            idx[:, at:at + LANES] = (rows[plane] - 1.0).astype(jnp.int32)
    static[...] = jnp.zeros(static.shape, F32)
    static[0:1, :] = flats[9] + roll_half(flats[10])
    static[1:2, :] = flats[11] + roll_half(flats[12])
    emit(dims, state, idx, static, outs, (perm_x, perm_y), loads[7:], len(parts))


def connection_kernel(dims, size_y, tiles, rows, trans, pidx, tr):
    _, _, n_fault, n_exp = dims
    tile = tiles[...]
    tile_x = jnp.floor((tile.astype(F32) + 0.5) * (1.0 / size_y)).astype(jnp.int32)
    tile_y = tile - tile_x * size_y
    across = tile_x - lax.axis_index("gx") + 1
    along = tile_y - lax.axis_index("gy") + 1
    pidx[...] = (across * 3 + along) * (n_exp * LANES) + rows[...]
    for r in range(n_fault):
        tr[r:r + 1, :] = trans[:, r * LANES:(r + 1) * LANES]


def gather_kernel(dims, table, idx, own):
    cx, cy, n_fault, _ = dims

    def put(r, f, value):
        own[f * n_fault + r:f * n_fault + r + 1, :] = value

    gather_loop(table, cx * cy, False, idx, 0, n_fault * LANES, put)


def choose_packets(axis, count, mine, rec_a, rec_b, far, pick):
    at = lax.axis_index(axis)
    even = even_at(axis)
    near = slice(0, PACK)
    a, b = rec_a[near, :], rec_b[near, :]
    if len(far) == 1:
        up_far = down_far = far[0][...]
    else:
        up = ((at >> 1) & 1) == 0
        c, d = far[0][...], far[1][...]
        up_far, down_far = jnp.where(up, c, d), jnp.where(up, d, c)
    pick[2] = mine[near, :]
    pick[3] = jnp.where(at + 1 < count, jnp.where(even, a, b), 0.0)
    pick[1] = jnp.where(at >= 1, jnp.where(even, b, a), 0.0)
    pick[4] = jnp.where(at + 2 < count, up_far, 0.0)
    pick[0] = jnp.where(at >= 2, down_far, 0.0)


def middle_kernel(dims, sizes, far_x, skip, *refs):
    _, _, _, n_exp = dims
    mine, rec_a, rec_b = refs[skip:skip + 3]
    refs = refs[skip + 3:]
    far = refs[:far_x]
    yfa, yfb, msg_a, msg_b, msg_c, pick = refs[far_x:]
    even = even_at("gx")
    choose_packets("gx", sizes[0], mine, rec_a, rec_b, far, pick)
    outs = (msg_a, msg_b, msg_c)
    for ref in outs:
        ref[0:PACK, :] = jnp.zeros((PACK, LANES), F32)
    for hx in range(3):
        for plane in range(2):
            for f in range(3):
                at = plane * PLANE + f * 3
                row = (
                    pick[hx, at + 2:at + 3, :]
                    + pick[hx + 1, at + 1:at + 2, :]
                    + pick[hx + 2, at:at + 1, :]
                )
                for ref in outs:
                    ref[at + hx:at + hx + 1, :] = row
        for ref in outs:
            ref[9 + hx:10 + hx, :] = pick[hx + 1, 9:10, :]
            ref[12 + hx:13 + hx, :] = pick[hx + 1, 10:11, :]
    rows = 3 * n_exp
    src = slice(PACK, PACK + rows)
    stack = (
        jnp.where(even, rec_b[src, :], rec_a[src, :]),
        mine[src, :],
        jnp.where(even, rec_a[src, :], rec_b[src, :]),
    )
    for hx in range(3):
        at = PACK + hx * rows
        msg_a[at:at + rows, :] = stack[hx]
        msg_b[at:at + rows, :] = stack[hx]
    at = PACK + 3 * rows
    msg_a[at:at + yfa.shape[0], :] = yfa[...]
    msg_b[at:at + yfb.shape[0], :] = yfb[...]


def roll_half(x):
    return pltpu.roll(x, LANES // 2, 1)


def low_half(shape):
    return lax.broadcasted_iota(jnp.int32, shape, 1) < LANES // 2


def segment_values(packs, seg_ref):
    tops = [packs[y, 0:PLANE, :] for y in range(5)]
    bottoms = [packs[y, PLANE:PACK, :] for y in range(5)]
    lo = low_half((PLANE, LANES))

    def home(hy):
        return tops[hy + 3] + roll_half(tops[hy + 2]) + bottoms[hy + 1]

    plane0 = jnp.where(lo, home(-1), roll_half(home(0)))
    plane1 = jnp.where(lo, home(1), 0.0)
    for f in range(3):
        seg_ref[f * 8:f * 8 + 3, :] = plane0[f * 3:f * 3 + 3, :]
        seg_ref[f * 8 + 3:f * 8 + 6, :] = plane1[f * 3:f * 3 + 3, :]
        seg_ref[f * 8 + 6:f * 8 + 8, :] = jnp.zeros((2, LANES), F32)


def well_constants(packs, const_ref):
    tops = [packs[y, 0:PLANE, :] for y in (1, 2, 3)]
    rolled = [roll_half(t) for t in tops]
    lo = low_half((PLANE, LANES))
    same0 = jnp.where(lo, tops[0], rolled[1])
    same1 = jnp.where(lo, tops[2], 0.0)
    other0 = jnp.where(lo, rolled[0], tops[1])
    other1 = rolled[2]
    const_ref[...] = jnp.zeros(const_ref.shape, F32)
    for at, (a, b), src in ((0, (same0, same1), 9), (8, (other0, other1), 9), (16, (same0, same1), 12)):
        const_ref[at:at + 3, :] = a[src:src + 3, :]
        const_ref[at + 3:at + 6, :] = b[src:src + 3, :]


def running_sum(x):
    lane = lax.broadcasted_iota(jnp.int32, x.shape, 1) & 15
    for shift in (1, 2, 4, 8):
        x = x + jnp.where(lane >= shift, pltpu.roll(x, shift, 1), 0.0)
    return x


def well_mix(seg_ref):
    field = tuple(seg_ref[f * 8:f * 8 + 8, :] for f in range(3))
    sats, factors = props(field)
    mob = mobilities(sats, factors)
    total = mob[0] + mob[1] + mob[2]
    mix = (mob[0] * DENSITY[0] + mob[1] * DENSITY[1] + mob[2] * DENSITY[2]) / total
    return field, sats, factors, mob, total, mix


def well_rates(seg_ref, const_ref):
    weight, bhp, live = (const_ref[i * 8:i * 8 + 8, :] for i in range(3))
    field, _, _, mob, _, mix = well_mix(seg_ref)
    press = bhp + HEAD_SCALE * running_sum(live * mix)
    return [weight * mob[a] * (field[0] - press) for a in range(3)]


def well_rate_tangents(seg_ref, dseg_ref, const_ref):
    weight, bhp, live = (const_ref[i * 8:i * 8 + 8, :] for i in range(3))
    field, sats, factors, mob, total, mix = well_mix(seg_ref)
    press = bhp + HEAD_SCALE * running_sum(live * mix)
    dfield = tuple(dseg_ref[f * 8:f * 8 + 8, :] for f in range(3))
    _, dmob = tangents(sats, factors, mob, dfield)
    dtotal = dmob[0] + dmob[1] + dmob[2]
    dnum = dmob[0] * DENSITY[0] + dmob[1] * DENSITY[1] + dmob[2] * DENSITY[2]
    dpress = HEAD_SCALE * running_sum(live * ((dnum - mix * dtotal) / total))
    return [
        weight * (dmob[a] * (field[0] - press) + mob[a] * (dfield[0] - dpress)) for a in range(3)
    ]


def stack_partners(dims, mine, rec_a, rec_b, partner):
    _, _, _, n_exp = dims
    even = even_at("gy")
    used = 9 * n_exp
    for f in range(3):
        for hx in range(3):
            at = PACK + hx * 3 * n_exp + f * n_exp
            src = slice(at, at + n_exp)
            first, second = rec_a[src, :], rec_b[src, :]
            blocks = (jnp.where(even, second, first), mine[src, :], jnp.where(even, first, second))
            for hy in range(3):
                to = (hx * 3 + hy) * n_exp
                partner[f, to:to + n_exp, :] = blocks[hy]
        if used < partner.shape[1]:
            partner[f, used:, :] = jnp.zeros((partner.shape[1] - used, LANES), F32)


def pick_partners(dims, partner, pidx, table, out):
    _, _, n_fault, _ = dims
    count = partner.shape[1]
    table[...] = split_lanes(partner[...].reshape(3 * count, LANES))

    def put(r, f, value):
        out[f * n_fault + r:f * n_fault + r + 1, :] = value

    gather_loop(table, count, True, pidx, 0, n_fault * LANES, put)


def halo(axis, rec_a, rec_b, at, count):
    even = even_at(axis)
    a, b = rec_a[at:at + count, :], rec_b[at:at + count, :]
    return jnp.where(even, b, a), jnp.where(even, a, b)


def halo_part(dims, axis, rec_a, rec_b, part):
    cx, cy, _, n_exp = dims
    at, count = (PACK + 3 * n_exp, cy) if axis == "gx" else (PACK + 9 * n_exp, cx)
    return halo(axis, rec_a, rec_b, at + part * count, count)


def halo_fields(dims, axis, rec_a, rec_b):
    parts = [halo_part(dims, axis, rec_a, rec_b, f) for f in range(3)]
    return [tuple(v[side] for v in parts) for side in range(2)]


def outermost(dims, axis, ref):
    cx, cy, _, _ = dims
    if axis == "gx":
        return [tuple(ref[f, 0] for f in range(3)), tuple(ref[f, cx - 1] for f in range(3))]
    return [tuple(ref[f, :, 0, :] for f in range(3)), tuple(ref[f, :, cy - 1, :] for f in range(3))]


def edge_fluxes(dims, axis, trans, field, rec_a, rec_b):
    far, near = halo_fields(dims, axis, rec_a, rec_b), outermost(dims, axis, field)
    return [
        face(trans[k], low[0], mob_of(low), high[0], mob_of(high))
        for k, (low, high) in enumerate(((far[0], near[0]), (near[1], far[1])))
    ]


def edge_tangents(dims, axis, trans, field, direction, rec_a, rec_b, drec_a, drec_b):
    far, near = halo_fields(dims, axis, rec_a, rec_b), outermost(dims, axis, field)
    dfar, dnear = halo_fields(dims, axis, drec_a, drec_b), outermost(dims, axis, direction)
    there = [point(far[k], dfar[k]) for k in range(2)]
    here = [point(near[k], dnear[k]) for k in range(2)]
    return [between(trans[0], there[0], here[0]), between(trans[1], here[1], there[1])]


def residual_edge_kernel(dims, size, make, field, gx_a, gx_b, trans, fluxes, *out):
    if make:
        low, high = halo_part(dims, "gx", gx_a, gx_b, 3)
        outer_trans("gx", size, trans, low, high, out[0])
        trans = out[0]
    for k, flux in enumerate(edge_fluxes(dims, "gx", trans, field, gx_a, gx_b)):
        for a in range(3):
            fluxes[k, a] = flux[a]


def jacobian_edge_kernel(dims, field, direction, trans, gx_a, gx_b, dgx_a, dgx_b, fluxes):
    for k, flux in enumerate(edge_tangents(dims, "gx", trans, field, direction, gx_a, gx_b, dgx_a, dgx_b)):
        for a in range(3):
            fluxes[k, a] = flux[a]


def edge_trans(t_a, t_b):
    return 2.0 * t_a * t_b / (t_a + t_b)


def inner_trans(dims, perm, fx, fy, fz, edge_x, edge_y):
    cx, cy, _, _ = dims
    last_row = lax.broadcasted_iota(jnp.int32, (cy, LANES), 0) == cy - 1
    last_lane = lax.broadcasted_iota(jnp.int32, (cy, LANES), 1) == LANES - 1
    for x in range(cx):
        if x + 1 < cx:
            fx[x] = edge_trans(perm[0, x], perm[0, x + 1])
        t = perm[1, x]
        fy[x] = jnp.where(last_row, 0.0, edge_trans(t, pltpu.roll(t, cy - 1, 0)))
        t = perm[2, x]
        fz[x] = jnp.where(last_lane, 0.0, edge_trans(t, pltpu.roll(t, LANES - 1, 1)))
    edge_x[0], edge_x[1] = perm[0, 0], perm[0, cx - 1]
    edge_y[0], edge_y[1] = perm[1, :, 0, :], perm[1, :, cy - 1, :]


def outer_trans(axis, count, edge, low, high, out):
    at = lax.axis_index(axis)
    out[0] = jnp.where(at > 0, edge_trans(low, edge[0]), 0.0)
    out[1] = jnp.where(at < count - 1, edge_trans(edge[1], high), 0.0)


def mob_of(field):
    return mobilities(*props(field))


def residual_planes(dims, field, pore, fx, fy, fz, acc):
    cx, cy, _, _ = dims

    def plane(x):
        fld = tuple(field[f, x] for f in range(3))
        sats, factors = props(fld)
        return fld[0], mobilities(sats, factors), sats, factors

    cur, below = plane(0), None
    for x in range(cx):
        p, mob, sats, factors = cur
        row = lambda v: pltpu.roll(v, cy - 1, 0)
        lane = lambda v: pltpu.roll(v, LANES - 1, 1)
        y_up = face(fy[x], p, mob, row(p), [row(m) for m in mob])
        z_up = face(fz[x], p, mob, lane(p), [lane(m) for m in mob], 1.0)
        nxt = above = None
        if x + 1 < cx:
            nxt = plane(x + 1)
            above = face(fx[x], p, mob, nxt[0], nxt[1])
        for a in range(3):
            inflow = (y_up[a] - pltpu.roll(y_up[a], 1, 0)) + (z_up[a] - pltpu.roll(z_up[a], 1, 1))
            if above is not None:
                inflow = inflow + above[a]
            if below is not None:
                inflow = inflow - below[a]
            acc[a, x] = pore[x] * (factors[a] * sats[a]) - inflow
        cur, below = nxt, above


def point(field, dfield):
    sats, factors = props(field)
    mob = mobilities(sats, factors)
    dsats, dmob = tangents(sats, factors, mob, dfield)
    return field[0], mob, dfield[0], dmob, sats, factors, dsats


def between(trans, c, n, depth=0.0):
    return face_tangent(trans, c[0], c[1], n[0], n[1], c[2], c[3], n[2], n[3], depth)


def jacobian_planes(dims, field, dfield, pore, fx, fy, fz, acc):
    cx, cy, _, _ = dims

    def plane(x):
        return point(tuple(field[f, x] for f in range(3)), tuple(dfield[f, x] for f in range(3)))

    def moved(c, shift):
        return shift(c[0]), [shift(m) for m in c[1]], shift(c[2]), [shift(m) for m in c[3]]

    cur, below = plane(0), None
    for x in range(cx):
        y_up = between(fy[x], cur, moved(cur, lambda v: pltpu.roll(v, cy - 1, 0)))
        z_up = between(fz[x], cur, moved(cur, lambda v: pltpu.roll(v, LANES - 1, 1)), 1.0)
        nxt = above = None
        if x + 1 < cx:
            nxt = plane(x + 1)
            above = between(fx[x], cur, nxt)
        _, _, dp, _, sats, factors, dsats = cur
        for a in range(3):
            inflow = (y_up[a] - pltpu.roll(y_up[a], 1, 0)) + (z_up[a] - pltpu.roll(z_up[a], 1, 1))
            if above is not None:
                inflow = inflow + above[a]
            if below is not None:
                inflow = inflow - below[a]
            gain = pore[x] * (factors[a] * (dsats[a] + COMPRESS[a] * sats[a] * dp))
            acc[a, x] = gain - inflow
        cur, below = nxt, above


def add_outer(dims, x_fluxes, y_fluxes, acc):
    cx, cy, _, _ = dims
    for a in range(3):
        acc[a, 0] = acc[a, 0] + x_fluxes[0, a]
        acc[a, cx - 1] = acc[a, cx - 1] - x_fluxes[1, a]
        acc[a, :, 0, :] = acc[a, :, 0, :] + y_fluxes[0][a]
        acc[a, :, cy - 1, :] = acc[a, :, cy - 1, :] - y_fluxes[1][a]


def residual_inner_kernel(dims, make, field, pore, *refs):
    if make:
        perm, acc, fx, fy, fz, edge_x, edge_y = refs
        inner_trans(dims, perm, fx, fy, fz, edge_x, edge_y)
    else:
        fx, fy, fz, acc = refs
    residual_planes(dims, field, pore, fx, fy, fz, acc)


def jacobian_inner_kernel(dims, field, direction, pore, fx, fy, fz, acc):
    jacobian_planes(dims, field, direction, pore, fx, fy, fz, acc)


def rows_of(ref, count):
    return tuple(ref[f * count:(f + 1) * count, :] for f in range(3))


def finish_faults(dims, inner, old_mass, flux, idx, values, x_fluxes, y_fluxes, acc):
    cx, cy, n_fault, _ = dims
    for a in range(3):
        values[a, 0:n_fault, :] = -flux[a]
    total = scatter_loop(values, idx, 0, n_fault * LANES, cx * cy, True)
    for a in range(3):
        part = inner[a] + total[a].reshape(cx, cy, LANES)
        acc[a] = part if old_mass is None else part - old_mass[a]
    add_outer(dims, x_fluxes, y_fluxes, acc)


def residual_fault_kernel(dims, size, make, *refs):
    _, _, n_fault, _ = dims
    inner, old_mass, field, idx, pidx, tr, own, x_fluxes, mine, gy_a, gy_b, trans, acc, partner_vals = refs[:14]
    if make:
        low, high = halo_part(dims, "gy", gy_a, gy_b, 3)
        outer_trans("gy", size, trans, low, high, refs[14])
        trans = refs[14]
    partner, values, ptable = refs[-3:]
    stack_partners(dims, mine, gy_a, gy_b, partner)
    pick_partners(dims, partner, pidx, ptable, partner_vals)
    mine_f, other_f = rows_of(own, n_fault), rows_of(partner_vals, n_fault)
    flux = face(tr[...], mine_f[0], mob_of(mine_f), other_f[0], mob_of(other_f))
    y_fluxes = edge_fluxes(dims, "gy", trans, field, gy_a, gy_b)
    finish_faults(dims, inner, old_mass, flux, idx, values, x_fluxes, y_fluxes, acc)


def jacobian_fault_kernel(dims, *refs):
    _, _, n_fault, _ = dims
    inner, field, direction, idx, pidx, tr, own, other, down, trans, x_fluxes = refs[:11]
    gy_a, gy_b, mine, dgy_a, dgy_b, acc, partner, values, ptable, dother = refs[11:]
    stack_partners(dims, mine, dgy_a, dgy_b, partner)
    pick_partners(dims, partner, pidx, ptable, dother)
    flux = between(
        tr[...],
        point(rows_of(own, n_fault), rows_of(down, n_fault)),
        point(rows_of(other, n_fault), rows_of(dother, n_fault)),
    )
    y_fluxes = edge_tangents(dims, "gy", trans, field, direction, gy_a, gy_b, dgy_a, dgy_b)
    finish_faults(dims, inner, None, flux, idx, values, x_fluxes, y_fluxes, acc)


def well_sums(dims, rates, idx, values, turned):
    cx, cy, n_fault, _ = dims
    for a in range(3):
        values[a] = rates[a]
    start = n_fault * LANES
    total = scatter_loop(values, idx, start, start + 6 * LANES, cx * cy, turned)
    return [part.reshape(cx, cy, LANES) for part in total]


def residual_kernel(dims, sizes, final, far_y, *refs):
    refs = list(refs)
    take = lambda n: [refs.pop(0) for _ in range(n)]
    partial, scaling, idx, static = take(4)
    mine, gy_a, gy_b = take(3)
    far = take(far_y)
    direction, seg, const = take(3)
    outs = take(6)
    if final:
        residual, well = take(2)
    packs, values = take(2)
    choose_packets("gy", sizes[1], mine, gy_a, gy_b, far, packs)
    segment_values(packs, seg)
    well_constants(packs, const)
    rates = well_rates(seg, const)
    if final:
        done = running_sum(rates[0] + rates[1] + rates[2])[1:2, :]
        value = done / packs[2, 13:14, :] - 1.0
        lane = lax.broadcasted_iota(jnp.int32, value.shape, 1)
        column = lax.broadcasted_iota(jnp.int32, well.shape, 2)
        count = well.shape[2]
        result = jnp.zeros(well.shape, F32)
        for w in range(count):
            last = LANES // 2 + (w + 1) * (LANES // 2 // count) - 1
            result = jnp.where(column == w, jnp.sum(jnp.where(lane == last, value, 0.0)), result)
        well[...] = result
    sums = well_sums(dims, rates, idx, values, False)
    for a in range(3):
        res = partial[a] + sums[a]
        if final:
            residual[a] = res
        direction[a] = scaling[a] * res
    emit(dims, direction, idx, static, outs)


def jacobian_kernel(dims, sizes, final, far_y, *refs):
    refs = list(refs)
    take = lambda n: [refs.pop(0) for _ in range(n)]
    partial, field, direction, scaling, idx, static, seg, const = take(8)
    mine, dgy_a, dgy_b = take(3)
    far = take(far_y)
    (result,) = take(1)
    outs = None if final else take(6)
    packs, values, dseg = take(3)
    choose_packets("gy", sizes[1], mine, dgy_a, dgy_b, far, packs)
    segment_values(packs, dseg)
    sums = well_sums(dims, well_rate_tangents(seg, dseg, const), idx, values, final)
    for a in range(3):
        step = 2.0 * direction[a] - scaling[a] * (partial[a] + sums[a])
        result[a] = step if final else field[a] - step
    if not final:
        emit(dims, result, idx, static, outs)


def exchange_pairs(axis, kind, size_x, size_y):
    def partner(i, count):
        step = 1 if kind < 2 else 2
        shift = step if kind % 2 else 0
        if shift and not shift <= i < count - shift:
            return None
        return ((i + shift) ^ step) - shift

    out = []
    for i in range(size_x):
        for j in range(size_y):
            if axis == 0:
                got = partner(i, size_x)
                far = (got, j) if got is not None else ((i, j ^ 1) if kind < 2 else (i ^ 1, j))
            else:
                got = partner(j, size_y)
                far = (i, got) if got is not None else ((i ^ 1, j) if kind < 2 else (i, j ^ 1))
            out.append((i * size_y + j, far[0] * size_y + far[1]))
    return out


def body(
    state, perm, pore, old_mass, scaling, fault_cell, fault_tile, fault_row, fault_trans,
    fault_export, perf_cell, well_segments, well_index, bhp, target,
):
    size_x, size_y = lax.axis_size("gx"), lax.axis_size("gy")
    _, cx, cy, _ = state.shape
    wells, segs = well_index.shape[2:]
    n_fault, n_exp = fault_cell.shape[-1] // LANES, fault_export.shape[-1] // LANES
    dims = (cx, cy, n_fault, n_exp)
    far_x = 1 if size_x == 4 else 2
    far_y = 1 if size_y == 4 else 2
    params = pltpu.CompilerParams(vmem_limit_bytes=VMEM_BYTES)
    anywhere = pl.BlockSpec(memory_space=pl.ANY)
    hbm = pl.BlockSpec(memory_space=pltpu.HBM)
    vmem = pl.BlockSpec(memory_space=pltpu.VMEM)
    shape = lambda *dims_: jax.ShapeDtypeStruct(dims_, F32)
    rows = cx * cy
    gx_rows = PACK + 3 * n_exp + 3 * cy
    gy_rows = PACK + 9 * n_exp + 3 * cx
    table = jax.ShapeDtypeStruct((3 * LANES, 2 * rows), BF16)
    near_rows = -(-9 * n_exp // 16) * 16

    def call(kernel, args, outs, scratch=(), specs=None):
        return pl.pallas_call(
            kernel,
            out_shape=outs,
            in_specs=specs or [vmem] * len(args),
            out_specs=[vmem] * len(outs),
            scratch_shapes=scratch,
            compiler_params=params,
        )(*args)

    def message_shapes(first):
        more_x, more_y = (cy, cx) if first else (0, 0)
        return [
            shape(gx_rows + more_x, LANES), shape(gx_rows + more_x, LANES), shape(PACK, LANES),
            shape(3 * cx + more_y, LANES), shape(3 * cx + more_y, LANES), table,
        ]

    def send(value, axis, kind):
        return lax.ppermute(value, ("gx", "gy"), exchange_pairs(axis, kind, size_x, size_y))

    def send_x(messages):
        msg_a, msg_b, packet = messages[:3]
        far = [send(packet, 0, 2 + k) for k in range(far_x)]
        rec_b = send(msg_b, 0, 1)
        rec_a = send(msg_a, 0, 0)
        return rec_a, rec_b, far

    def send_y(messages, got, after):
        msg_a, _, _, yfa, yfb, _ = messages
        rec_a, rec_b, far = got
        total = PACK + 9 * n_exp + yfa.shape[0]
        mid_a, mid_b, mid_c = call(
            functools.partial(middle_kernel, dims, sizes, far_x, len(after)),
            [*after, msg_a, rec_a, rec_b, *far, yfa, yfb],
            [shape(total, LANES), shape(total, LANES), shape(PACK, LANES)],
            [pltpu.VMEM((5, PACK, LANES), F32)],
            [anywhere] * len(after) + [vmem] * (5 + far_x),
        )
        got_b = send(mid_b, 1, 1)
        got_a = send(mid_a, 1, 0)
        got_far = [send(mid_c, 1, 2 + k) for k in range(far_y)]
        return (mid_a, got_a, got_b), got_far

    sizes = (size_x, size_y)
    grid = shape(3, cx, cy, LANES)
    wide_rows = shape(3 * n_fault, LANES)
    small = shape(24, LANES)
    packs = pltpu.VMEM((5, PACK, LANES), F32)
    fault_work = [
        pltpu.VMEM((3, near_rows, LANES), F32), pltpu.VMEM((3, n_fault, LANES), F32),
        pltpu.VMEM((3 * near_rows, 2 * LANES), BF16),
    ]
    well_work = [packs, pltpu.VMEM((3, 8, LANES), F32)]
    columns = (n_fault + 6 + n_exp) * LANES

    sources = [state, perm, fault_cell, fault_export, perf_cell, well_index, well_segments, bhp, target]
    results = call(
        functools.partial(first_kernel, dims),
        [pltpu.with_memory_space_constraint(v, pltpu.HBM) for v in sources],
        message_shapes(True) + [jax.ShapeDtypeStruct((1, columns), jnp.int32), shape(8, LANES), shape(*state.shape)],
        [pltpu.VMEM((2, cy, LANES), F32)]
        + [(pltpu.VMEM if i < 4 else pltpu.SMEM)(v.shape, v.dtype) for i, v in enumerate(sources[2:])]
        + [pltpu.VMEM((2, cx, 8, LANES), F32), pltpu.VMEM((13 * 8, LANES), F32), pltpu.SemaphoreType.DMA((11 + 3 * (cx // 2),))],
        [hbm] * len(sources),
    )
    messages, (idx, static, current) = results[:6], results[6:]

    def own_cells(cells_table):
        return call(functools.partial(gather_kernel, dims), [cells_table, idx], [wide_rows])[0]

    for step in range(2):
        final = step == 1
        got = send_x(messages)
        gx_got = got[:2]
        if final:
            (inner,) = call(
                functools.partial(residual_inner_kernel, dims, False), [current, pore, *trans], [grid]
            )
        else:
            inner, *trans, edge_x, edge_y = call(
                functools.partial(residual_inner_kernel, dims, True), [current, pore, perm],
                [grid, shape(cx, cy, LANES), shape(cx, cy, LANES), shape(cx, cy, LANES),
                 shape(2, cy, LANES), shape(2, cx, LANES)],
            )
            pidx, tr = call(
                functools.partial(connection_kernel, dims, size_y),
                [fault_tile.reshape(1, -1), fault_row.reshape(1, -1), fault_trans.reshape(1, -1)],
                [jax.ShapeDtypeStruct((1, n_fault * LANES), jnp.int32), shape(n_fault, LANES)],
            )
        own = own_cells(messages[5])
        gy_got, gy_far = send_y(messages, got, (inner, own) if final else (inner, own, pidx))
        edge_shape = shape(2, 3, cy, LANES)
        results = call(
            functools.partial(residual_edge_kernel, dims, size_x, not final),
            [current, *gx_got, outer_x if final else edge_x],
            [edge_shape] + ([] if final else [shape(2, cy, LANES)]),
        )
        x_fluxes = results[0]
        if not final:
            outer_x = results[1]
        results = call(
            functools.partial(residual_fault_kernel, dims, size_y, not final),
            [inner, old_mass, current, idx, pidx, tr, own, x_fluxes, *gy_got, outer_y if final else edge_y],
            [grid, wide_rows] + ([] if final else [shape(2, cx, LANES)]),
            fault_work,
        )
        partial, other = results[:2]
        if not final:
            outer_y = results[2]
        results = call(
            functools.partial(residual_kernel, dims, sizes, final, far_y),
            [partial, scaling, idx, static, *gy_got, *gy_far],
            [grid, small, small] + message_shapes(False) + ([grid, shape(1, 1, wells)] if final else []),
            well_work,
        )
        direction, seg, const = results[:3]
        messages = results[3:9]
        if final:
            residual, well = results[9:]
        got = send_x(messages)
        (inner,) = call(
            functools.partial(jacobian_inner_kernel, dims), [current, direction, pore, *trans], [grid]
        )
        down = own_cells(messages[5])
        dgy_got, dgy_far = send_y(messages, got, (inner, down))
        (x_fluxes,) = call(
            functools.partial(jacobian_edge_kernel, dims),
            [current, direction, outer_x, *gx_got, *got[:2]],
            [edge_shape],
        )
        (partial,) = call(
            functools.partial(jacobian_fault_kernel, dims),
            [inner, current, direction, idx, pidx, tr, own, other, down, outer_y, x_fluxes, *gy_got[1:], *dgy_got],
            [grid],
            fault_work + [pltpu.VMEM((3 * n_fault, LANES), F32)],
        )
        results = call(
            functools.partial(jacobian_kernel, dims, sizes, final, far_y),
            [partial, current, direction, scaling, idx, static, seg, const, *dgy_got, *dgy_far],
            [grid] + ([] if final else message_shapes(False)),
            well_work + [pltpu.VMEM((24, LANES), F32)],
        )
        current, messages = results[0], results[1:]
    return residual, current, well


def solution(mesh):
    grid = P(None, "gx", "gy", None)
    tile = P("gx", "gy", None)
    return jax.shard_map(
        body,
        mesh=mesh,
        in_specs=(
            grid, grid, tile, grid, grid, tile, tile, tile, tile, tile,
            P("gx", "gy", None, None, None, None), tile, P("gx", "gy", None, None), tile, tile,
        ),
        out_specs=(grid, grid, tile),
        check_vma=False,
    )
```

```python
import functools

import jax
import jax.numpy as jnp
from jax import lax
from jax.experimental import pallas as pl
from jax.experimental.pallas import tpu as pltpu
from jax.sharding import PartitionSpec as P

VISCOSITY = (0.5, 2.0, 0.1)
COMPRESS = (0.02, 0.05, 0.3)
DENSITY = (1.0, 0.8, 0.2)
GRAVITY = 0.2
INV_SMOOTHING = 10.0
HEAD_SCALE = 0.3

LANES = 128
PACK = 32
PLANE = 16
VMEM_BYTES = 40 * 1024 * 1024
F32 = jnp.float32
BF16 = jnp.bfloat16


def props(field):
    p, sw, sg = field
    sats = (sw, 1.0 - sw - sg, sg)
    factors = tuple(jnp.exp(COMPRESS[a] * p) for a in range(3))
    return sats, factors


def mobilities(sats, factors):
    return tuple(sats[a] * sats[a] * factors[a] * (1.0 / VISCOSITY[a]) for a in range(3))


def tangents(sats, factors, mob, dfield):
    dp, dsw, dsg = dfield
    dsats = (dsw, -(dsw + dsg), dsg)
    dmob = tuple(
        mob[a] * (COMPRESS[a] * dp) + sats[a] * factors[a] * (2.0 / VISCOSITY[a]) * dsats[a]
        for a in range(3)
    )
    return dsats, dmob


def face(trans, p_c, mob_c, p_n, mob_n, depth=0.0):
    out = []
    diff = p_n - p_c
    for a in range(3):
        if a == 0 or depth:
            pot = diff - GRAVITY * DENSITY[a] * depth if depth else diff
            weight = jax.nn.sigmoid(pot * INV_SMOOTHING)
            scaled = trans * pot
        out.append(scaled * (mob_c[a] + weight * (mob_n[a] - mob_c[a])))
    return out


def face_tangent(trans, p_c, mob_c, p_n, mob_n, dp_c, dmob_c, dp_n, dmob_n, depth=0.0):
    out = []
    diff = p_n - p_c
    ddiff = dp_n - dp_c
    for a in range(3):
        if a == 0 or depth:
            pot = diff - GRAVITY * DENSITY[a] * depth if depth else diff
            weight = jax.nn.sigmoid(pot * INV_SMOOTHING)
            dweight = (weight * (1.0 - weight)) * (ddiff * INV_SMOOTHING)
        step = mob_n[a] - mob_c[a]
        mean = mob_c[a] + weight * step
        dmean = dmob_c[a] + weight * (dmob_n[a] - dmob_c[a]) + dweight * step
        out.append(trans * (mean * ddiff + pot * dmean))
    return out


def split2(x):
    high = x.astype(BF16)
    return high, (x - high.astype(F32)).astype(BF16)


def one_hot(place, count):
    at = lax.broadcasted_iota(jnp.int32, (count, place.shape[1]), 0).astype(F32).astype(BF16)
    return jnp.where(at == place.astype(F32).astype(BF16), jnp.ones((), BF16), jnp.zeros((), BF16))


def even_at(axis):
    return (lax.axis_index(axis) & 1) == 0


def gather_loop(table, count, by_lane, idx_ref, start, columns, put):
    kept = count if by_lane else LANES
    for c in range(start, columns, 256):
        width = min(256, columns - c)
        idx = idx_ref[:, c:c + width]
        row, lane = idx >> 7, idx & (LANES - 1)
        hot = one_hot(lane, LANES) if by_lane else one_hot(row, count)
        picked = jnp.dot(table[...], jnp.concatenate([hot, hot], axis=0), preferred_element_type=F32)
        rest = row if by_lane else lane
        for h in range(width // LANES):
            cols = slice(h * LANES, (h + 1) * LANES)
            mask = lax.broadcasted_iota(jnp.int32, (kept, LANES), 0) == rest[:, cols]
            for f in range(3):
                block = picked[f * kept:(f + 1) * kept, cols]
                value = jnp.sum(jnp.where(mask, block, 0.0), axis=0, keepdims=True)
                put(c // LANES + h, f, value)


def scatter_loop(values_ref, idx_ref, start, columns, count, turned):
    total = jnp.zeros((3 * LANES, count) if turned else (count, 3 * LANES), F32)
    for c in range(start, columns, 256):
        width = min(256, columns - c)
        idx = idx_ref[:, c:c + width]
        hot = one_hot(idx >> 7, count)
        lane = (idx & (LANES - 1)).astype(F32).astype(BF16)
        at = lax.broadcasted_iota(jnp.int32, (LANES, width), 0).astype(F32).astype(BF16)
        mask = at == lane
        highs, lows = [], []
        for f in range(3):
            r = (c - start) // LANES
            row = jnp.concatenate(
                [values_ref[f, r + h:r + h + 1, :] for h in range(width // LANES)], axis=1
            )
            high, low = split2(row)
            highs.append(jnp.where(mask, high, jnp.zeros((), BF16)))
            lows.append(jnp.where(mask, low, jnp.zeros((), BF16)))
        right = jnp.concatenate(
            [jnp.concatenate(highs, axis=0), jnp.concatenate(lows, axis=0)], axis=1
        )
        left = jnp.concatenate([hot, hot], axis=1)
        total = total + lax.dot_general(
            *((right, left) if turned else (left, right)), (((1,), (1,)), ((), ())), preferred_element_type=F32
        )
    if turned:
        return [total[f * LANES:(f + 1) * LANES, :].T for f in range(3)]
    return [total[:, f * LANES:(f + 1) * LANES] for f in range(3)]


def split_lanes(cells):
    return jnp.concatenate(split2(cells), axis=1)


def emit(dims, field_ref, idx_ref, static_ref, outs, perm_refs=None, loads=()):
    gxa, gxb, gxp, yfa, yfb, table_ref = outs
    cx, cy, n_fault, n_exp = dims
    rows = cx * cy
    zeros = jnp.zeros((PACK, LANES), F32)
    for ref in (gxa, gxb, gxp):
        ref[0:PACK, :] = zeros
        ref[9:11, :] = static_ref[0:2, :]
    even_x, even_y = even_at("gx"), even_at("gy")
    base = PACK + 3 * n_exp

    def put_faces(out_a, out_b, at, low, high, even):
        count = low.shape[0]
        out_a[at:at + count, :] = jnp.where(even, high, low)
        out_b[at:at + count, :] = jnp.where(even, low, high)

    for f in range(3):
        if loads:
            loads[f].wait()
        put_faces(gxa, gxb, base + f * cy, field_ref[f, 0], field_ref[f, cx - 1], even_x)
        put_faces(yfa, yfb, f * cx, field_ref[f, :, 0, :], field_ref[f, :, cy - 1, :], even_y)
        high, low = split2(field_ref[f].reshape(rows, LANES).T)
        table_ref[f * LANES:(f + 1) * LANES, 0:rows] = high
        table_ref[f * LANES:(f + 1) * LANES, rows:2 * rows] = low
    if perm_refs is not None:
        for load in loads[3:]:
            load.wait()
        perm_x, perm_y = perm_refs
        put_faces(gxa, gxb, base + 3 * cy, perm_x[0], perm_x[1], even_x)
        put_faces(yfa, yfb, 3 * cx, perm_y[0, :, 0, :], perm_y[1, :, 7, :], even_y)

    def put(r, f, value):
        if r < n_fault + 6:
            plane, e = divmod(r - n_fault, 3)
            at = plane * PLANE + f * 3 + e
            for ref in (gxa, gxb, gxp):
                ref[at:at + 1, :] = value
        else:
            at = PACK + f * n_exp + r - n_fault - 6
            for ref in (gxa, gxb):
                ref[at:at + 1, :] = value

    gather_loop(table_ref, rows, False, idx_ref, n_fault * LANES, (n_fault + 6 + n_exp) * LANES, put)


def flat_row(v, buf):
    buf[...] = jnp.zeros(buf.shape, F32)
    buf[0:v.shape[0], 0:v.shape[1]] = v
    moved = pltpu.roll(buf[...], 0, 1, stride=v.shape[1], stride_axis=0)
    return jnp.sum(moved, axis=0, keepdims=True)


def first_kernel(dims, *refs):
    sources, outs, (idx, static) = refs[:9], refs[9:15], refs[15:17]
    targets, (perm_y, buf, sems) = refs[17:26], refs[26:]
    cx, cy, n_fault, n_exp = dims
    state, perm_x, cells, exports, perf, windex, wseg, bhp, target = targets
    state_hbm, perm_hbm = sources[:2]
    pairs = list(zip(sources[2:], targets[2:]))
    pairs += [(state_hbm.at[f], state.at[f]) for f in range(3)]
    pairs += [(perm_hbm.at[0, 0], perm_x.at[0]), (perm_hbm.at[0, cx - 1], perm_x.at[1])]
    pairs += [(perm_hbm.at[1, :, 0:8, :], perm_y.at[0]), (perm_hbm.at[1, :, cy - 8:cy, :], perm_y.at[1])]
    loads = [pltpu.make_async_copy(src, dst, sems.at[i]) for i, (src, dst) in enumerate(pairs)]
    for load in loads:
        load.start()
    for load in loads[:7]:
        load.wait()
    count = n_fault * LANES
    idx[:, 0:count] = cells[0]
    idx[:, count + 6 * LANES:] = exports[0]
    for e in range(3):
        flat = [flat_row(perf[0, 0, e, k].astype(F32) + 1.0, buf) for k in range(3)]
        rows = (flat[0] + roll_half(flat[1]), flat[2])
        for plane in range(2):
            at = count + (plane * 3 + e) * LANES
            idx[:, at:at + LANES] = (rows[plane] - 1.0).astype(jnp.int32)
    shape = windex.shape[2:]
    well = lax.broadcasted_iota(jnp.int32, shape, 0)

    def spread(ref):
        value = jnp.full(shape, ref[0, 0, 0])
        for w in range(1, shape[0]):
            value = jnp.where(well == w, ref[0, 0, w], value)
        return value

    live = (lax.broadcasted_iota(jnp.int32, shape, 1) < spread(wseg)).astype(F32)
    static[...] = jnp.zeros(static.shape, F32)
    static[0:1, :] = flat_row(live * windex[0, 0], buf) + roll_half(flat_row(spread(bhp), buf))
    static[1:2, :] = flat_row(live, buf) + roll_half(flat_row(spread(target), buf))
    emit(dims, state, idx, static, outs, (perm_x, perm_y), loads[7:])


def connection_kernel(dims, size_y, tiles, rows, trans, pidx, tr):
    _, _, n_fault, n_exp = dims
    tile = tiles[...]
    tile_x = jnp.floor((tile.astype(F32) + 0.5) * (1.0 / size_y)).astype(jnp.int32)
    tile_y = tile - tile_x * size_y
    across = tile_x - lax.axis_index("gx") + 1
    along = tile_y - lax.axis_index("gy") + 1
    pidx[...] = (across * 3 + along) * (n_exp * LANES) + rows[...]
    for r in range(n_fault):
        tr[r:r + 1, :] = trans[:, r * LANES:(r + 1) * LANES]


def gather_kernel(dims, table, idx, own):
    cx, cy, n_fault, _ = dims

    def put(r, f, value):
        own[f * n_fault + r:f * n_fault + r + 1, :] = value

    gather_loop(table, cx * cy, False, idx, 0, n_fault * LANES, put)


def choose_packets(axis, count, mine, rec_a, rec_b, far, pick):
    at = lax.axis_index(axis)
    even = even_at(axis)
    near = slice(0, PACK)
    a, b = rec_a[near, :], rec_b[near, :]
    if len(far) == 1:
        up_far = down_far = far[0][...]
    else:
        up = ((at >> 1) & 1) == 0
        c, d = far[0][...], far[1][...]
        up_far, down_far = jnp.where(up, c, d), jnp.where(up, d, c)
    pick[2] = mine[near, :]
    pick[3] = jnp.where(at + 1 < count, jnp.where(even, a, b), 0.0)
    pick[1] = jnp.where(at >= 1, jnp.where(even, b, a), 0.0)
    pick[4] = jnp.where(at + 2 < count, up_far, 0.0)
    pick[0] = jnp.where(at >= 2, down_far, 0.0)


def middle_kernel(dims, sizes, far_x, _, __, mine, rec_b, rec_a, *refs):
    _, _, _, n_exp = dims
    far = refs[:far_x]
    yfa, yfb, msg_a, msg_b, msg_c, pick = refs[far_x:]
    even = even_at("gx")
    choose_packets("gx", sizes[0], mine, rec_a, rec_b, far, pick)
    outs = (msg_a, msg_b, msg_c)
    for ref in outs:
        ref[0:PACK, :] = jnp.zeros((PACK, LANES), F32)
    for hx in range(3):
        for plane in range(2):
            for f in range(3):
                at = plane * PLANE + f * 3
                row = (
                    pick[hx, at + 2:at + 3, :]
                    + pick[hx + 1, at + 1:at + 2, :]
                    + pick[hx + 2, at:at + 1, :]
                )
                for ref in outs:
                    ref[at + hx:at + hx + 1, :] = row
        for ref in outs:
            ref[9 + hx:10 + hx, :] = pick[hx + 1, 9:10, :]
            ref[12 + hx:13 + hx, :] = pick[hx + 1, 10:11, :]
    rows = 3 * n_exp
    src = slice(PACK, PACK + rows)
    stack = (
        jnp.where(even, rec_b[src, :], rec_a[src, :]),
        mine[src, :],
        jnp.where(even, rec_a[src, :], rec_b[src, :]),
    )
    for hx in range(3):
        at = PACK + hx * rows
        msg_a[at:at + rows, :] = stack[hx]
        msg_b[at:at + rows, :] = stack[hx]
    at = PACK + 3 * rows
    msg_a[at:at + yfa.shape[0], :] = yfa[...]
    msg_b[at:at + yfb.shape[0], :] = yfb[...]


def roll_half(x):
    return pltpu.roll(x, LANES // 2, 1)


def low_half(shape):
    return lax.broadcasted_iota(jnp.int32, shape, 1) < LANES // 2


def segment_values(packs, seg_ref):
    tops = [packs[y, 0:PLANE, :] for y in range(5)]
    bottoms = [packs[y, PLANE:PACK, :] for y in range(5)]
    lo = low_half((PLANE, LANES))

    def home(hy):
        return tops[hy + 3] + roll_half(tops[hy + 2]) + bottoms[hy + 1]

    plane0 = jnp.where(lo, home(-1), roll_half(home(0)))
    plane1 = jnp.where(lo, home(1), 0.0)
    for f in range(3):
        seg_ref[f * 8:f * 8 + 3, :] = plane0[f * 3:f * 3 + 3, :]
        seg_ref[f * 8 + 3:f * 8 + 6, :] = plane1[f * 3:f * 3 + 3, :]
        seg_ref[f * 8 + 6:f * 8 + 8, :] = jnp.zeros((2, LANES), F32)


def well_constants(packs, const_ref):
    tops = [packs[y, 0:PLANE, :] for y in (1, 2, 3)]
    rolled = [roll_half(t) for t in tops]
    lo = low_half((PLANE, LANES))
    same0 = jnp.where(lo, tops[0], rolled[1])
    same1 = jnp.where(lo, tops[2], 0.0)
    other0 = jnp.where(lo, rolled[0], tops[1])
    other1 = rolled[2]
    const_ref[...] = jnp.zeros(const_ref.shape, F32)
    for at, (a, b), src in ((0, (same0, same1), 9), (8, (other0, other1), 9), (16, (same0, same1), 12)):
        const_ref[at:at + 3, :] = a[src:src + 3, :]
        const_ref[at + 3:at + 6, :] = b[src:src + 3, :]


def running_sum(x):
    lane = lax.broadcasted_iota(jnp.int32, x.shape, 1) & 15
    for shift in (1, 2, 4, 8):
        x = x + jnp.where(lane >= shift, pltpu.roll(x, shift, 1), 0.0)
    return x


def well_mix(seg_ref):
    field = tuple(seg_ref[f * 8:f * 8 + 8, :] for f in range(3))
    sats, factors = props(field)
    mob = mobilities(sats, factors)
    total = mob[0] + mob[1] + mob[2]
    mix = (mob[0] * DENSITY[0] + mob[1] * DENSITY[1] + mob[2] * DENSITY[2]) / total
    return field, sats, factors, mob, total, mix


def well_rates(seg_ref, const_ref):
    weight, bhp, live = (const_ref[i * 8:i * 8 + 8, :] for i in range(3))
    field, _, _, mob, _, mix = well_mix(seg_ref)
    press = bhp + HEAD_SCALE * running_sum(live * mix)
    return [weight * mob[a] * (field[0] - press) for a in range(3)]


def well_rate_tangents(seg_ref, dseg_ref, const_ref):
    weight, bhp, live = (const_ref[i * 8:i * 8 + 8, :] for i in range(3))
    field, sats, factors, mob, total, mix = well_mix(seg_ref)
    press = bhp + HEAD_SCALE * running_sum(live * mix)
    dfield = tuple(dseg_ref[f * 8:f * 8 + 8, :] for f in range(3))
    _, dmob = tangents(sats, factors, mob, dfield)
    dtotal = dmob[0] + dmob[1] + dmob[2]
    dnum = dmob[0] * DENSITY[0] + dmob[1] * DENSITY[1] + dmob[2] * DENSITY[2]
    dpress = HEAD_SCALE * running_sum(live * ((dnum - mix * dtotal) / total))
    return [
        weight * (dmob[a] * (field[0] - press) + mob[a] * (dfield[0] - dpress)) for a in range(3)
    ]


def stack_partners(dims, mine, rec_a, rec_b, partner):
    _, _, _, n_exp = dims
    even = even_at("gy")
    used = 9 * n_exp
    for f in range(3):
        for hx in range(3):
            at = PACK + hx * 3 * n_exp + f * n_exp
            src = slice(at, at + n_exp)
            first, second = rec_a[src, :], rec_b[src, :]
            blocks = (jnp.where(even, second, first), mine[src, :], jnp.where(even, first, second))
            for hy in range(3):
                to = (hx * 3 + hy) * n_exp
                partner[f, to:to + n_exp, :] = blocks[hy]
        if used < partner.shape[1]:
            partner[f, used:, :] = jnp.zeros((partner.shape[1] - used, LANES), F32)


def pick_partners(dims, partner, pidx, table, out):
    _, _, n_fault, _ = dims
    count = partner.shape[1]
    table[...] = split_lanes(partner[...].reshape(3 * count, LANES))

    def put(r, f, value):
        out[f * n_fault + r:f * n_fault + r + 1, :] = value

    gather_loop(table, count, True, pidx, 0, n_fault * LANES, put)


def halo(axis, rec_a, rec_b, at, count):
    even = even_at(axis)
    a, b = rec_a[at:at + count, :], rec_b[at:at + count, :]
    return jnp.where(even, b, a), jnp.where(even, a, b)


def halo_part(dims, axis, rec_a, rec_b, part):
    cx, cy, _, n_exp = dims
    at, count = (PACK + 3 * n_exp, cy) if axis == "gx" else (PACK + 9 * n_exp, cx)
    return halo(axis, rec_a, rec_b, at + part * count, count)


def halo_fields(dims, axis, rec_a, rec_b):
    parts = [halo_part(dims, axis, rec_a, rec_b, f) for f in range(3)]
    return [tuple(v[side] for v in parts) for side in range(2)]


def outermost(dims, axis, ref):
    cx, cy, _, _ = dims
    if axis == "gx":
        return [tuple(ref[f, 0] for f in range(3)), tuple(ref[f, cx - 1] for f in range(3))]
    return [tuple(ref[f, :, 0, :] for f in range(3)), tuple(ref[f, :, cy - 1, :] for f in range(3))]


def edge_fluxes(dims, axis, trans, field, rec_a, rec_b):
    far, near = halo_fields(dims, axis, rec_a, rec_b), outermost(dims, axis, field)
    return [
        face(trans[k], low[0], mob_of(low), high[0], mob_of(high))
        for k, (low, high) in enumerate(((far[0], near[0]), (near[1], far[1])))
    ]


def edge_tangents(dims, axis, trans, field, direction, rec_a, rec_b, drec_a, drec_b):
    far, near = halo_fields(dims, axis, rec_a, rec_b), outermost(dims, axis, field)
    dfar, dnear = halo_fields(dims, axis, drec_a, drec_b), outermost(dims, axis, direction)
    there = [point(far[k], dfar[k]) for k in range(2)]
    here = [point(near[k], dnear[k]) for k in range(2)]
    return [between(trans[0], there[0], here[0]), between(trans[1], here[1], there[1])]


def residual_edge_kernel(dims, size, make, field, gx_a, gx_b, trans, fluxes, *out):
    if make:
        low, high = halo_part(dims, "gx", gx_a, gx_b, 3)
        outer_trans("gx", size, trans, low, high, out[0])
        trans = out[0]
    for k, flux in enumerate(edge_fluxes(dims, "gx", trans, field, gx_a, gx_b)):
        for a in range(3):
            fluxes[k, a] = flux[a]


def jacobian_edge_kernel(dims, field, direction, trans, gx_a, gx_b, dgx_a, dgx_b, fluxes):
    for k, flux in enumerate(edge_tangents(dims, "gx", trans, field, direction, gx_a, gx_b, dgx_a, dgx_b)):
        for a in range(3):
            fluxes[k, a] = flux[a]


def edge_trans(t_a, t_b):
    return 2.0 * t_a * t_b / (t_a + t_b)


def inner_trans(dims, perm, fx, fy, fz, edge_x, edge_y):
    cx, cy, _, _ = dims
    last_row = lax.broadcasted_iota(jnp.int32, (cy, LANES), 0) == cy - 1
    last_lane = lax.broadcasted_iota(jnp.int32, (cy, LANES), 1) == LANES - 1
    for x in range(cx):
        if x + 1 < cx:
            fx[x] = edge_trans(perm[0, x], perm[0, x + 1])
        t = perm[1, x]
        fy[x] = jnp.where(last_row, 0.0, edge_trans(t, pltpu.roll(t, cy - 1, 0)))
        t = perm[2, x]
        fz[x] = jnp.where(last_lane, 0.0, edge_trans(t, pltpu.roll(t, LANES - 1, 1)))
    edge_x[0], edge_x[1] = perm[0, 0], perm[0, cx - 1]
    edge_y[0], edge_y[1] = perm[1, :, 0, :], perm[1, :, cy - 1, :]


def outer_trans(axis, count, edge, low, high, out):
    at = lax.axis_index(axis)
    out[0] = jnp.where(at > 0, edge_trans(low, edge[0]), 0.0)
    out[1] = jnp.where(at < count - 1, edge_trans(edge[1], high), 0.0)


def mob_of(field):
    return mobilities(*props(field))


def residual_planes(dims, field, pore, fx, fy, fz, acc):
    cx, cy, _, _ = dims

    def plane(x):
        fld = tuple(field[f, x] for f in range(3))
        sats, factors = props(fld)
        return fld[0], mobilities(sats, factors), sats, factors

    cur, below = plane(0), None
    for x in range(cx):
        p, mob, sats, factors = cur
        row = lambda v: pltpu.roll(v, cy - 1, 0)
        lane = lambda v: pltpu.roll(v, LANES - 1, 1)
        y_up = face(fy[x], p, mob, row(p), [row(m) for m in mob])
        z_up = face(fz[x], p, mob, lane(p), [lane(m) for m in mob], 1.0)
        nxt = above = None
        if x + 1 < cx:
            nxt = plane(x + 1)
            above = face(fx[x], p, mob, nxt[0], nxt[1])
        for a in range(3):
            inflow = (y_up[a] - pltpu.roll(y_up[a], 1, 0)) + (z_up[a] - pltpu.roll(z_up[a], 1, 1))
            if above is not None:
                inflow = inflow + above[a]
            if below is not None:
                inflow = inflow - below[a]
            acc[a, x] = pore[x] * (factors[a] * sats[a]) - inflow
        cur, below = nxt, above


def point(field, dfield):
    sats, factors = props(field)
    mob = mobilities(sats, factors)
    dsats, dmob = tangents(sats, factors, mob, dfield)
    return field[0], mob, dfield[0], dmob, sats, factors, dsats


def between(trans, c, n, depth=0.0):
    return face_tangent(trans, c[0], c[1], n[0], n[1], c[2], c[3], n[2], n[3], depth)


def jacobian_planes(dims, field, dfield, pore, fx, fy, fz, acc):
    cx, cy, _, _ = dims

    def plane(x):
        return point(tuple(field[f, x] for f in range(3)), tuple(dfield[f, x] for f in range(3)))

    def moved(c, shift):
        return shift(c[0]), [shift(m) for m in c[1]], shift(c[2]), [shift(m) for m in c[3]]

    cur, below = plane(0), None
    for x in range(cx):
        y_up = between(fy[x], cur, moved(cur, lambda v: pltpu.roll(v, cy - 1, 0)))
        z_up = between(fz[x], cur, moved(cur, lambda v: pltpu.roll(v, LANES - 1, 1)), 1.0)
        nxt = above = None
        if x + 1 < cx:
            nxt = plane(x + 1)
            above = between(fx[x], cur, nxt)
        _, _, dp, _, sats, factors, dsats = cur
        for a in range(3):
            inflow = (y_up[a] - pltpu.roll(y_up[a], 1, 0)) + (z_up[a] - pltpu.roll(z_up[a], 1, 1))
            if above is not None:
                inflow = inflow + above[a]
            if below is not None:
                inflow = inflow - below[a]
            gain = pore[x] * (factors[a] * (dsats[a] + COMPRESS[a] * sats[a] * dp))
            acc[a, x] = gain - inflow
        cur, below = nxt, above


def add_outer(dims, x_fluxes, y_fluxes, acc):
    cx, cy, _, _ = dims
    for a in range(3):
        acc[a, 0] = acc[a, 0] + x_fluxes[0, a]
        acc[a, cx - 1] = acc[a, cx - 1] - x_fluxes[1, a]
        acc[a, :, 0, :] = acc[a, :, 0, :] + y_fluxes[0][a]
        acc[a, :, cy - 1, :] = acc[a, :, cy - 1, :] - y_fluxes[1][a]


def residual_inner_kernel(dims, make, field, pore, *refs):
    if make:
        perm, acc, fx, fy, fz, edge_x, edge_y = refs
        inner_trans(dims, perm, fx, fy, fz, edge_x, edge_y)
    else:
        fx, fy, fz, acc = refs
    residual_planes(dims, field, pore, fx, fy, fz, acc)


def jacobian_inner_kernel(dims, field, direction, pore, fx, fy, fz, acc):
    jacobian_planes(dims, field, direction, pore, fx, fy, fz, acc)


def rows_of(ref, count):
    return tuple(ref[f * count:(f + 1) * count, :] for f in range(3))


def finish_faults(dims, inner, old_mass, flux, idx, values, x_fluxes, y_fluxes, acc):
    cx, cy, n_fault, _ = dims
    for a in range(3):
        values[a, 0:n_fault, :] = -flux[a]
    total = scatter_loop(values, idx, 0, n_fault * LANES, cx * cy, True)
    for a in range(3):
        part = inner[a] + total[a].reshape(cx, cy, LANES)
        acc[a] = part if old_mass is None else part - old_mass[a]
    add_outer(dims, x_fluxes, y_fluxes, acc)


def residual_fault_kernel(dims, size, make, *refs):
    _, _, n_fault, _ = dims
    inner, old_mass, field, idx, pidx, tr, own, x_fluxes, gy_b, gy_a, mine, trans, acc, partner_vals = refs[:14]
    if make:
        low, high = halo_part(dims, "gy", gy_a, gy_b, 3)
        outer_trans("gy", size, trans, low, high, refs[14])
        trans = refs[14]
    partner, values, ptable = refs[-3:]
    stack_partners(dims, mine, gy_a, gy_b, partner)
    pick_partners(dims, partner, pidx, ptable, partner_vals)
    mine_f, other_f = rows_of(own, n_fault), rows_of(partner_vals, n_fault)
    flux = face(tr[...], mine_f[0], mob_of(mine_f), other_f[0], mob_of(other_f))
    y_fluxes = edge_fluxes(dims, "gy", trans, field, gy_a, gy_b)
    finish_faults(dims, inner, old_mass, flux, idx, values, x_fluxes, y_fluxes, acc)


def jacobian_fault_kernel(dims, *refs):
    _, _, n_fault, _ = dims
    inner, field, direction, idx, pidx, tr, own, other, down, trans, x_fluxes = refs[:11]
    gy_a, gy_b, dgy_b, dgy_a, mine, acc, partner, values, ptable, dother = refs[11:]
    stack_partners(dims, mine, dgy_a, dgy_b, partner)
    pick_partners(dims, partner, pidx, ptable, dother)
    flux = between(
        tr[...],
        point(rows_of(own, n_fault), rows_of(down, n_fault)),
        point(rows_of(other, n_fault), rows_of(dother, n_fault)),
    )
    y_fluxes = edge_tangents(dims, "gy", trans, field, direction, gy_a, gy_b, dgy_a, dgy_b)
    finish_faults(dims, inner, None, flux, idx, values, x_fluxes, y_fluxes, acc)


def well_sums(dims, rates, idx, values, turned):
    cx, cy, n_fault, _ = dims
    for a in range(3):
        values[a] = rates[a]
    start = n_fault * LANES
    total = scatter_loop(values, idx, start, start + 6 * LANES, cx * cy, turned)
    return [part.reshape(cx, cy, LANES) for part in total]


def residual_kernel(dims, sizes, final, far_y, *refs):
    refs = list(refs)
    take = lambda n: [refs.pop(0) for _ in range(n)]
    partial, scaling, idx, static = take(4)
    mine, gy_a, gy_b = take(3)
    far = take(far_y)
    direction, seg, const = take(3)
    outs = take(6)
    if final:
        residual, well = take(2)
    packs, values = take(2)
    choose_packets("gy", sizes[1], mine, gy_a, gy_b, far, packs)
    segment_values(packs, seg)
    well_constants(packs, const)
    rates = well_rates(seg, const)
    if final:
        done = running_sum(rates[0] + rates[1] + rates[2])[1:2, :]
        value = done / packs[2, 13:14, :] - 1.0
        lane = lax.broadcasted_iota(jnp.int32, value.shape, 1)
        column = lax.broadcasted_iota(jnp.int32, well.shape, 2)
        count = well.shape[2]
        result = jnp.zeros(well.shape, F32)
        for w in range(count):
            last = LANES // 2 + (w + 1) * (LANES // 2 // count) - 1
            result = jnp.where(column == w, jnp.sum(jnp.where(lane == last, value, 0.0)), result)
        well[...] = result
    sums = well_sums(dims, rates, idx, values, False)
    for a in range(3):
        res = partial[a] + sums[a]
        if final:
            residual[a] = res
        direction[a] = scaling[a] * res
    emit(dims, direction, idx, static, outs)


def jacobian_kernel(dims, sizes, final, far_y, *refs):
    refs = list(refs)
    take = lambda n: [refs.pop(0) for _ in range(n)]
    partial, field, direction, scaling, idx, static, seg, const = take(8)
    mine, dgy_a, dgy_b = take(3)
    far = take(far_y)
    (result,) = take(1)
    outs = None if final else take(6)
    packs, values, dseg = take(3)
    choose_packets("gy", sizes[1], mine, dgy_a, dgy_b, far, packs)
    segment_values(packs, dseg)
    sums = well_sums(dims, well_rate_tangents(seg, dseg, const), idx, values, final)
    for a in range(3):
        step = 2.0 * direction[a] - scaling[a] * (partial[a] + sums[a])
        result[a] = step if final else field[a] - step
    if not final:
        emit(dims, result, idx, static, outs)


def exchange_pairs(axis, kind, size_x, size_y):
    def partner(i, count):
        step = 1 if kind < 2 else 2
        shift = step if kind % 2 else 0
        if shift and not shift <= i < count - shift:
            return None
        return ((i + shift) ^ step) - shift

    out = []
    for i in range(size_x):
        for j in range(size_y):
            if axis == 0:
                got = partner(i, size_x)
                far = (got, j) if got is not None else ((i, j ^ 1) if kind < 2 else (i ^ 1, j))
            else:
                got = partner(j, size_y)
                far = (i, got) if got is not None else ((i ^ 1, j) if kind < 2 else (i, j ^ 1))
            out.append((i * size_y + j, far[0] * size_y + far[1]))
    return out


def body(
    state, perm, pore, old_mass, scaling, fault_cell, fault_tile, fault_row, fault_trans,
    fault_export, perf_cell, well_segments, well_index, bhp, target,
):
    size_x, size_y = lax.axis_size("gx"), lax.axis_size("gy")
    _, cx, cy, _ = state.shape
    wells, segs = well_index.shape[2:]
    n_fault, n_exp = fault_cell.shape[-1] // LANES, fault_export.shape[-1] // LANES
    dims = (cx, cy, n_fault, n_exp)
    far_x = 1 if size_x == 4 else 2
    far_y = 1 if size_y == 4 else 2
    params = pltpu.CompilerParams(vmem_limit_bytes=VMEM_BYTES)
    anywhere = pl.BlockSpec(memory_space=pl.ANY)
    hbm = pl.BlockSpec(memory_space=pltpu.HBM)
    vmem = pl.BlockSpec(memory_space=pltpu.VMEM)
    shape = lambda *dims_: jax.ShapeDtypeStruct(dims_, F32)
    rows = cx * cy
    gx_rows = PACK + 3 * n_exp + 3 * cy
    gy_rows = PACK + 9 * n_exp + 3 * cx
    table = jax.ShapeDtypeStruct((3 * LANES, 2 * rows), BF16)
    near_rows = -(-9 * n_exp // 16) * 16

    def call(kernel, args, outs, scratch=(), specs=None):
        return pl.pallas_call(
            kernel,
            out_shape=outs,
            in_specs=specs or [vmem] * len(args),
            out_specs=[vmem] * len(outs),
            scratch_shapes=scratch,
            compiler_params=params,
        )(*args)

    def message_shapes(first):
        more_x, more_y = (cy, cx) if first else (0, 0)
        return [
            shape(gx_rows + more_x, LANES), shape(gx_rows + more_x, LANES), shape(PACK, LANES),
            shape(3 * cx + more_y, LANES), shape(3 * cx + more_y, LANES), table,
        ]

    def send(value, axis, kind):
        return lax.ppermute(value, ("gx", "gy"), exchange_pairs(axis, kind, size_x, size_y))

    def send_x(messages):
        msg_a, msg_b, packet = messages[:3]
        far = [send(packet, 0, 2 + k) for k in range(far_x)]
        rec_b = send(msg_b, 0, 1)
        rec_a = send(msg_a, 0, 0)
        return rec_a, rec_b, far

    def send_y(messages, got, after):
        msg_a, _, _, yfa, yfb, _ = messages
        rec_a, rec_b, far = got
        total = PACK + 9 * n_exp + yfa.shape[0]
        mid_a, mid_b, mid_c = call(
            functools.partial(middle_kernel, dims, sizes, far_x),
            [*after, msg_a, rec_b, rec_a, *far, yfa, yfb],
            [shape(total, LANES), shape(total, LANES), shape(PACK, LANES)],
            [pltpu.VMEM((5, PACK, LANES), F32)],
            [anywhere] * 2 + [vmem] * (5 + far_x),
        )
        got_b = send(mid_b, 1, 1)
        got_a = send(mid_a, 1, 0)
        got_far = [send(mid_c, 1, 2 + k) for k in range(far_y)]
        return (mid_a, got_a, got_b), got_far

    sizes = (size_x, size_y)
    grid = shape(3, cx, cy, LANES)
    wide_rows = shape(3 * n_fault, LANES)
    small = shape(24, LANES)
    packs = pltpu.VMEM((5, PACK, LANES), F32)
    fault_work = [
        pltpu.VMEM((3, near_rows, LANES), F32), pltpu.VMEM((3, n_fault, LANES), F32),
        pltpu.VMEM((3 * near_rows, 2 * LANES), BF16),
    ]
    well_work = [packs, pltpu.VMEM((3, 8, LANES), F32)]
    columns = (n_fault + 6 + n_exp) * LANES

    sources = [state, perm, fault_cell, fault_export, perf_cell, well_index, well_segments, bhp, target]
    results = call(
        functools.partial(first_kernel, dims),
        [pltpu.with_memory_space_constraint(v, pltpu.HBM) for v in sources],
        message_shapes(True) + [jax.ShapeDtypeStruct((1, columns), jnp.int32), shape(8, LANES), shape(*state.shape)],
        [pltpu.VMEM((2, cy, LANES), F32)]
        + [(pltpu.VMEM if i < 4 else pltpu.SMEM)(v.shape, v.dtype) for i, v in enumerate(sources[2:])]
        + [pltpu.VMEM((2, cx, 8, LANES), F32), pltpu.VMEM((8, LANES), F32), pltpu.SemaphoreType.DMA((14,))],
        [hbm] * len(sources),
    )
    messages, (idx, static, current) = results[:6], results[6:]

    def own_cells(cells_table):
        return call(functools.partial(gather_kernel, dims), [cells_table, idx], [wide_rows])[0]

    for step in range(2):
        final = step == 1
        got = send_x(messages)
        gx_got = got[:2]
        if final:
            (inner,) = call(
                functools.partial(residual_inner_kernel, dims, False), [current, pore, *trans], [grid]
            )
        else:
            inner, *trans, edge_x, edge_y = call(
                functools.partial(residual_inner_kernel, dims, True), [current, pore, perm],
                [grid, shape(cx, cy, LANES), shape(cx, cy, LANES), shape(cx, cy, LANES),
                 shape(2, cy, LANES), shape(2, cx, LANES)],
            )
            pidx, tr = call(
                functools.partial(connection_kernel, dims, size_y),
                [fault_tile.reshape(1, -1), fault_row.reshape(1, -1), fault_trans.reshape(1, -1)],
                [jax.ShapeDtypeStruct((1, n_fault * LANES), jnp.int32), shape(n_fault, LANES)],
            )
        own = own_cells(messages[5])
        gy_got, gy_far = send_y(messages, got, (inner, own))
        edge_shape = shape(2, 3, cy, LANES)
        results = call(
            functools.partial(residual_edge_kernel, dims, size_x, not final),
            [current, *gx_got, outer_x if final else edge_x],
            [edge_shape] + ([] if final else [shape(2, cy, LANES)]),
        )
        x_fluxes = results[0]
        if not final:
            outer_x = results[1]
        results = call(
            functools.partial(residual_fault_kernel, dims, size_y, not final),
            [inner, old_mass, current, idx, pidx, tr, own, x_fluxes, *gy_got[::-1], outer_y if final else edge_y],
            [grid, wide_rows] + ([] if final else [shape(2, cx, LANES)]),
            fault_work,
        )
        partial, other = results[:2]
        if not final:
            outer_y = results[2]
        results = call(
            functools.partial(residual_kernel, dims, sizes, final, far_y),
            [partial, scaling, idx, static, *gy_got, *gy_far],
            [grid, small, small] + message_shapes(False) + ([grid, shape(1, 1, wells)] if final else []),
            well_work,
        )
        direction, seg, const = results[:3]
        messages = results[3:9]
        if final:
            residual, well = results[9:]
        got = send_x(messages)
        (inner,) = call(
            functools.partial(jacobian_inner_kernel, dims), [current, direction, pore, *trans], [grid]
        )
        down = own_cells(messages[5])
        dgy_got, dgy_far = send_y(messages, got, (inner, down))
        (x_fluxes,) = call(
            functools.partial(jacobian_edge_kernel, dims),
            [current, direction, outer_x, *gx_got, *got[:2]],
            [edge_shape],
        )
        (partial,) = call(
            functools.partial(jacobian_fault_kernel, dims),
            [inner, current, direction, idx, pidx, tr, own, other, down, outer_y, x_fluxes, *gy_got[1:], *dgy_got[::-1]],
            [grid],
            fault_work + [pltpu.VMEM((3 * n_fault, LANES), F32)],
        )
        results = call(
            functools.partial(jacobian_kernel, dims, sizes, final, far_y),
            [partial, current, direction, scaling, idx, static, seg, const, *dgy_got, *dgy_far],
            [grid] + ([] if final else message_shapes(False)),
            well_work + [pltpu.VMEM((24, LANES), F32)],
        )
        current, messages = results[0], results[1:]
    return residual, current, well


def solution(mesh):
    grid = P(None, "gx", "gy", None)
    tile = P("gx", "gy", None)
    return jax.shard_map(
        body,
        mesh=mesh,
        in_specs=(
            grid, grid, tile, grid, grid, tile, tile, tile, tile, tile,
            P("gx", "gy", None, None, None, None), tile, P("gx", "gy", None, None), tile, tile,
        ),
        out_specs=(grid, grid, tile),
        check_vma=False,
    )
```
